32 devices in a mesh: fsdp: 8 (over z, y), ep: 4 (over x, core).
Axes of the slice: x: 2, y: 2, z: 4, core: 2. Of those that a mesh axis runs over, the one named last changes fastest.
Arguments:
- tokens: bfloat16 [4096, 3072], P(('fsdp', 'ep')), may hold values from -6 to 6
- expert_ids: int32 [4096, 2], P(('fsdp', 'ep')), may hold values from 0 to 3, all different within a row; in each aligned block of 128 rows (0 to 127, 128 to 255, ...) at most 128 rows name the same one
- gates: float32 [4096, 2], P(('fsdp', 'ep')), may hold values from 0.2 to 1
- up_weight: bfloat16 [4, 3072, 768], P('ep', 'fsdp'), may hold values from -0.109375 to 0.109375
- down_weight: bfloat16 [4, 768, 3072], P('ep', 'fsdp'), may hold values from -0.21875 to 0.21875
- cotangent: bfloat16 [4096, 3072], P(('fsdp', 'ep')), may hold values from -6 to 6
Outputs:
- mixed: bfloat16 [4096, 3072], P(('fsdp', 'ep'))
- token_grad: bfloat16 [4096, 3072], P(('fsdp', 'ep'))
- up_grad: bfloat16 [4, 3072, 768], P('ep', 'fsdp')
- down_grad: bfloat16 [4, 768, 3072], P('ep', 'fsdp')
The draws below stay inside these ranges and needn't reach their ends.
Inputs may be any that keep to these rules, and one draw needn't show every extreme that they name: `expert_ids`: each token names two different experts. Among the tokens of one device (aligned blocks of 128 tokens) no expert is named more than 128 times, and in some block one expert is named exactly 128 times.
All inputs are finite; a program needn't handle non-finite values.
Results may differ from the reference program's by a relative error of at most 0.012.
Values may be sent and summed in bfloat16 or wider, within the bound.
A program may use at most 128 MiB of HBM per device.

```python
import math
import jax
import jax.numpy as jnp
import numpy as np
from jax import lax

D = 3072
FF = 768
TOK_DEV = 128
CAP = 128
EXPERTS = 4
TOKENS = 4096
N_FSDP = 8
N_EP = 4


def levels(stream_key, extent, split, least, top_value):
    loudness, own = 1.0, jax.random.fold_in(stream_key, 6)
    for dim, parts in split:
        draws = jnp.exp(jax.random.uniform(jax.random.fold_in(own, dim), (parts,), jnp.float32, least / len(split), top_value / len(split)))
        loudness = loudness * jnp.repeat(draws, extent[dim] // parts).reshape([-1 if axis == dim else 1 for axis in range(len(extent))])
    return loudness


def assign_block(rng, own, number, rows, number_of, top, reach, skew):
    ranking = jax.random.permutation(rng, number_of)
    packed, usual = shares(number_of, rows * top, reach, skew, True), shares(number_of, rows * top, reach, skew, False)
    places = jnp.arange(number_of)

    def named(tallies, turn):
        used = int((tallies > 0).sum())
        fixed = max(1, used // 4)
        moved = fixed + (places - fixed + turn * (used - fixed)) % max(1, number_of - fixed)
        return jnp.zeros((number_of,), jnp.int32).at[ranking[jnp.where(places < fixed, places, moved)]].set(jnp.asarray(tallies, jnp.int32))

    tallies = jnp.where(number % 4 == 0, named(packed, number // 4), named(usual, number - number // 4 - 1))
    mixed = jax.random.permutation(jax.random.fold_in(own, 3), number_of)
    donor, taker = mixed[0:number_of // 2 * 2:2], mixed[1:number_of // 2 * 2:2]
    slack = jnp.minimum(tallies[donor] - 1, reach - tallies[taker]) // 2
    slack = jnp.where((donor == ranking[0]) | (taker == ranking[0]) | (tallies[taker] == 0), 0, jnp.maximum(slack, 0))
    moved = jax.random.randint(jax.random.fold_in(own, 4), (number_of // 2,), 0, 1 << 20) % (slack + 1)
    tallies = tallies.at[donor].add(-moved).at[taker].add(moved)
    items = jnp.searchsorted(jnp.cumsum(tallies), jnp.arange(rows * top), side="right").astype(jnp.int32)
    grid = items.reshape(top, rows).T
    grid = grid[jax.random.permutation(jax.random.fold_in(own, 1), rows)]
    turn = jax.random.randint(jax.random.fold_in(own, 2), (rows, 1), 0, top)
    return jnp.take_along_axis(grid, (jnp.arange(top)[None, :] + turn) % top, axis=1)


def shares(number_of, total, most, lean, full):
    loads = [(1 << 20) // math.isqrt(grade ** lean) + 1 for grade in range(1, number_of + 1)]
    largest = most if full else min(most, max(-(-total // number_of), total * loads[0] // sum(loads)))
    least = 1 if total - largest >= number_of - 1 else 0
    given, spare = [largest] + [least] * (number_of - 1), total - largest - least * (number_of - 1)
    while spare > 0:
        free = [i for i in range(1, number_of) if given[i] < largest] or [i for i in range(1, number_of) if given[i] < most]
        whole, remaining = sum([loads[i] for i in free]), spare
        for i in free:
            more = min(most - given[i], max(1, remaining * loads[i] // whole), spare)
            given[i] = given[i] + more
            spare = spare - more
    return np.array(given)


def centred(key, extent, scale, most, split=(), held_as=jnp.bfloat16):
    loudness = levels(key, extent, split, -0.22, 0.18) if split else 1.0
    values = jax.random.normal(key, extent, jnp.float32) * scale * loudness
    return jnp.minimum(jnp.maximum(values, -most), most).astype(held_as)


def setup_inputs(seed: int = 0) -> dict:
    splits = jax.random.split(jax.random.key(seed), 7)
    tokens = centred(splits[0], (TOKENS, D), 1.0, 6.0, ((0, 32),))
    expert_ids_keys = jax.random.split(jax.random.fold_in(splits[1], 1), TOKENS // TOK_DEV)
    expert_ids_turns = jax.random.permutation(jax.random.fold_in(splits[1], 3), TOKENS // TOK_DEV)
    expert_ids = jax.vmap(lambda own, number: assign_block(jax.random.fold_in(splits[1], 2), own, number, TOK_DEV, EXPERTS, 2, CAP, 2))(expert_ids_keys, expert_ids_turns).reshape((TOKENS, 2))
    gates = jnp.clip(0.2 + 0.8 * jax.random.uniform(splits[2], (TOKENS, 2), jnp.float32) ** levels(splits[2], (TOKENS, 2), ((0, 32),), -0.2, 0.2), 0.2, 1.0)
    up_weight = centred(splits[3], (EXPERTS, D, FF), D ** -0.5, 0.109375, ((0, 4), (1, 8)))
    down_weight = centred(splits[4], (EXPERTS, FF, D), FF ** -0.5, 0.21875, ((0, 4), (1, 8)))
    cotangent = centred(splits[5], (TOKENS, D), 1.0, 6.0, ((0, 32),))
    return dict(tokens=tokens, expert_ids=expert_ids, gates=gates, up_weight=up_weight, down_weight=down_weight, cotangent=cotangent)


def gelu_parts(pre):
    root = 0.7978845608028654
    inner = root * (pre + 0.044715 * pre * pre * pre)
    tanh_val = jnp.tanh(inner)
    value = 0.5 * pre * (1.0 + tanh_val)
    slope = 0.5 * (1.0 + tanh_val) + 0.5 * pre * (1.0 - tanh_val * tanh_val) * root * (1.0 + 3.0 * 0.044715 * pre * pre)
    return value, slope


def reference(tokens, expert_ids, gates, up_weight, down_weight, cotangent):
    width = tokens.shape[1]
    group = N_EP * TOK_DEV
    limit = N_EP * CAP
    flat_ids = expert_ids.reshape(-1)
    flat_gates = gates.reshape(-1)
    f32 = jnp.float32
    bf16 = jnp.bfloat16

    def per_expert(items):
        expert, up_mat, down_mat = items

        def per_group(index):
            chosen = lax.dynamic_slice_in_dim(flat_ids, index * 2 * group, 2 * group)
            hit = chosen == expert
            picks = jnp.nonzero(hit, size=limit, fill_value=0)[0].astype(jnp.int32)
            live = jnp.arange(limit, dtype=jnp.int32) < jnp.sum(hit.astype(jnp.int32))
            assign = (index * 2 * group + picks).astype(jnp.int32)
            rows = jnp.where(live[:, None], tokens[assign // 2], jnp.zeros((), bf16))
            pre = jnp.dot(rows, up_mat, preferred_element_type=f32)
            value, slope = gelu_parts(pre)
            hidden = value.astype(bf16)
            expert_out = jnp.dot(hidden, down_mat, preferred_element_type=f32).astype(bf16)
            scaled = (cotangent[assign // 2].astype(f32) * flat_gates[assign][:, None]).astype(bf16)
            grad_rows = jnp.where(live[:, None], scaled, jnp.zeros((), bf16))
            d_hidden = jnp.dot(grad_rows, down_mat.T, preferred_element_type=f32)
            d_pre = (d_hidden * slope).astype(bf16)
            back_rows = jnp.dot(d_pre, up_mat.T, preferred_element_type=f32).astype(bf16)
            up_part = jnp.dot(rows.T, d_pre, preferred_element_type=f32).astype(bf16)
            down_part = jnp.dot(hidden.T, grad_rows, preferred_element_type=f32).astype(bf16)
            place = jnp.where(live, assign, 2 * TOKENS)
            return expert_out, back_rows, place, up_part, down_part

        outs, backs, places, up_parts, down_parts = lax.map(per_group, jnp.arange(N_FSDP, dtype=jnp.int32))
        up_total = jnp.sum(up_parts.astype(f32), axis=0).astype(bf16)
        down_total = jnp.sum(down_parts.astype(f32), axis=0).astype(bf16)
        return outs, backs, places, up_total, down_total

    outs, backs, places, up_grad, down_grad = lax.map(
        per_expert, (jnp.arange(N_EP, dtype=jnp.int32), up_weight, down_weight))
    flat_places = places.reshape(-1)
    assigned = jnp.zeros((2 * TOKENS, width), f32).at[flat_places].add(
        outs.reshape(-1, width).astype(f32), mode="drop")
    returned = jnp.zeros((2 * TOKENS, width), f32).at[flat_places].add(
        backs.reshape(-1, width).astype(f32), mode="drop")
    mixed = jnp.sum(assigned.reshape(TOKENS, 2, width) * gates[:, :, None], axis=1).astype(bf16)
    token_grad = jnp.sum(returned.reshape(TOKENS, 2, width), axis=1).astype(bf16)
    return mixed, token_grad, up_grad, down_grad
```

```python
import functools

import jax
import jax.numpy as jnp
from jax import lax
from jax.experimental import pallas as pl
from jax.experimental.pallas import tpu as pltpu
from jax.sharding import PartitionSpec as P

F32 = jnp.float32
BF16 = jnp.bfloat16
MESH = pl.DeviceIdType.MESH
LANES = 128
CHUNKS = 3


def gelu_parts(pre):
    root = 0.7978845608028654
    inner = root * (pre + 0.044715 * pre * pre * pre)
    tanh_val = jnp.tanh(inner)
    value = 0.5 * pre * (1.0 + tanh_val)
    slope = 0.5 * (1.0 + tanh_val) + 0.5 * pre * (1.0 - tanh_val * tanh_val) * root * (
        1.0 + 3.0 * 0.044715 * pre * pre
    )
    return (value, slope)


def dot(left, right, dims):
    return lax.dot_general(left, right, (dims, ((), ())), preferred_element_type=F32)


NN = ((1,), (0,))
NT = ((1,), (1,))
TN = ((0,), (0,))


def tail_rows(size):
    return max(16, size // 6 // 16 * 16)


def tiles(count, size):
    def run(fn):
        @pl.loop(0, count // size)
        def _(i):
            fn(pl.ds(pl.multiple_of(i * size, size), size))

    return run


def kernel(
    nz, ny, nx,
    tok_in, cot_in, gate_in, up_in, down_in,
    mixed_out, tg_out, ug_out, dg_out,
    up, down, tok, cot, gate, slope, hidden, dpre, upart, dpart,
    ry_u, ry_d, rz_u, rz_d, rt_u, rt_d, ft_u, ft_d, rc_m, rc_t, rx_m, rx_t,
    local_sem, wz_s, wz_r, wt_s, wt_r, wo_s, wo_r, wy_s, wy_r,
    tx_s, tx_r, tc_s, tc_r, g_s, g_r,
    ry_s, ry_r, rz_s, rz_r, rt_s, rt_r, ft_s, ft_r, rc_s, rc_r, rx_s, rx_r,
):
    ne = 2 * nx
    f = lax.axis_index("fsdp")
    e = lax.axis_index("ep")
    z, y = lax.div(f, ny), lax.rem(f, ny)
    x, c = lax.div(e, 2), lax.rem(e, 2)
    T = tok_in.shape[0]
    D = tok_in.shape[1]
    R = ne * T
    FF = up.shape[1]

    def zp(k):
        return lax.rem(z + k + nz, nz)

    def inside(zz):
        return (zz >= 0) & (zz < nz)

    def yp(j):
        return lax.rem(y + j + ny, ny)

    def xp(k):
        return lax.rem(x + k + nx, nx)

    def fdev(zz, yy):
        return {"fsdp": zz * ny + yy}

    def edev(xx, cc):
        return {"ep": xx * 2 + cc}

    def rows(ref, index, size):
        return ref.at[pl.ds(pl.multiple_of(index * size, size), size)]

    def remote(src, dst, ss, rs, dev):
        return pltpu.make_async_remote_copy(
            src_ref=src, dst_ref=dst, send_sem=ss, recv_sem=rs,
            device_id=dev, device_id_type=MESH,
        )

    sends = []
    guarded = []

    def send_when(there, copies):
        @pl.when(there)
        def _():
            for copy in copies:
                copy.start()

        guarded.append((there, copies))


    def send(src, dst, ss, rs, dev):
        copy = remote(src, dst, ss, rs, dev)
        copy.start()
        sends.append(copy)
        return copy

    barrier = pltpu.get_barrier_semaphore()
    peers = [fdev(zp(k), y) for k in range(1, nz)]
    peers += [fdev(z, yp(j)) for j in range(1, ny)]
    peers += [{"ep": lax.rem(e + i, ne)} for i in range(1, ne)]
    for dev in peers:
        pl.semaphore_signal(barrier, inc=1, device_id=dev, device_id_type=MESH)
    locals_ = []
    for i, (src, dst) in enumerate((
        (up_in.at[0], rows(up, f, up_in.shape[1])),
        (down_in.at[0], rows(down, f, down_in.shape[1])),
        (tok_in, rows(tok, e, T)),
        (cot_in, rows(cot, e, T)),
    )):
        copy = pltpu.make_async_copy(src, dst, local_sem.at[i])
        copy.start()
        locals_.append(copy)
    rows(gate, e, T)[...] = gate_in[e]
    pl.semaphore_wait(barrier, len(peers))

    weights = ((up_in, up), (down_in, down))

    def span(ref, index, size, begin, count):
        return ref.at[pl.ds(pl.multiple_of(index * size + begin, 16), count)]

    def chain(w, sgn, b, src=None):
        full = weights[w][1]
        size = weights[w][0].shape[1]
        block = rows(full, b * ny + y, size)
        way = (1 - sgn) // 2
        return remote(block if src is None else src, block, wz_s.at[w, way, b],
                      wz_r.at[w, way, b], fdev(zp(sgn), y))

    def chain_tail(w, sgn, b, j):
        full = weights[w][1]
        size = weights[w][0].shape[1]
        q = tail_rows(size)
        block = span(full, b * ny + yp(-j), size, size - q, q)
        way = (1 - sgn) // 2
        return remote(block, block, wt_s.at[w, way, b, j - 1], wt_r.at[w, way, b, j - 1],
                      fdev(zp(sgn), y))

    def across(w, b, yy, j):
        full = weights[w][1]
        size = weights[w][0].shape[1]
        block = span(full, b * ny + yy, size, 0, size - tail_rows(size))
        return remote(block, block, wy_s.at[w, b, j - 1], wy_r.at[w, b, j - 1], fdev(z, yp(j)))

    def own_across(w, yy, j, src=None):
        full = weights[w][1]
        size = weights[w][0].shape[1]
        block = rows(full, z * ny + yy, size)
        return remote(block if src is None else src, block, wo_s.at[w, j - 1], wo_r.at[w, j - 1],
                      fdev(z, yp(j)))

    def weight_start(w):
        src = weights[w][0].at[0]
        for sgn in (1, -1):
            send_when(inside(z + sgn), [chain(w, sgn, z, src)])
        for j in range(1, ny):
            copy = own_across(w, y, j, src)
            copy.start()
            sends.append(copy)

    def tail_start(w):
        for j in range(1, ny):
            own_across(w, yp(-j), j).wait_recv()
        for sgn in (1, -1):
            send_when(inside(z + sgn), [chain_tail(w, sgn, z, j) for j in range(1, ny)])

    def hop(w, s):
        for sgn in (1, -1):
            b = zp(-sgn * s)
            there = inside(z - sgn * s)

            @pl.when(there)
            def _():
                chain(w, sgn, b).wait_recv()

            send_when(there & inside(z + sgn), [chain(w, sgn, b)])
            send_when(there, [across(w, b, y, j) for j in range(1, ny)])

    def hop_tail(w, s):
        for sgn in (1, -1):
            b = zp(-sgn * s)
            there = inside(z - sgn * s)

            @pl.when(there)
            def _():
                for j in range(1, ny):
                    chain_tail(w, sgn, b, j).wait_recv()

            send_when(there & inside(z + sgn), [chain_tail(w, sgn, b, j) for j in range(1, ny)])

    def weight_wait(w):
        locals_[w].wait()
        for k in range(1, nz):
            for j in range(1, ny):
                across(w, zp(k), yp(-j), j).wait_recv()

    acts = ((tok_in, tok), (cot_in, cot))

    def act_start(w):
        src, full = acts[w]
        for k in range(1, nx):
            send(src, rows(full, e, T), tx_s.at[w, k - 1], tx_r.at[w, k - 1], edev(xp(k), c))
        send(src, rows(full, e, T), tc_s.at[w, 0], tc_r.at[w, 0], edev(x, 1 - c))

    def act_forward(w):
        src, full = acts[w]
        started = []
        for k in range(1, nx):
            block = rows(full, xp(-k) * 2 + c, T)
            remote(block, block, tx_s.at[w, k - 1], tx_r.at[w, k - 1],
                   edev(xp(k), c)).wait_recv()
            copy = remote(block, block, tc_s.at[w, k], tc_r.at[w, k], edev(x, 1 - c))
            copy.start()
            started.append(copy)
        return started

    def act_wait(w):
        src, full = acts[w]
        locals_[2 + w].wait()
        for k in range(nx):
            block = rows(full, xp(-k) * 2 + 1 - c, T)
            remote(block, block, tc_s.at[w, k], tc_r.at[w, k], edev(x, 1 - c)).wait_recv()

    weight_start(0)
    act_start(0)
    for i in range(1, ne):
        other = lax.rem(e + i, ne)
        send(gate_in.at[other], rows(gate, e, T), g_s.at[i - 1], g_r.at[i - 1], {"ep": other})
    act_start(1)
    hop(0, 1)
    tok_forwards = act_forward(0)
    tail_start(0)
    hop(0, 2)
    hop_tail(0, 1)
    hop(0, 3)
    weight_start(1)
    hop_tail(0, 2)
    hop_tail(0, 3)
    cot_forwards = act_forward(1)

    act_wait(1)
    for copy in cot_forwards:
        copy.wait_send()
    for i in range(1, ne):
        block = rows(gate, lax.rem(e - i + ne, ne), T)
        remote(block, block, g_s.at[i - 1], g_r.at[i - 1], {"ep": lax.rem(e + i, ne)}).wait_recv()

    @tiles(R, 16)
    def _(r):
        cot[r, :] = (cot[r, :].astype(F32) * gate[r, 0:1]).astype(BF16)

    act_wait(0)
    hop(1, 1)
    tail_start(1)
    weight_wait(0)

    @tiles(FF, 256)
    def _(n):
        slope[:, n] = dot(tok[...], up[:, n], NN)

    hop(1, 2)
    hop_tail(1, 1)

    @tiles(R, 16)
    def _(r):
        value, grad = gelu_parts(slope[r, :])
        hidden[r, :] = value.astype(BF16)
        slope[r, :] = grad

    @tiles(D, 512)
    def _(n):
        dpart[:, n] = dot(hidden[...], cot[:, n], TN).astype(BF16)

    parts = ((upart, ry_u, rz_u, rt_u, ft_u, ug_out), (dpart, ry_d, rz_d, rt_d, ft_d, dg_out))

    flip = lax.div(z, 2)
    near = z + flip * (3 - 2 * z)
    order = [d + flip * (3 - 2 * d) for d in (near * 0 + 3, 2 - 2 * near, 1 + near, near)]

    def give(w, d, yy, j):
        part, ry = parts[w][:2]
        size = parts[w][-1].shape[1]
        return remote(span(part, d * ny + yy, size, 0, size - tail_rows(size)),
                      ry.at[(j - 1) * nz + d], ry_s.at[w, d, j - 1], ry_r.at[w, d, j - 1],
                      fdev(z, yp(j)))

    def run_block(w, way, d, nxt):
        part, ry, rz = parts[w][:3]
        size = parts[w][-1].shape[1]
        return remote(rows(part, d * ny + y, size), rz.at[way, d], rz_s.at[w, d],
                      rz_r.at[w, way, d], fdev(nxt, y))

    def run_tail(w, way, d, nxt, j):
        part, rt = parts[w][0], parts[w][3]
        size = parts[w][-1].shape[1]
        q = tail_rows(size)
        return remote(span(part, d * ny + yp(j), size, size - q, q), rt.at[way, d, j - 1],
                      rt_s.at[w, d, j - 1], rt_r.at[w, way, d, j - 1], fdev(nxt, y))

    def last_tail(w, j):
        part, ft = parts[w][0], parts[w][4]
        size = parts[w][-1].shape[1]
        q = tail_rows(size)
        return remote(span(part, z * ny + yp(j), size, size - q, q), ft.at[j - 1],
                      ft_s.at[w, j - 1], ft_r.at[w, j - 1], fdev(z, yp(j)))

    def part_start(w):
        for d in order:
            for j in range(1, ny):
                copy = give(w, d, yp(j), j)
                copy.start()
                sends.append(copy)

    def add(part, start, count, others):
        @tiles(count, 16)
        def _(r):
            at = pl.ds(pl.multiple_of(start + r.start, 16), 16)
            total = part[at, :].astype(F32)
            for other in others:
                total += other[r, :].astype(F32)
            part[at, :] = total.astype(BF16)

    def pair(w, d):
        part, ry = parts[w][:2]
        size = parts[w][-1].shape[1]
        for j in range(1, ny):
            give(w, d, y, j).wait_recv()
        add(part, (d * ny + y) * size, size - tail_rows(size),
            [ry.at[(j - 1) * nz + d] for j in range(1, ny)])

    def run(w, p):
        part, ry, rz, rt = parts[w][:4]
        size = parts[w][-1].shape[1]
        q = tail_rows(size)
        d = order[p]
        way = jnp.where(d > z, 0, 1)
        sgn = 1 - 2 * way
        nxt = z + sgn
        pair(w, d)

        @pl.when(inside(z - sgn))
        def _():
            run_block(w, way, d, nxt).wait_recv()
            for j in range(1, ny):
                run_tail(w, way, d, nxt, j).wait_recv()
            add(part, (d * ny + y) * size, size, [rz.at[way, d]])
            for j in range(1, ny):
                add(part, (d * ny + yp(j)) * size + size - q, q, [rt.at[way, d, j - 1]])

        copies = [run_block(w, way, d, nxt)]
        copies += [run_tail(w, way, d, nxt, j) for j in range(1, ny)]
        for copy in copies:
            copy.start()
            sends.append(copy)

    def part_last(w):
        part, ry, rz, rt = parts[w][:4]
        size = parts[w][-1].shape[1]
        q = tail_rows(size)
        pair(w, z)
        for way in range(2):
            sgn = 1 - 2 * way

            @pl.when(inside(z - sgn))
            def _():
                for j in range(1, ny):
                    run_tail(w, way, z, zp(1), j).wait_recv()
                    add(part, (z * ny + yp(j)) * size + size - q, q, [rt.at[way, z, j - 1]])

        for j in range(1, ny):
            copy = last_tail(w, j)
            copy.start()
            sends.append(copy)
        for way in range(2):
            sgn = 1 - 2 * way

            @pl.when(inside(z - sgn))
            def _():
                run_block(w, way, z, zp(1)).wait_recv()
                add(part, (z * ny + y) * size, size, [rz.at[way, z]])

    def part_end(w):
        part, ry, rz, rt, ft, out = parts[w]
        size = out.shape[1]
        q = tail_rows(size)
        for j in range(1, ny):
            last_tail(w, j).wait_recv()
        add(part, (z * ny + y) * size + size - q, q, [ft.at[j - 1] for j in range(1, ny)])

        @tiles(size, 16)
        def _(r):
            out[0, r, :] = part[pl.ds(pl.multiple_of(f * size + r.start, 16), 16), :]

    backs = ((cot, rc_m, rx_m, mixed_out), (tok, rc_t, rx_t, tg_out))

    def back_start(w):
        full, rc, rx, out = backs[w]
        for k in range(nx):
            k = (k + 1) % nx
            send(rows(full, xp(k) * 2 + 1 - c, T), rc.at[k], rc_s.at[w, k], rc_r.at[w, k],
                 edev(x, 1 - c))

    def back_pair(w):
        full, rc, rx, out = backs[w]
        for k in range(nx):
            k = (k + 1) % nx
            index = xp(k) * 2 + c
            slot = rc.at[k]
            remote(slot, slot, rc_s.at[w, k], rc_r.at[w, k], edev(x, 1 - c)).wait_recv()

            @tiles(T, 16)
            def _(r):
                at = pl.ds(pl.multiple_of(index * T + r.start, 16), 16)
                full[at, :] = (full[at, :].astype(F32) + rc[k, r, :].astype(F32)).astype(BF16)

            if k:
                send(rows(full, index, T), rx.at[k - 1], rx_s.at[w, k - 1], rx_r.at[w, k - 1],
                     edev(xp(k), c))

    def back_end(w):
        full, rc, rx, out = backs[w]
        for k in range(1, nx):
            slot = rx.at[k - 1]
            remote(slot, slot, rx_s.at[w, k - 1], rx_r.at[w, k - 1], edev(xp(k), c)).wait_recv()

        @tiles(T, 16)
        def _(r):
            at = pl.ds(pl.multiple_of(e * T + r.start, 16), 16)
            total = full[at, :].astype(F32)
            for k in range(1, nx):
                total += rx[k - 1, r, :].astype(F32)
            out[r, :] = total.astype(BF16)

    hop(1, 3)
    hop_tail(1, 2)
    part_start(1)
    hop_tail(1, 3)
    weight_wait(1)

    @tiles(FF, 256)
    def _(n):
        dpre[:, n] = (dot(cot[...], down[n, :], NT) * slope[:, n]).astype(BF16)

    run(1, 0)

    @tiles(D, 384)
    def _(n):
        upart[n, :] = dot(tok[:, n], dpre[...], TN).astype(BF16)

    part_start(0)
    run(1, 1)

    @tiles(D, 512)
    def _(n):
        cot[:, n] = (dot(hidden[...], down[:, n], NN) * gate[:, 0:1]).astype(BF16)

    back_start(0)
    run(1, 2)
    for copy in tok_forwards:
        copy.wait_send()

    @tiles(D, 512)
    def _(n):
        tok[:, n] = dot(dpre[...], up[n, :], NT).astype(BF16)

    back_start(1)
    back_pair(0)
    back_pair(1)
    run(0, 0)
    part_last(1)
    back_end(0)
    run(0, 1)
    back_end(1)
    part_end(1)
    run(0, 2)
    part_last(0)
    part_end(0)
    for copy in sends:
        copy.wait_send()
    for there, copies in guarded:
        @pl.when(there)
        def _():
            for copy in copies:
                copy.wait_send()


def body(tokens, expert_ids, gates, up_weight, down_weight, cotangent):
    nf, ne = lax.axis_size("fsdp"), lax.axis_size("ep")
    nz = 4
    ny, nx = nf // nz, ne // 2
    T, D = tokens.shape
    R = ne * T
    su, FF = up_weight.shape[1:]
    sd = down_weight.shape[1]
    chosen = expert_ids[None] == jnp.arange(ne, dtype=jnp.int32)[:, None, None]
    dense = jnp.sum(jnp.where(chosen, gates[None], 0.0), axis=2)
    gcols = jnp.broadcast_to(dense[:, :, None], (ne, T, LANES))
    qu, qd = (tail_rows(size) for size in (su, sd))
    anyspace = pl.BlockSpec(memory_space=pl.ANY)
    vmem = pl.BlockSpec(memory_space=pltpu.VMEM)
    sem = pltpu.SemaphoreType.DMA
    V = pltpu.VMEM
    scratch = [
        V((D, FF), BF16), V((FF, D), BF16), V((R, D), BF16), V((R, D), BF16),
        V((R, LANES), F32), V((R, FF), F32), V((R, FF), BF16), V((R, FF), BF16),
        V((D, FF), BF16), V((FF, D), BF16),
        V(((ny - 1) * nz, su - qu, FF), BF16), V(((ny - 1) * nz, sd - qd, D), BF16),
        V((2, nz, su, FF), BF16), V((2, nz, sd, D), BF16),
        V((2, nz, ny - 1, qu, FF), BF16), V((2, nz, ny - 1, qd, D), BF16),
        V((ny - 1, qu, FF), BF16), V((ny - 1, qd, D), BF16),
        V((nx, T, D), BF16), V((nx, T, D), BF16),
        V((nx - 1, T, D), BF16), V((nx - 1, T, D), BF16),
        sem((4,)),
        sem((2, 2, nz)), sem((2, 2, nz)),
        sem((2, 2, nz, ny - 1)), sem((2, 2, nz, ny - 1)),
        sem((2, ny - 1)), sem((2, ny - 1)),
        sem((2, nz, ny - 1)), sem((2, nz, ny - 1)),
        sem((2, nx - 1)), sem((2, nx - 1)),
        sem((2, nx)), sem((2, nx)),
        sem((ne - 1,)), sem((ne - 1,)),
        sem((2, nz, ny - 1)), sem((2, nz, ny - 1)),
        sem((2, nz)), sem((2, 2, nz)),
        sem((2, nz, ny - 1)), sem((2, 2, nz, ny - 1)),
        sem((2, ny - 1)), sem((2, ny - 1)),
        sem((2, nx)), sem((2, nx)),
        sem((2, nx - 1)), sem((2, nx - 1)),
    ]
    return pl.pallas_call(
        functools.partial(kernel, nz, ny, nx),
        out_shape=(
            jax.ShapeDtypeStruct((T, D), BF16),
            jax.ShapeDtypeStruct((T, D), BF16),
            jax.ShapeDtypeStruct((1, su, FF), BF16),
            jax.ShapeDtypeStruct((1, sd, D), BF16),
        ),
        in_specs=[anyspace, anyspace, vmem, anyspace, anyspace],
        out_specs=(vmem, vmem, vmem, vmem),
        scratch_shapes=scratch,
        compiler_params=pltpu.CompilerParams(
            collective_id=0, has_side_effects=True, vmem_limit_bytes=64 * 1024 * 1024 - 262144
        ),
    )(tokens, cotangent, gcols, up_weight, down_weight)


def grouped(nz, *refs):
    (tok_in, cot_in, ids_in, gate_in, up_in, down_in,
     mixed_out, tg_out, ug_out, dg_out,
     up, down, tok, cot, upl, perm, uex, gd, gcol, slope, dh, hidden, dpre, upart, dpart,
     rz_u, rz_d, yrecv, rc_m, rc_t, r2_m, r2_t, r3_m, r3_t,
     local_sem, us, ur, ds_s, ds_r, yx_s, yx_r, tx_s, tx_r, ty_s, ty_r, fx_s, fx_r, fy_s, fy_r,
     tc_s, tc_r, g_s, g_r, ru_s, ru_r, rd_s, rd_r, yg_s, yg_r, b1_s, b1_r, b2_s, b2_r, b3_s, b3_r) = refs
    f = lax.axis_index("fsdp")
    e = lax.axis_index("ep")
    z, y = lax.div(f, 2), lax.rem(f, 2)
    x, c = lax.div(e, 2), lax.rem(e, 2)
    T, D = tok_in.shape
    SU, FF = up_in.shape[1:]
    SD = down_in.shape[1]
    H = FF // 2
    R = 8 * T
    W = D // CHUNKS
    HALF = W // 2

    def inside(zz):
        return (zz >= 0) & (zz < nz)

    def zp(k):
        return lax.rem(z + k + nz, nz)

    def zdev(zz):
        return {"fsdp": lax.rem(zz + nz, nz) * 2 + y}

    ydev = {"fsdp": z * 2 + 1 - y}
    xdev = {"ep": (1 - x) * 2 + c}
    cdev = {"ep": x * 2 + 1 - c}

    def blk(yy, xx, cc):
        return cc * 4 + yy * 2 + xx

    me = blk(y, x, c)

    def rows(index, size):
        return pl.ds(pl.multiple_of(index * size, size), size)

    def lanes(index, size):
        return pl.ds(pl.multiple_of(index * size, size), size)

    def cols(n):
        return pl.ds(n * W, W)

    def cols_a(n):
        return pl.ds(n * W, HALF)

    def cols_b(n):
        return pl.ds(n * W + HALF, HALF)

    def remote(src, dst, ss, rs, dev):
        return pltpu.make_async_remote_copy(
            src_ref=src, dst_ref=dst, send_sem=ss, recv_sem=rs,
            device_id=dev, device_id_type=MESH,
        )

    sends = []
    guarded = []

    def go(copy, keep=sends):
        copy.start()
        keep.append(copy)

    def go_when(there, copy):
        @pl.when(there)
        def _():
            copy.start()

        guarded.append((there, copy))

    barrier = pltpu.get_barrier_semaphore()
    offsets = [(i // 4, i // 2 % 2, i % 2) for i in range(1, 8)]

    def gdev(dy, dx, dc):
        yy = 1 - y if dy else y
        xx = 1 - x if dx else x
        cc = 1 - c if dc else c
        return yy, xx, cc

    peers = [{"fsdp": zp(k) * 2 + y, "ep": e} for k in range(1, nz)]
    for offset in offsets:
        yy, xx, cc = gdev(*offset)
        peers.append({"fsdp": z * 2 + yy, "ep": xx * 2 + cc})
    for dev in peers:
        pl.semaphore_signal(barrier, inc=1, device_id=dev, device_id_type=MESH)
    locals_ = []
    for i, (src, dst) in enumerate((
        (up_in.at[0], upl),
        (down_in.at[0], down.at[rows(z, SD)]),
        (tok_in, tok.at[rows(me, T)]),
        (cot_in, cot.at[rows(me, T)]),
    )):
        copy = pltpu.make_async_copy(src, dst, local_sem.at[i])
        copy.start()
        locals_.append(copy)

    expert = lax.broadcasted_iota(jnp.int32, (8, T), 0)
    gd[me] = jnp.where(ids_in[0:1, :] == expert, gate_in[0:1, :], 0.0) + jnp.where(
        ids_in[1:2, :] == expert, gate_in[1:2, :], 0.0)

    @pl.loop(0, 2 * nz)
    def _(i):
        half, zz = lax.div(i, nz), lax.rem(i, nz)
        column = lax.broadcasted_iota(jnp.int32, (SD, FF), 1)
        unit = lax.broadcasted_iota(jnp.int32, (SD, FF), 0) + SD * (2 * zz + half)
        perm[rows(i, SD), :] = jnp.where(column == unit, 1.0, 0.0).astype(BF16)

    locals_[0].wait()
    halfrows = lambda h: pl.ds(pl.multiple_of(h * H, H), H)
    up[rows(f, SU), :] = dot(upl[...], perm[halfrows(y), :], NT).astype(BF16)
    uex[...] = dot(upl[...], perm[halfrows(1 - y), :], NT).astype(BF16)
    pl.semaphore_wait(barrier, len(peers))

    def sub(p):
        return y if p == 0 else 1 - y

    def chain_u(p, sgn, b):
        block = up.at[rows(2 * b + sub(p), SU)]
        way = (1 - sgn) // 2
        return remote(block, block, us.at[p, way, b], ur.at[p, way, b], zdev(z + sgn))

    def chain_d(n, sgn, b):
        block = down.at[rows(b, SD), cols(n)]
        way = (1 - sgn) // 2
        return remote(block, block, ds_s.at[n, way, b], ds_r.at[n, way, b], zdev(z + sgn))

    def own_start(chain, n):
        for sgn in (1, -1):
            go_when(inside(z + sgn), chain(n, sgn, z))

    def hop(chain, n, s):
        for sgn in (1, -1):
            b = zp(-sgn * s)
            there = inside(z - sgn * s)

            @pl.when(there)
            def _():
                chain(n, sgn, b).wait_recv()

            go_when(there & inside(z + sgn), chain(n, sgn, b))

    y_exchange = remote(uex, up.at[rows(f, SU)], yx_s.at[0], yx_r.at[0], ydev)

    acts = ((tok_in, tok), (cot_in, cot))
    forwards = ([[] for _ in range(CHUNKS)], [[] for _ in range(CHUNKS)])

    def act_own(w, n):
        src, full = acts[w]
        there = full.at[rows(me, T), cols(n)]
        go(remote(src.at[:, cols(n)], there, tx_s.at[w, n], tx_r.at[w, n], xdev))
        go(remote(src.at[:, cols(n)], there, ty_s.at[w, n], ty_r.at[w, n], ydev))
        go(remote(src.at[:, cols(n)], there, tc_s.at[w, n, 0], tc_r.at[w, n, 0], cdev))

    def act_fwd(w, n):
        full = acts[w][1]
        keep = forwards[w][n]
        bx, by = blk(y, 1 - x, c), blk(1 - y, x, c)
        here = full.at[rows(bx, T), cols(n)]
        part = full.at[rows(bx * 2 + 1, T // 2), cols(n)]
        remote(here, here, tx_s.at[w, n], tx_r.at[w, n], xdev).wait_recv()
        go(remote(part, part, fy_s.at[w, n], fy_r.at[w, n], ydev), keep)
        go(remote(here, here, tc_s.at[w, n, 1], tc_r.at[w, n, 1], cdev), keep)
        here = full.at[rows(by, T), cols(n)]
        part = full.at[rows(by * 2, T // 2), cols(n)]
        remote(here, here, ty_s.at[w, n], ty_r.at[w, n], ydev).wait_recv()
        go(remote(part, part, fx_s.at[w, n], fx_r.at[w, n], xdev), keep)
        go(remote(here, here, tc_s.at[w, n, 2], tc_r.at[w, n, 2], cdev), keep)

    def act_diag(w, n):
        full = acts[w][1]
        bd = blk(1 - y, 1 - x, c)
        low = full.at[rows(bd * 2, T // 2), cols(n)]
        high = full.at[rows(bd * 2 + 1, T // 2), cols(n)]
        here = full.at[rows(bd, T), cols(n)]
        remote(low, low, fx_s.at[w, n], fx_r.at[w, n], xdev).wait_recv()
        remote(high, high, fy_s.at[w, n], fy_r.at[w, n], ydev).wait_recv()
        go(remote(here, here, tc_s.at[w, n, 3], tc_r.at[w, n, 3], cdev), forwards[w][n])

    def act_done(w, n):
        full = acts[w][1]
        others = ((y, x), (y, 1 - x), (1 - y, x), (1 - y, 1 - x))
        for k, (yy, xx) in enumerate(others):
            here = full.at[rows(blk(yy, xx, 1 - c), T), cols(n)]
            remote(here, here, tc_s.at[w, n, k], tc_r.at[w, n, k], cdev).wait_recv()

    def gates_start():
        for i, offset in enumerate(offsets):
            yy, xx, cc = gdev(*offset)
            go(remote(gd.at[me], gd.at[me], g_s.at[i], g_r.at[i],
                      {"fsdp": z * 2 + yy, "ep": xx * 2 + cc}))

    def gates_done():
        for i, offset in enumerate(offsets):
            yy, xx, cc = gdev(*offset)
            here = gd.at[blk(yy, xx, cc)]
            remote(here, here, g_s.at[i], g_r.at[i],
                   {"fsdp": z * 2 + yy, "ep": xx * 2 + cc}).wait_recv()

        @pl.loop(0, 8)
        def _(b):
            mine = lax.broadcasted_iota(jnp.int32, (8, T), 0) == e
            row = jnp.sum(jnp.where(mine, gd[b], 0.0), axis=0, keepdims=True)
            eye = lax.broadcasted_iota(jnp.int32, (T, T), 0) == lax.broadcasted_iota(
                jnp.int32, (T, T), 1)
            column = jnp.sum(jnp.where(eye, row, 0.0), axis=1, keepdims=True)
            gcol[rows(b, T), :] = jnp.broadcast_to(column, (T, LANES))

    flip = lax.div(z, 2)
    near = z + flip * (3 - 2 * z)
    order = [d + flip * (3 - 2 * d) for d in (near * 0 + 3, 2 - 2 * near, 1 + near, near)]
    is_end = near == 0

    def pre_step(s):
        plane = order[3 - s]

        @tiles(R, 256)
        def _(r):
            part = dot(tok[r, lanes(plane, 2 * SU)], up[rows(plane, 2 * SU), :], NN)
            if s == 0:
                slope[r, :] = part
            elif s < nz - 1:
                slope[r, :] += part
            else:
                value, grad = gelu_parts(slope[r, :] + part)
                hidden[r, :] = value.astype(BF16)
                slope[r, :] = grad

    def scale(n):
        for copy in forwards[1][n]:
            copy.wait_send()

        @tiles(R, 16)
        def _(r):
            cot[r, cols(n)] = (cot[r, cols(n)].astype(F32) * gcol[r, 0:1]).astype(BF16)

    def chunk_tiles(n, size):
        def run(fn):
            @pl.loop(0, W // size)
            def _(i):
                fn(pl.ds(pl.multiple_of(n * W + i * size, size), size))

        return run

    def down_part(n):
        @chunk_tiles(n, 512)
        def _(t):
            dpart[:, t] = dot(hidden[...], cot[:, t], TN).astype(BF16)

    def back_hidden(n):
        @tiles(R, 256)
        def _(r):
            part = dot(cot[r, cols(n)], down[:, cols(n)], NT)
            if n == 0:
                dh[r, :] = part
            elif n < CHUNKS - 1:
                dh[r, :] += part
            else:
                dpre[r, :] = ((dh[r, :] + part) * slope[r, :]).astype(BF16)

    def mixed_part(n):
        @chunk_tiles(n, 512)
        def _(t):
            @tiles(R, 512)
            def _(r):
                cot[r, t] = (dot(hidden[r, :], down[:, t], NN) * gcol[r, 0:1]).astype(BF16)

    def token_part(n):
        @chunk_tiles(n, 512)
        def _(t):
            @tiles(R, 512)
            def _(r):
                tok[r, t] = dot(dpre[r, :], up[t, :], NT).astype(BF16)

    def up_part(q, pos):
        at = rows(2 * order[pos] + (1 - sub(q)), SU)
        upart[at, :] = dot(tok[:, at], dpre[...], TN).astype(BF16)

    def send_down(n, d, way, nxt):
        return remote(dpart.at[rows(d, SD), cols(n)], rz_d.at[way, d, :, cols(n)],
                      rd_s.at[n, d], rd_r.at[n, way, d], zdev(nxt))

    def send_up(q, d, way, nxt):
        return remote(upart.at[rows(2 * d + (1 - sub(q)), SU)], rz_u.at[q, way, d],
                      ru_s.at[q, d], ru_r.at[q, way, d], zdev(nxt))

    def add_down(n, d, way):
        @tiles(SD, 16)
        def _(r):
            at = pl.ds(pl.multiple_of(d * SD + r.start, 16), 16)
            dpart[at, cols(n)] = (dpart[at, cols(n)].astype(F32)
                                  + rz_d[way, d, r, cols(n)].astype(F32)).astype(BF16)

    def add_up(q, d, way):
        @tiles(SU, 32)
        def _(r):
            at = pl.ds(pl.multiple_of((2 * d + (1 - sub(q))) * SU + r.start, 32), 32)
            upart[at, :] = (upart[at, :].astype(F32)
                            + rz_u[q, way, d, r, :].astype(F32)).astype(BF16)

    downs, ups = (send_down, add_down), (send_up, add_up)

    def course(pos):
        d = order[pos]
        way = jnp.where(d > z, 0, 1)
        return d, way, z + 1 - 2 * way

    def begin(kind, n, pos):
        d, way, nxt = course(pos)
        go_when(is_end, kind[0](n, d, way, nxt))

    def middle(kind, n, pos):
        d, way, nxt = course(pos)
        copy = kind[0](n, d, way, nxt)

        @pl.when(jnp.logical_not(is_end))
        def _():
            copy.wait_recv()
            kind[1](n, d, way)
            copy.start()

        guarded.append((jnp.logical_not(is_end), copy))

    def last(kind, n):
        for way in range(2):
            @pl.when(inside(z - 1 + 2 * way))
            def _():
                kind[0](n, z, way, zp(1)).wait_recv()
                kind[1](n, z, way)

    def down_end(n):
        last(downs, n)

        @tiles(SD, 16)
        def _(r):
            dg_out[0, r, cols(n)] = dpart[pl.ds(pl.multiple_of(z * SD + r.start, 16), 16), cols(n)]

    other_up = upart.at[rows(2 * z + 1 - y, SU)]
    y_return = remote(other_up, yrecv, yg_s.at[0], yg_r.at[0], ydev)

    def up_end():
        last(ups, 1)
        y_return.wait_recv()
        ug_out[0] = (dot(upart[rows(f, SU), :], perm[halfrows(y), :], NN)
                     + dot(yrecv[...], perm[halfrows(1 - y), :], NN)).astype(BF16)

    backs = ((cot, rc_m, r2_m, r3_m, mixed_out), (tok, rc_t, r2_t, r3_t, tg_out))
    G = 4 * T

    def back1(w, n):
        full, rc = backs[w][:2]
        go(remote(full.at[rows(1 - c, G), cols(n)], rc.at[:, cols(n)],
                  b1_s.at[w, n], b1_r.at[w, n], cdev))

    def back2(w, n):
        full, rc, r2 = backs[w][:3]
        here = rc.at[:, cols(n)]
        remote(here, here, b1_s.at[w, n], b1_r.at[w, n], cdev).wait_recv()

        @tiles(G, 16)
        def _(r):
            at = pl.ds(pl.multiple_of(c * G + r.start, 16), 16)
            full[at, cols(n)] = (full[at, cols(n)].astype(F32)
                                 + rc[r, cols(n)].astype(F32)).astype(BF16)

        for yy in range(2):
            go(remote(full.at[rows(blk(yy, 1 - x, c), T), cols_a(n)],
                      r2.at[pl.ds(yy * T, T), cols_a(n)],
                      b2_s.at[w, n, yy], b2_r.at[w, n, yy], xdev))
        go(remote(full.at[rows(c * 2 + 1 - y, 2 * T), cols_b(n)], r2.at[:, cols_b(n)],
                  b2_s.at[w, n, 2], b2_r.at[w, n, 2], ydev))

    def back3(w, n):
        full, rc, r2, r3 = backs[w][:4]
        for yy in range(2):
            here = r2.at[pl.ds(yy * T, T), cols_a(n)]
            remote(here, here, b2_s.at[w, n, yy], b2_r.at[w, n, yy], xdev).wait_recv()
        here = r2.at[:, cols_b(n)]
        remote(here, here, b2_s.at[w, n, 2], b2_r.at[w, n, 2], ydev).wait_recv()
        ba, bb = blk(1 - y, x, c), blk(y, 1 - x, c)

        @tiles(T, 16)
        def _(r):
            at = pl.ds(pl.multiple_of(ba * T + r.start, 16), 16)
            there = pl.ds(pl.multiple_of((1 - y) * T + r.start, 16), 16)
            full[at, cols_a(n)] = (full[at, cols_a(n)].astype(F32)
                                   + r2[there, cols_a(n)].astype(F32)).astype(BF16)
            at = pl.ds(pl.multiple_of(bb * T + r.start, 16), 16)
            there = pl.ds(pl.multiple_of((1 - x) * T + r.start, 16), 16)
            full[at, cols_b(n)] = (full[at, cols_b(n)].astype(F32)
                                   + r2[there, cols_b(n)].astype(F32)).astype(BF16)

        go(remote(full.at[rows(ba, T), cols_a(n)], r3.at[:, cols_a(n)],
                  b3_s.at[w, n, 0], b3_r.at[w, n, 0], ydev))
        go(remote(full.at[rows(bb, T), cols_b(n)], r3.at[:, cols_b(n)],
                  b3_s.at[w, n, 1], b3_r.at[w, n, 1], xdev))

    def back4(w, n):
        full, rc, r2, r3, out = backs[w]
        for k, (span, dev) in enumerate(((cols_a(n), ydev), (cols_b(n), xdev))):
            here = r3.at[:, span]
            remote(here, here, b3_s.at[w, n, k], b3_r.at[w, n, k], dev).wait_recv()

        @tiles(T, 16)
        def _(r):
            at = pl.ds(pl.multiple_of(me * T + r.start, 16), 16)
            for span, lane in ((cols_a(n), y), (cols_b(n), x)):
                there = pl.ds(pl.multiple_of(lane * T + r.start, 16), 16)
                out[r, span] = (full[at, span].astype(F32) + r2[there, span].astype(F32)
                                + r3[r, span].astype(F32)).astype(BF16)

    go(y_exchange)
    own_start(chain_u, 0)
    for n in range(CHUNKS):
        act_own(0, n)
    gates_start()
    hop(chain_u, 0, 1)
    locals_[1].wait()
    hop(chain_u, 0, 2)
    y_exchange.wait_recv()
    own_start(chain_u, 1)
    for n in range(CHUNKS):
        act_fwd(0, n)
    act_own(1, 0)
    hop(chain_u, 0, 3)
    gates_done()
    hop(chain_u, 1, 1)
    for n in range(CHUNKS):
        act_diag(0, n)
    act_own(1, 1)
    locals_[2].wait()
    for n in range(CHUNKS):
        act_done(0, n)
    pre_step(0)
    act_fwd(1, 0)
    pre_step(1)
    hop(chain_u, 1, 2)
    own_start(chain_d, 0)
    act_diag(1, 0)
    act_own(1, 2)
    pre_step(2)
    act_fwd(1, 1)
    hop(chain_u, 1, 3)
    own_start(chain_d, 1)
    pre_step(3)
    hop(chain_d, 0, 1)
    locals_[3].wait()
    act_done(1, 0)
    scale(0)
    down_part(0)
    for pos in range(3):
        begin(downs, 0, pos)
    hop(chain_d, 0, 2)
    act_diag(1, 1)
    act_fwd(1, 2)
    act_done(1, 1)
    scale(1)
    hop(chain_d, 0, 3)
    own_start(chain_d, 2)
    down_part(1)
    for pos in range(3):
        begin(downs, 1, pos)
    hop(chain_d, 1, 1)
    back_hidden(0)
    mixed_part(0)
    back1(0, 0)
    hop(chain_d, 1, 2)
    middle(downs, 0, 0)
    act_diag(1, 2)
    back2(0, 0)
    act_done(1, 2)
    hop(chain_d, 1, 3)
    scale(2)
    down_part(2)
    for pos in range(3):
        begin(downs, 2, pos)
    hop(chain_d, 2, 1)
    back_hidden(1)
    mixed_part(1)
    back1(0, 1)
    back3(0, 0)
    hop(chain_d, 2, 2)
    middle(downs, 0, 2)
    back2(0, 1)
    middle(downs, 1, 0)
    middle(downs, 1, 2)
    back4(0, 0)
    hop(chain_d, 2, 3)
    back_hidden(2)
    for pos in range(3):
        up_part(0, pos)
        begin(ups, 0, pos)
    mixed_part(2)
    back1(0, 2)
    middle(downs, 0, 1)
    up_part(0, 3)
    back3(0, 1)
    back2(0, 2)
    for pos in range(4):
        up_part(1, pos)
        if pos < 3:
            begin(ups, 1, pos)
    for n in range(CHUNKS):
        for copy in forwards[0][n]:
            copy.wait_send()
    token_part(0)
    back1(1, 0)
    middle(downs, 2, 0)
    middle(downs, 2, 2)
    middle(ups, 0, 0)
    back4(0, 1)
    back3(0, 2)
    back2(1, 0)
    token_part(1)
    back1(1, 1)
    middle(downs, 1, 1)
    middle(downs, 2, 1)
    middle(ups, 0, 2)
    token_part(2)
    back1(1, 2)
    back4(0, 2)
    back3(1, 0)
    back2(1, 1)
    down_end(0)
    down_end(1)
    middle(ups, 0, 1)
    down_end(2)
    last(ups, 0)
    go(y_return)
    middle(ups, 1, 0)
    back4(1, 0)
    back3(1, 1)
    back2(1, 2)
    middle(ups, 1, 2)
    back4(1, 1)
    back3(1, 2)
    middle(ups, 1, 1)
    back4(1, 2)
    up_end()
    for copy in sends:
        copy.wait_send()
    for there, copy in guarded:
        @pl.when(there)
        def _():
            copy.wait_send()


def grouped_body(nz, tokens, expert_ids, gates, up_weight, down_weight, cotangent):
    T, D = tokens.shape
    R = 8 * T
    SU, FF = up_weight.shape[1:]
    SD = down_weight.shape[1]
    H = FF // 2
    N = CHUNKS
    anyspace = pl.BlockSpec(memory_space=pl.ANY)
    vmem = pl.BlockSpec(memory_space=pltpu.VMEM)
    sem = pltpu.SemaphoreType.DMA
    V = pltpu.VMEM

    def pair(*shape):
        return [sem(shape), sem(shape)]

    scratch = [
        V((D, H), BF16), V((H, D), BF16), V((R, D), BF16), V((R, D), BF16),
        V((SU, FF), BF16), V((FF, FF), BF16), V((SU, H), BF16),
        V((8, 8, T), F32), V((R, LANES), F32), V((R, H), F32), V((R, H), F32),
        V((R, H), BF16), V((R, H), BF16), V((D, H), BF16), V((H, D), BF16),
        V((2, 2, nz, SU, H), BF16), V((2, nz, SD, D), BF16), V((SU, H), BF16),
        V((4 * T, D), BF16), V((4 * T, D), BF16), V((2 * T, D), BF16), V((2 * T, D), BF16),
        V((T, D), BF16), V((T, D), BF16),
        sem((4,)),
        *pair(2, 2, nz), *pair(N, 2, nz), *pair(1),
        *pair(2, N), *pair(2, N), *pair(2, N), *pair(2, N), *pair(2, N, 4), *pair(7),
        sem((2, nz)), sem((2, 2, nz)), sem((N, nz)), sem((N, 2, nz)), *pair(1),
        *pair(2, N), *pair(2, N, 3), *pair(2, N, 2),
    ]
    return pl.pallas_call(
        functools.partial(grouped, nz),
        out_shape=(
            jax.ShapeDtypeStruct((T, D), BF16),
            jax.ShapeDtypeStruct((T, D), BF16),
            jax.ShapeDtypeStruct((1, SU, FF), BF16),
            jax.ShapeDtypeStruct((1, SD, D), BF16),
        ),
        in_specs=[anyspace, anyspace, vmem, vmem, anyspace, anyspace],
        out_specs=(vmem, vmem, vmem, vmem),
        scratch_shapes=scratch,
        compiler_params=pltpu.CompilerParams(
            collective_id=0, has_side_effects=True, vmem_limit_bytes=64 * 1024 * 1024 - 262144
        ),
    )(tokens, cotangent, expert_ids.T, gates.T, up_weight, down_weight)


def solution(mesh):
    placed = (
        P(("fsdp", "ep"), None),
        P(("fsdp", "ep"), None),
        P(("fsdp", "ep"), None),
        P("ep", "fsdp", None),
        P("ep", "fsdp", None),
        P(("fsdp", "ep"), None),
    )
    nf, ne = mesh.shape["fsdp"], mesh.shape["ep"]
    run = functools.partial(grouped_body, 4) if (nf, ne) == (8, 4) else body
    return jax.shard_map(
        run,
        mesh=mesh,
        in_specs=placed,
        out_specs=(
            P(("fsdp", "ep"), None),
            P(("fsdp", "ep"), None),
            P("ep", "fsdp", None),
            P("ep", "fsdp", None),
        ),
        check_vma=False,
    )
```

```python
import functools

import jax
import jax.numpy as jnp
from jax import lax
from jax.experimental import pallas as pl
from jax.experimental.pallas import tpu as pltpu
from jax.sharding import PartitionSpec as P

F32 = jnp.float32
BF16 = jnp.bfloat16
MESH = pl.DeviceIdType.MESH
LANES = 128
WIDTHS = (512, 1024, 1024, 512)


def gelu_parts(pre):
    root = 0.7978845608028654
    inner = root * (pre + 0.044715 * pre * pre * pre)
    tanh_val = jnp.tanh(inner)
    value = 0.5 * pre * (1.0 + tanh_val)
    slope = 0.5 * (1.0 + tanh_val) + 0.5 * pre * (1.0 - tanh_val * tanh_val) * root * (
        1.0 + 3.0 * 0.044715 * pre * pre
    )
    return (value, slope)


def dot(left, right, dims):
    return lax.dot_general(left, right, (dims, ((), ())), preferred_element_type=F32)


NN = ((1,), (0,))
NT = ((1,), (1,))
TN = ((0,), (0,))


def tail_rows(size):
    return max(16, size // 6 // 16 * 16)


def tiles(count, size):
    def run(fn):
        @pl.loop(0, count // size)
        def _(i):
            fn(pl.ds(pl.multiple_of(i * size, size), size))

    return run


def kernel(
    nz, ny, nx,
    tok_in, cot_in, gate_in, up_in, down_in,
    mixed_out, tg_out, ug_out, dg_out,
    up, down, tok, cot, gate, slope, hidden, dpre, upart, dpart,
    ry_u, ry_d, rz_u, rz_d, rt_u, rt_d, ft_u, ft_d, rc_m, rc_t, rx_m, rx_t,
    local_sem, wz_s, wz_r, wt_s, wt_r, wo_s, wo_r, wy_s, wy_r,
    tx_s, tx_r, tc_s, tc_r, g_s, g_r,
    ry_s, ry_r, rz_s, rz_r, rt_s, rt_r, ft_s, ft_r, rc_s, rc_r, rx_s, rx_r,
):
    ne = 2 * nx
    f = lax.axis_index("fsdp")
    e = lax.axis_index("ep")
    z, y = lax.div(f, ny), lax.rem(f, ny)
    x, c = lax.div(e, 2), lax.rem(e, 2)
    T = tok_in.shape[0]
    D = tok_in.shape[1]
    R = ne * T
    FF = up.shape[1]

    def zp(k):
        return lax.rem(z + k + nz, nz)

    def inside(zz):
        return (zz >= 0) & (zz < nz)

    def yp(j):
        return lax.rem(y + j + ny, ny)

    def xp(k):
        return lax.rem(x + k + nx, nx)

    def fdev(zz, yy):
        return {"fsdp": zz * ny + yy}

    def edev(xx, cc):
        return {"ep": xx * 2 + cc}

    def rows(ref, index, size):
        return ref.at[pl.ds(pl.multiple_of(index * size, size), size)]

    def remote(src, dst, ss, rs, dev):
        return pltpu.make_async_remote_copy(
            src_ref=src, dst_ref=dst, send_sem=ss, recv_sem=rs,
            device_id=dev, device_id_type=MESH,
        )

    sends = []
    guarded = []

    def send_when(there, copies):
        @pl.when(there)
        def _():
            for copy in copies:
                copy.start()

        guarded.append((there, copies))


    def send(src, dst, ss, rs, dev):
        copy = remote(src, dst, ss, rs, dev)
        copy.start()
        sends.append(copy)
        return copy

    barrier = pltpu.get_barrier_semaphore()
    peers = [fdev(zp(k), y) for k in range(1, nz)]
    peers += [fdev(z, yp(j)) for j in range(1, ny)]
    peers += [{"ep": lax.rem(e + i, ne)} for i in range(1, ne)]
    for dev in peers:
        pl.semaphore_signal(barrier, inc=1, device_id=dev, device_id_type=MESH)
    locals_ = []
    for i, (src, dst) in enumerate((
        (up_in.at[0], rows(up, f, up_in.shape[1])),
        (down_in.at[0], rows(down, f, down_in.shape[1])),
        (tok_in, rows(tok, e, T)),
        (cot_in, rows(cot, e, T)),
    )):
        copy = pltpu.make_async_copy(src, dst, local_sem.at[i])
        copy.start()
        locals_.append(copy)
    rows(gate, e, T)[...] = gate_in[e]
    pl.semaphore_wait(barrier, len(peers))

    weights = ((up_in, up), (down_in, down))

    def span(ref, index, size, begin, count):
        return ref.at[pl.ds(pl.multiple_of(index * size + begin, 16), count)]

    def chain(w, sgn, b, src=None):
        full = weights[w][1]
        size = weights[w][0].shape[1]
        block = rows(full, b * ny + y, size)
        way = (1 - sgn) // 2
        return remote(block if src is None else src, block, wz_s.at[w, way, b],
                      wz_r.at[w, way, b], fdev(zp(sgn), y))

    def chain_tail(w, sgn, b, j):
        full = weights[w][1]
        size = weights[w][0].shape[1]
        q = tail_rows(size)
        block = span(full, b * ny + yp(-j), size, size - q, q)
        way = (1 - sgn) // 2
        return remote(block, block, wt_s.at[w, way, b, j - 1], wt_r.at[w, way, b, j - 1],
                      fdev(zp(sgn), y))

    def across(w, b, yy, j):
        full = weights[w][1]
        size = weights[w][0].shape[1]
        block = span(full, b * ny + yy, size, 0, size - tail_rows(size))
        return remote(block, block, wy_s.at[w, b, j - 1], wy_r.at[w, b, j - 1], fdev(z, yp(j)))

    def own_across(w, yy, j, src=None):
        full = weights[w][1]
        size = weights[w][0].shape[1]
        block = rows(full, z * ny + yy, size)
        return remote(block if src is None else src, block, wo_s.at[w, j - 1], wo_r.at[w, j - 1],
                      fdev(z, yp(j)))

    def weight_start(w):
        src = weights[w][0].at[0]
        for sgn in (1, -1):
            send_when(inside(z + sgn), [chain(w, sgn, z, src)])
        for j in range(1, ny):
            copy = own_across(w, y, j, src)
            copy.start()
            sends.append(copy)

    def tail_start(w):
        for j in range(1, ny):
            own_across(w, yp(-j), j).wait_recv()
        for sgn in (1, -1):
            send_when(inside(z + sgn), [chain_tail(w, sgn, z, j) for j in range(1, ny)])

    def hop(w, s):
        for sgn in (1, -1):
            b = zp(-sgn * s)
            there = inside(z - sgn * s)

            @pl.when(there)
            def _():
                chain(w, sgn, b).wait_recv()

            send_when(there & inside(z + sgn), [chain(w, sgn, b)])
            send_when(there, [across(w, b, y, j) for j in range(1, ny)])

    def hop_tail(w, s):
        for sgn in (1, -1):
            b = zp(-sgn * s)
            there = inside(z - sgn * s)

            @pl.when(there)
            def _():
                for j in range(1, ny):
                    chain_tail(w, sgn, b, j).wait_recv()

            send_when(there & inside(z + sgn), [chain_tail(w, sgn, b, j) for j in range(1, ny)])

    def weight_wait(w):
        locals_[w].wait()
        for k in range(1, nz):
            for j in range(1, ny):
                across(w, zp(k), yp(-j), j).wait_recv()

    acts = ((tok_in, tok), (cot_in, cot))

    def act_start(w):
        src, full = acts[w]
        for k in range(1, nx):
            send(src, rows(full, e, T), tx_s.at[w, k - 1], tx_r.at[w, k - 1], edev(xp(k), c))
        send(src, rows(full, e, T), tc_s.at[w, 0], tc_r.at[w, 0], edev(x, 1 - c))

    def act_forward(w):
        src, full = acts[w]
        started = []
        for k in range(1, nx):
            block = rows(full, xp(-k) * 2 + c, T)
            remote(block, block, tx_s.at[w, k - 1], tx_r.at[w, k - 1],
                   edev(xp(k), c)).wait_recv()
            copy = remote(block, block, tc_s.at[w, k], tc_r.at[w, k], edev(x, 1 - c))
            copy.start()
            started.append(copy)
        return started

    def act_wait(w):
        src, full = acts[w]
        locals_[2 + w].wait()
        for k in range(nx):
            block = rows(full, xp(-k) * 2 + 1 - c, T)
            remote(block, block, tc_s.at[w, k], tc_r.at[w, k], edev(x, 1 - c)).wait_recv()

    weight_start(0)
    act_start(0)
    for i in range(1, ne):
        other = lax.rem(e + i, ne)
        send(gate_in.at[other], rows(gate, e, T), g_s.at[i - 1], g_r.at[i - 1], {"ep": other})
    act_start(1)
    hop(0, 1)
    tok_forwards = act_forward(0)
    tail_start(0)
    hop(0, 2)
    hop_tail(0, 1)
    hop(0, 3)
    weight_start(1)
    hop_tail(0, 2)
    hop_tail(0, 3)
    cot_forwards = act_forward(1)

    act_wait(1)
    for copy in cot_forwards:
        copy.wait_send()
    for i in range(1, ne):
        block = rows(gate, lax.rem(e - i + ne, ne), T)
        remote(block, block, g_s.at[i - 1], g_r.at[i - 1], {"ep": lax.rem(e + i, ne)}).wait_recv()

    @tiles(R, 16)
    def _(r):
        cot[r, :] = (cot[r, :].astype(F32) * gate[r, 0:1]).astype(BF16)

    act_wait(0)
    hop(1, 1)
    tail_start(1)
    weight_wait(0)

    @tiles(FF, 256)
    def _(n):
        slope[:, n] = dot(tok[...], up[:, n], NN)

    hop(1, 2)
    hop_tail(1, 1)

    @tiles(R, 16)
    def _(r):
        value, grad = gelu_parts(slope[r, :])
        hidden[r, :] = value.astype(BF16)
        slope[r, :] = grad

    @tiles(D, 512)
    def _(n):
        dpart[:, n] = dot(hidden[...], cot[:, n], TN).astype(BF16)

    parts = ((upart, ry_u, rz_u, rt_u, ft_u, ug_out), (dpart, ry_d, rz_d, rt_d, ft_d, dg_out))

    flip = lax.div(z, 2)
    near = z + flip * (3 - 2 * z)
    order = [d + flip * (3 - 2 * d) for d in (near * 0 + 3, 2 - 2 * near, 1 + near, near)]

    def give(w, d, yy, j):
        part, ry = parts[w][:2]
        size = parts[w][-1].shape[1]
        return remote(span(part, d * ny + yy, size, 0, size - tail_rows(size)),
                      ry.at[(j - 1) * nz + d], ry_s.at[w, d, j - 1], ry_r.at[w, d, j - 1],
                      fdev(z, yp(j)))

    def run_block(w, way, d, nxt):
        part, ry, rz = parts[w][:3]
        size = parts[w][-1].shape[1]
        return remote(rows(part, d * ny + y, size), rz.at[way, d], rz_s.at[w, d],
                      rz_r.at[w, way, d], fdev(nxt, y))

    def run_tail(w, way, d, nxt, j):
        part, rt = parts[w][0], parts[w][3]
        size = parts[w][-1].shape[1]
        q = tail_rows(size)
        return remote(span(part, d * ny + yp(j), size, size - q, q), rt.at[way, d, j - 1],
                      rt_s.at[w, d, j - 1], rt_r.at[w, way, d, j - 1], fdev(nxt, y))

    def last_tail(w, j):
        part, ft = parts[w][0], parts[w][4]
        size = parts[w][-1].shape[1]
        q = tail_rows(size)
        return remote(span(part, z * ny + yp(j), size, size - q, q), ft.at[j - 1],
                      ft_s.at[w, j - 1], ft_r.at[w, j - 1], fdev(z, yp(j)))

    def part_start(w):
        for d in order:
            for j in range(1, ny):
                copy = give(w, d, yp(j), j)
                copy.start()
                sends.append(copy)

    def add(part, start, count, others):
        @tiles(count, 16)
        def _(r):
            at = pl.ds(pl.multiple_of(start + r.start, 16), 16)
            total = part[at, :].astype(F32)
            for other in others:
                total += other[r, :].astype(F32)
            part[at, :] = total.astype(BF16)

    def pair(w, d):
        part, ry = parts[w][:2]
        size = parts[w][-1].shape[1]
        for j in range(1, ny):
            give(w, d, y, j).wait_recv()
        add(part, (d * ny + y) * size, size - tail_rows(size),
            [ry.at[(j - 1) * nz + d] for j in range(1, ny)])

    def run(w, p):
        part, ry, rz, rt = parts[w][:4]
        size = parts[w][-1].shape[1]
        q = tail_rows(size)
        d = order[p]
        way = jnp.where(d > z, 0, 1)
        sgn = 1 - 2 * way
        nxt = z + sgn
        pair(w, d)

        @pl.when(inside(z - sgn))
        def _():
            run_block(w, way, d, nxt).wait_recv()
            for j in range(1, ny):
                run_tail(w, way, d, nxt, j).wait_recv()
            add(part, (d * ny + y) * size, size, [rz.at[way, d]])
            for j in range(1, ny):
                add(part, (d * ny + yp(j)) * size + size - q, q, [rt.at[way, d, j - 1]])

        copies = [run_block(w, way, d, nxt)]
        copies += [run_tail(w, way, d, nxt, j) for j in range(1, ny)]
        for copy in copies:
            copy.start()
            sends.append(copy)

    def part_last(w):
        part, ry, rz, rt = parts[w][:4]
        size = parts[w][-1].shape[1]
        q = tail_rows(size)
        pair(w, z)
        for way in range(2):
            sgn = 1 - 2 * way

            @pl.when(inside(z - sgn))
            def _():
                for j in range(1, ny):
                    run_tail(w, way, z, zp(1), j).wait_recv()
                    add(part, (z * ny + yp(j)) * size + size - q, q, [rt.at[way, z, j - 1]])

        for j in range(1, ny):
            copy = last_tail(w, j)
            copy.start()
            sends.append(copy)
        for way in range(2):
            sgn = 1 - 2 * way

            @pl.when(inside(z - sgn))
            def _():
                run_block(w, way, z, zp(1)).wait_recv()
                add(part, (z * ny + y) * size, size, [rz.at[way, z]])

    def part_end(w):
        part, ry, rz, rt, ft, out = parts[w]
        size = out.shape[1]
        q = tail_rows(size)
        for j in range(1, ny):
            last_tail(w, j).wait_recv()
        add(part, (z * ny + y) * size + size - q, q, [ft.at[j - 1] for j in range(1, ny)])

        @tiles(size, 16)
        def _(r):
            out[0, r, :] = part[pl.ds(pl.multiple_of(f * size + r.start, 16), 16), :]

    backs = ((cot, rc_m, rx_m, mixed_out), (tok, rc_t, rx_t, tg_out))

    def back_start(w):
        full, rc, rx, out = backs[w]
        for k in range(nx):
            k = (k + 1) % nx
            send(rows(full, xp(k) * 2 + 1 - c, T), rc.at[k], rc_s.at[w, k], rc_r.at[w, k],
                 edev(x, 1 - c))

    def back_pair(w):
        full, rc, rx, out = backs[w]
        for k in range(nx):
            k = (k + 1) % nx
            index = xp(k) * 2 + c
            slot = rc.at[k]
            remote(slot, slot, rc_s.at[w, k], rc_r.at[w, k], edev(x, 1 - c)).wait_recv()

            @tiles(T, 16)
            def _(r):
                at = pl.ds(pl.multiple_of(index * T + r.start, 16), 16)
                full[at, :] = (full[at, :].astype(F32) + rc[k, r, :].astype(F32)).astype(BF16)

            if k:
                send(rows(full, index, T), rx.at[k - 1], rx_s.at[w, k - 1], rx_r.at[w, k - 1],
                     edev(xp(k), c))

    def back_end(w):
        full, rc, rx, out = backs[w]
        for k in range(1, nx):
            slot = rx.at[k - 1]
            remote(slot, slot, rx_s.at[w, k - 1], rx_r.at[w, k - 1], edev(xp(k), c)).wait_recv()

        @tiles(T, 16)
        def _(r):
            at = pl.ds(pl.multiple_of(e * T + r.start, 16), 16)
            total = full[at, :].astype(F32)
            for k in range(1, nx):
                total += rx[k - 1, r, :].astype(F32)
            out[r, :] = total.astype(BF16)

    hop(1, 3)
    hop_tail(1, 2)
    part_start(1)
    hop_tail(1, 3)
    weight_wait(1)

    @tiles(FF, 256)
    def _(n):
        dpre[:, n] = (dot(cot[...], down[n, :], NT) * slope[:, n]).astype(BF16)

    run(1, 0)

    @tiles(D, 384)
    def _(n):
        upart[n, :] = dot(tok[:, n], dpre[...], TN).astype(BF16)

    part_start(0)
    run(1, 1)

    @tiles(D, 512)
    def _(n):
        cot[:, n] = (dot(hidden[...], down[:, n], NN) * gate[:, 0:1]).astype(BF16)

    back_start(0)
    run(1, 2)
    for copy in tok_forwards:
        copy.wait_send()

    @tiles(D, 512)
    def _(n):
        tok[:, n] = dot(dpre[...], up[n, :], NT).astype(BF16)

    back_start(1)
    back_pair(0)
    back_pair(1)
    run(0, 0)
    part_last(1)
    back_end(0)
    run(0, 1)
    back_end(1)
    part_end(1)
    run(0, 2)
    part_last(0)
    part_end(0)
    for copy in sends:
        copy.wait_send()
    for there, copies in guarded:
        @pl.when(there)
        def _():
            for copy in copies:
                copy.wait_send()


def body(tokens, expert_ids, gates, up_weight, down_weight, cotangent):
    nf, ne = lax.axis_size("fsdp"), lax.axis_size("ep")
    nz = 4
    ny, nx = nf // nz, ne // 2
    T, D = tokens.shape
    R = ne * T
    su, FF = up_weight.shape[1:]
    sd = down_weight.shape[1]
    chosen = expert_ids[None] == jnp.arange(ne, dtype=jnp.int32)[:, None, None]
    dense = jnp.sum(jnp.where(chosen, gates[None], 0.0), axis=2)
    gcols = jnp.broadcast_to(dense[:, :, None], (ne, T, LANES))
    qu, qd = (tail_rows(size) for size in (su, sd))
    anyspace = pl.BlockSpec(memory_space=pl.ANY)
    vmem = pl.BlockSpec(memory_space=pltpu.VMEM)
    sem = pltpu.SemaphoreType.DMA
    V = pltpu.VMEM
    scratch = [
        V((D, FF), BF16), V((FF, D), BF16), V((R, D), BF16), V((R, D), BF16),
        V((R, LANES), F32), V((R, FF), F32), V((R, FF), BF16), V((R, FF), BF16),
        V((D, FF), BF16), V((FF, D), BF16),
        V(((ny - 1) * nz, su - qu, FF), BF16), V(((ny - 1) * nz, sd - qd, D), BF16),
        V((2, nz, su, FF), BF16), V((2, nz, sd, D), BF16),
        V((2, nz, ny - 1, qu, FF), BF16), V((2, nz, ny - 1, qd, D), BF16),
        V((ny - 1, qu, FF), BF16), V((ny - 1, qd, D), BF16),
        V((nx, T, D), BF16), V((nx, T, D), BF16),
        V((nx - 1, T, D), BF16), V((nx - 1, T, D), BF16),
        sem((4,)),
        sem((2, 2, nz)), sem((2, 2, nz)),
        sem((2, 2, nz, ny - 1)), sem((2, 2, nz, ny - 1)),
        sem((2, ny - 1)), sem((2, ny - 1)),
        sem((2, nz, ny - 1)), sem((2, nz, ny - 1)),
        sem((2, nx - 1)), sem((2, nx - 1)),
        sem((2, nx)), sem((2, nx)),
        sem((ne - 1,)), sem((ne - 1,)),
        sem((2, nz, ny - 1)), sem((2, nz, ny - 1)),
        sem((2, nz)), sem((2, 2, nz)),
        sem((2, nz, ny - 1)), sem((2, 2, nz, ny - 1)),
        sem((2, ny - 1)), sem((2, ny - 1)),
        sem((2, nx)), sem((2, nx)),
        sem((2, nx - 1)), sem((2, nx - 1)),
    ]
    return pl.pallas_call(
        functools.partial(kernel, nz, ny, nx),
        out_shape=(
            jax.ShapeDtypeStruct((T, D), BF16),
            jax.ShapeDtypeStruct((T, D), BF16),
            jax.ShapeDtypeStruct((1, su, FF), BF16),
            jax.ShapeDtypeStruct((1, sd, D), BF16),
        ),
        in_specs=[anyspace, anyspace, vmem, anyspace, anyspace],
        out_specs=(vmem, vmem, vmem, vmem),
        scratch_shapes=scratch,
        compiler_params=pltpu.CompilerParams(
            collective_id=0, has_side_effects=True, vmem_limit_bytes=64 * 1024 * 1024 - 262144
        ),
    )(tokens, cotangent, gcols, up_weight, down_weight)


def grouped(nz, *refs):
    (tok_in, cot_in, ids_in, gate_in, up_in, down_in,
     mixed_out, tg_out, ug_out, dg_out,
     up, down, tok, cot, upl, perm, uex, gd, gcol, slope, dh, hidden, dpre, upart, dpart,
     rz_u, rz_d, yrecv, rc_m, rc_t, r2_m, r2_t, r3_m, r3_t,
     local_sem, us, ur, ds_s, ds_r, yx_s, yx_r, tx_s, tx_r, ty_s, ty_r, fx_s, fx_r, fy_s, fy_r,
     tc_s, tc_r, g_s, g_r, ru_s, ru_r, rd_s, rd_r, yg_s, yg_r, b1_s, b1_r, b2_s, b2_r, b3_s, b3_r) = refs
    f = lax.axis_index("fsdp")
    e = lax.axis_index("ep")
    z, y = lax.div(f, 2), lax.rem(f, 2)
    x, c = lax.div(e, 2), lax.rem(e, 2)
    T, D = tok_in.shape
    SU, FF = up_in.shape[1:]
    SD = down_in.shape[1]
    H = FF // 2
    R = 8 * T
    N = len(WIDTHS)
    begins = [D * sum(WIDTHS[:n]) // sum(WIDTHS) for n in range(N + 1)]

    def inside(zz):
        return (zz >= 0) & (zz < nz)

    def zp(k):
        return lax.rem(z + k + nz, nz)

    def zdev(zz):
        return {"fsdp": lax.rem(zz + nz, nz) * 2 + y}

    ydev = {"fsdp": z * 2 + 1 - y}
    xdev = {"ep": (1 - x) * 2 + c}
    cdev = {"ep": x * 2 + 1 - c}

    def blk(yy, xx, cc):
        return cc * 4 + yy * 2 + xx

    me = blk(y, x, c)

    def rows(index, size):
        return pl.ds(pl.multiple_of(index * size, size), size)

    def lanes(index, size):
        return pl.ds(pl.multiple_of(index * size, size), size)

    def cols(n):
        return pl.ds(begins[n], begins[n + 1] - begins[n])

    def cols_a(n):
        return pl.ds(begins[n], (begins[n + 1] - begins[n]) // 2)

    def cols_b(n):
        half = (begins[n + 1] - begins[n]) // 2
        return pl.ds(begins[n] + half, half)

    def remote(src, dst, ss, rs, dev):
        return pltpu.make_async_remote_copy(
            src_ref=src, dst_ref=dst, send_sem=ss, recv_sem=rs,
            device_id=dev, device_id_type=MESH,
        )

    sends = []
    guarded = []

    def go(copy, keep=sends):
        copy.start()
        keep.append(copy)

    def go_when(there, copy):
        @pl.when(there)
        def _():
            copy.start()

        guarded.append((there, copy))

    barrier = pltpu.get_barrier_semaphore()
    offsets = [(i // 4, i // 2 % 2, i % 2) for i in range(1, 8)]

    def gdev(dy, dx, dc):
        yy = 1 - y if dy else y
        xx = 1 - x if dx else x
        cc = 1 - c if dc else c
        return yy, xx, cc

    peers = [{"fsdp": zp(k) * 2 + y, "ep": e} for k in range(1, nz)]
    for offset in offsets:
        yy, xx, cc = gdev(*offset)
        peers.append({"fsdp": z * 2 + yy, "ep": xx * 2 + cc})
    for dev in peers:
        pl.semaphore_signal(barrier, inc=1, device_id=dev, device_id_type=MESH)
    locals_ = []
    for i, (src, dst) in enumerate((
        (up_in.at[0], upl),
        (down_in.at[0], down.at[rows(z, SD)]),
        (tok_in, tok.at[rows(me, T)]),
        (cot_in, cot.at[rows(me, T)]),
    )):
        copy = pltpu.make_async_copy(src, dst, local_sem.at[i])
        copy.start()
        locals_.append(copy)

    expert = lax.broadcasted_iota(jnp.int32, (8, T), 0)
    gd[me] = jnp.where(ids_in[0:1, :] == expert, gate_in[0:1, :], 0.0) + jnp.where(
        ids_in[1:2, :] == expert, gate_in[1:2, :], 0.0)

    @pl.loop(0, 2 * nz)
    def _(i):
        half, zz = lax.div(i, nz), lax.rem(i, nz)
        column = lax.broadcasted_iota(jnp.int32, (SD, FF), 1)
        unit = lax.broadcasted_iota(jnp.int32, (SD, FF), 0) + SD * (2 * zz + half)
        perm[rows(i, SD), :] = jnp.where(column == unit, 1.0, 0.0).astype(BF16)

    pl.semaphore_wait(barrier, len(peers))

    def permute_up():
        locals_[0].wait()
        up[rows(f, SU), :] = dot(upl[...], perm[rows(y, H), :], NT).astype(BF16)
        uex[...] = dot(upl[...], perm[rows(1 - y, H), :], NT).astype(BF16)
        locals_[1].wait()

    def sub(p):
        return y if p == 0 else 1 - y

    def chain_u(p, sgn, b):
        block = up.at[rows(2 * b + sub(p), SU)]
        way = (1 - sgn) // 2
        return remote(block, block, us.at[p, way, b], ur.at[p, way, b], zdev(z + sgn))

    def chain_d(n, sgn, b):
        block = down.at[rows(b, SD), cols(n)]
        way = (1 - sgn) // 2
        return remote(block, block, ds_s.at[n, way, b], ds_r.at[n, way, b], zdev(z + sgn))

    def own_start(chain, n):
        for sgn in (1, -1):
            go_when(inside(z + sgn), chain(n, sgn, z))

    def hop(chain, n, s):
        for sgn in (1, -1):
            b = zp(-sgn * s)
            there = inside(z - sgn * s)

            @pl.when(there)
            def _():
                chain(n, sgn, b).wait_recv()

            go_when(there & inside(z + sgn), chain(n, sgn, b))

    y_exchange = remote(uex, up.at[rows(f, SU)], yx_s.at[0], yx_r.at[0], ydev)

    acts = ((tok_in, tok), (cot_in, cot))
    forwards = ([[] for _ in range(N)], [[] for _ in range(N)])

    def act_own(w, n):
        src, full = acts[w]
        there = full.at[rows(me, T), cols(n)]
        go(remote(src.at[:, cols(n)], there, tx_s.at[w, n], tx_r.at[w, n], xdev))
        go(remote(src.at[:, cols(n)], there, ty_s.at[w, n], ty_r.at[w, n], ydev))
        go(remote(src.at[:, cols(n)], there, tc_s.at[w, n, 0], tc_r.at[w, n, 0], cdev))

    def act_fwd(w, n):
        full = acts[w][1]
        keep = forwards[w][n]
        bx, by = blk(y, 1 - x, c), blk(1 - y, x, c)
        here = full.at[rows(bx, T), cols(n)]
        part = full.at[rows(bx * 2 + 1, T // 2), cols(n)]
        remote(here, here, tx_s.at[w, n], tx_r.at[w, n], xdev).wait_recv()
        go(remote(part, part, fy_s.at[w, n], fy_r.at[w, n], ydev), keep)
        go(remote(here, here, tc_s.at[w, n, 1], tc_r.at[w, n, 1], cdev), keep)
        here = full.at[rows(by, T), cols(n)]
        part = full.at[rows(by * 2, T // 2), cols(n)]
        remote(here, here, ty_s.at[w, n], ty_r.at[w, n], ydev).wait_recv()
        go(remote(part, part, fx_s.at[w, n], fx_r.at[w, n], xdev), keep)
        go(remote(here, here, tc_s.at[w, n, 2], tc_r.at[w, n, 2], cdev), keep)

    def act_diag(w, n):
        full = acts[w][1]
        bd = blk(1 - y, 1 - x, c)
        low = full.at[rows(bd * 2, T // 2), cols(n)]
        high = full.at[rows(bd * 2 + 1, T // 2), cols(n)]
        here = full.at[rows(bd, T), cols(n)]
        remote(low, low, fx_s.at[w, n], fx_r.at[w, n], xdev).wait_recv()
        remote(high, high, fy_s.at[w, n], fy_r.at[w, n], ydev).wait_recv()
        go(remote(here, here, tc_s.at[w, n, 3], tc_r.at[w, n, 3], cdev), forwards[w][n])

    def act_done(w, n):
        full = acts[w][1]
        others = ((y, x), (y, 1 - x), (1 - y, x), (1 - y, 1 - x))
        for k, (yy, xx) in enumerate(others):
            here = full.at[rows(blk(yy, xx, 1 - c), T), cols(n)]
            remote(here, here, tc_s.at[w, n, k], tc_r.at[w, n, k], cdev).wait_recv()

    def gates_start():
        for i, offset in enumerate(offsets):
            yy, xx, cc = gdev(*offset)
            go(remote(gd.at[me], gd.at[me], g_s.at[i], g_r.at[i],
                      {"fsdp": z * 2 + yy, "ep": xx * 2 + cc}))

    def gates_done():
        for i, offset in enumerate(offsets):
            yy, xx, cc = gdev(*offset)
            here = gd.at[blk(yy, xx, cc)]
            remote(here, here, g_s.at[i], g_r.at[i],
                   {"fsdp": z * 2 + yy, "ep": xx * 2 + cc}).wait_recv()

        @pl.loop(0, 8)
        def _(b):
            mine = lax.broadcasted_iota(jnp.int32, (8, T), 0) == e
            row = jnp.sum(jnp.where(mine, gd[b], 0.0), axis=0, keepdims=True)
            eye = lax.broadcasted_iota(jnp.int32, (T, T), 0) == lax.broadcasted_iota(
                jnp.int32, (T, T), 1)
            column = jnp.sum(jnp.where(eye, row, 0.0), axis=1, keepdims=True)
            gcol[rows(b, T), :] = jnp.broadcast_to(column, (T, LANES))

    flip = lax.div(z, 2)
    near = z + flip * (3 - 2 * z)
    order = [d + flip * (3 - 2 * d) for d in (near * 0 + 3, 2 - 2 * near, 1 + near, near)]
    is_end = near == 0

    def pre_step(s):
        plane = order[3 - s]
        if s == 0:
            locals_[2].wait()
            locals_[3].wait()

        @tiles(R, 256)
        def _(r):
            part = dot(tok[r, lanes(plane, 2 * SU)], up[rows(plane, 2 * SU), :], NN)
            if s == 0:
                slope[r, :] = part
            elif s < nz - 1:
                slope[r, :] += part
            else:
                value, grad = gelu_parts(slope[r, :] + part)
                hidden[r, :] = (value * gcol[r, 0:1]).astype(BF16)
                slope[r, :] = grad * gcol[r, 0:1]

    def tokens_sent():
        for copies in forwards[0]:
            for copy in copies:
                copy.wait_send()

    def chunk_tiles(n, size):
        def run(fn):
            @pl.loop(0, (begins[n + 1] - begins[n]) // size)
            def _(i):
                fn(pl.ds(pl.multiple_of(begins[n] + i * size, size), size))

        return run

    def down_part(n):
        @chunk_tiles(n, 512)
        def _(t):
            dpart[:, t] = dot(hidden[...], cot[:, t], TN).astype(BF16)

    def back_hidden(n):
        @tiles(R, 256)
        def _(r):
            part = dot(cot[r, cols(n)], down[:, cols(n)], NT)
            if n == 0:
                dh[r, :] = part
            elif n < N - 1:
                dh[r, :] += part
            else:
                dpre[r, :] = ((dh[r, :] + part) * slope[r, :]).astype(BF16)

    def mixed_part(n):
        for copy in forwards[1][n]:
            copy.wait_send()

        @chunk_tiles(n, 512)
        def _(t):
            @tiles(R, 512)
            def _(r):
                cot[r, t] = dot(hidden[r, :], down[:, t], NN).astype(BF16)

    def token_part(n):
        @chunk_tiles(n, 512)
        def _(t):
            @tiles(R, 512)
            def _(r):
                tok[r, t] = dot(dpre[r, :], up[t, :], NT).astype(BF16)

    def up_part(q, pos):
        at = rows(2 * order[pos] + (1 - sub(q)), SU)
        upart[at, :] = dot(tok[:, at], dpre[...], TN).astype(BF16)

    def send_down(n, d, way, nxt):
        return remote(dpart.at[rows(d, SD), cols(n)], rz_d.at[way, d, :, cols(n)],
                      rd_s.at[n, d], rd_r.at[n, way, d], zdev(nxt))

    def send_up(q, d, way, nxt):
        return remote(upart.at[rows(2 * d + (1 - sub(q)), SU)], rz_u.at[q, way, d],
                      ru_s.at[q, d], ru_r.at[q, way, d], zdev(nxt))

    def add_down(n, d, way):
        @tiles(SD, 16)
        def _(r):
            at = pl.ds(pl.multiple_of(d * SD + r.start, 16), 16)
            dpart[at, cols(n)] = (dpart[at, cols(n)].astype(F32)
                                  + rz_d[way, d, r, cols(n)].astype(F32)).astype(BF16)

    def add_up(q, d, way):
        @tiles(SU, 32)
        def _(r):
            at = pl.ds(pl.multiple_of((2 * d + (1 - sub(q))) * SU + r.start, 32), 32)
            upart[at, :] = (upart[at, :].astype(F32)
                            + rz_u[q, way, d, r, :].astype(F32)).astype(BF16)

    downs, ups = (send_down, add_down), (send_up, add_up)

    def course(pos):
        d = order[pos]
        way = jnp.where(d > z, 0, 1)
        return d, way, z + 1 - 2 * way

    def begin(kind, n, pos):
        d, way, nxt = course(pos)
        go_when(is_end, kind[0](n, d, way, nxt))

    def middle(kind, n, pos):
        d, way, nxt = course(pos)
        copy = kind[0](n, d, way, nxt)

        @pl.when(jnp.logical_not(is_end))
        def _():
            copy.wait_recv()
            kind[1](n, d, way)
            copy.start()

        guarded.append((jnp.logical_not(is_end), copy))

    def last(kind, n):
        for way in range(2):
            @pl.when(inside(z - 1 + 2 * way))
            def _():
                kind[0](n, z, way, zp(1)).wait_recv()
                kind[1](n, z, way)

    def down_end(n):
        last(downs, n)

        @tiles(SD, 16)
        def _(r):
            dg_out[0, r, cols(n)] = dpart[pl.ds(pl.multiple_of(z * SD + r.start, 16), 16), cols(n)]

    other_up = upart.at[rows(2 * z + 1 - y, SU)]
    y_return = remote(other_up, yrecv, yg_s.at[0], yg_r.at[0], ydev)

    def up_end():
        last(ups, 1)
        y_return.wait_recv()
        ug_out[0] = (dot(upart[rows(f, SU), :], perm[rows(y, H), :], NN)
                     + dot(yrecv[...], perm[rows(1 - y, H), :], NN)).astype(BF16)

    backs = ((cot, rc_m, r2_m, r3_m, mixed_out), (tok, rc_t, r2_t, r3_t, tg_out))
    G = 4 * T

    def back1(w, n):
        full, rc = backs[w][:2]
        go(remote(full.at[rows(1 - c, G), cols(n)], rc.at[:, cols(n)],
                  b1_s.at[w, n], b1_r.at[w, n], cdev))

    def back2(w, n):
        full, rc, r2 = backs[w][:3]
        here = rc.at[:, cols(n)]
        remote(here, here, b1_s.at[w, n], b1_r.at[w, n], cdev).wait_recv()

        @tiles(G, 16)
        def _(r):
            at = pl.ds(pl.multiple_of(c * G + r.start, 16), 16)
            full[at, cols(n)] = (full[at, cols(n)].astype(F32)
                                 + rc[r, cols(n)].astype(F32)).astype(BF16)

        for yy in range(2):
            go(remote(full.at[rows(blk(yy, 1 - x, c), T), cols_a(n)],
                      r2.at[pl.ds(yy * T, T), cols_a(n)],
                      b2_s.at[w, n, yy], b2_r.at[w, n, yy], xdev))
        go(remote(full.at[rows(c * 2 + 1 - y, 2 * T), cols_b(n)], r2.at[:, cols_b(n)],
                  b2_s.at[w, n, 2], b2_r.at[w, n, 2], ydev))

    def back3(w, n):
        full, rc, r2, r3 = backs[w][:4]
        for yy in range(2):
            here = r2.at[pl.ds(yy * T, T), cols_a(n)]
            remote(here, here, b2_s.at[w, n, yy], b2_r.at[w, n, yy], xdev).wait_recv()
        here = r2.at[:, cols_b(n)]
        remote(here, here, b2_s.at[w, n, 2], b2_r.at[w, n, 2], ydev).wait_recv()
        ba, bb = blk(1 - y, x, c), blk(y, 1 - x, c)

        @tiles(T, 16)
        def _(r):
            at = pl.ds(pl.multiple_of(ba * T + r.start, 16), 16)
            there = pl.ds(pl.multiple_of((1 - y) * T + r.start, 16), 16)
            full[at, cols_a(n)] = (full[at, cols_a(n)].astype(F32)
                                   + r2[there, cols_a(n)].astype(F32)).astype(BF16)
            at = pl.ds(pl.multiple_of(bb * T + r.start, 16), 16)
            there = pl.ds(pl.multiple_of((1 - x) * T + r.start, 16), 16)
            full[at, cols_b(n)] = (full[at, cols_b(n)].astype(F32)
                                   + r2[there, cols_b(n)].astype(F32)).astype(BF16)

        go(remote(full.at[rows(ba, T), cols_a(n)], r3.at[:, cols_a(n)],
                  b3_s.at[w, n, 0], b3_r.at[w, n, 0], ydev))
        go(remote(full.at[rows(bb, T), cols_b(n)], r3.at[:, cols_b(n)],
                  b3_s.at[w, n, 1], b3_r.at[w, n, 1], xdev))

    def back4(w, n):
        full, rc, r2, r3, out = backs[w]
        for k, (span, dev) in enumerate(((cols_a(n), ydev), (cols_b(n), xdev))):
            here = r3.at[:, span]
            remote(here, here, b3_s.at[w, n, k], b3_r.at[w, n, k], dev).wait_recv()

        @tiles(T, 16)
        def _(r):
            at = pl.ds(pl.multiple_of(me * T + r.start, 16), 16)
            for span, lane in ((cols_a(n), y), (cols_b(n), x)):
                there = pl.ds(pl.multiple_of(lane * T + r.start, 16), 16)
                out[r, span] = (full[at, span].astype(F32) + r2[there, span].astype(F32)
                                + r3[r, span].astype(F32)).astype(BF16)

    permute_up()
    own_start(chain_d, 0)
    go(y_exchange)
    act_own(0, 2)
    act_own(0, 3)
    own_start(chain_u, 0)
    hop(chain_d, 0, 1)
    y_exchange.wait_recv()
    act_own(0, 1)
    own_start(chain_u, 1)
    gates_start()
    hop(chain_u, 0, 1)
    act_fwd(0, 3)
    act_fwd(0, 2)
    hop(chain_u, 1, 1)
    act_diag(0, 3)
    act_own(0, 0)
    act_fwd(0, 1)
    hop(chain_u, 0, 2)
    act_diag(0, 2)
    act_fwd(0, 0)
    hop(chain_u, 1, 2)
    act_own(1, 1)
    act_diag(0, 1)
    act_done(0, 2)
    act_diag(0, 0)
    act_done(0, 0)
    act_done(0, 3)
    own_start(chain_d, 1)
    own_start(chain_d, 3)
    act_done(0, 1)
    gates_done()
    act_own(1, 0)
    hop(chain_u, 0, 3)
    hop(chain_d, 0, 2)
    pre_step(0)
    act_fwd(1, 1)
    pre_step(1)
    act_fwd(1, 0)
    pre_step(2)
    own_start(chain_d, 2)
    act_own(1, 3)
    hop(chain_u, 1, 3)
    act_own(1, 2)
    act_diag(1, 1)
    pre_step(3)
    act_done(1, 1)
    act_diag(1, 0)
    down_part(1)
    begin(downs, 1, 2)
    act_done(1, 0)
    begin(downs, 1, 0)
    act_fwd(1, 3)
    hop(chain_d, 1, 1)
    down_part(0)
    act_fwd(1, 2)
    begin(downs, 0, 1)
    begin(downs, 1, 1)
    hop(chain_d, 0, 3)
    act_diag(1, 3)
    back_hidden(0)
    act_done(1, 3)
    mixed_part(0)
    back1(0, 0)
    hop(chain_d, 1, 2)
    down_part(3)
    begin(downs, 0, 0)
    hop(chain_d, 2, 1)
    begin(downs, 3, 2)
    begin(downs, 3, 1)
    act_diag(1, 2)
    back2(0, 0)
    hop(chain_d, 1, 3)
    act_done(1, 2)
    back_hidden(1)
    mixed_part(1)
    back1(0, 1)
    hop(chain_d, 2, 2)
    begin(downs, 0, 2)
    back3(0, 0)
    down_part(2)
    middle(downs, 1, 2)
    back2(0, 1)
    begin(downs, 2, 0)
    begin(downs, 3, 0)
    hop(chain_d, 3, 1)
    hop(chain_d, 2, 3)
    back_hidden(2)
    mixed_part(2)
    back1(0, 2)
    middle(downs, 3, 2)
    middle(downs, 0, 0)
    begin(downs, 2, 1)
    hop(chain_d, 3, 2)
    back3(0, 1)
    hop(chain_d, 3, 3)
    back2(0, 2)
    back_hidden(3)
    up_part(0, 0)
    middle(downs, 1, 0)
    up_part(1, 1)
    mixed_part(3)
    begin(ups, 0, 0)
    up_part(1, 0)
    back1(0, 3)
    up_part(0, 2)
    begin(ups, 1, 0)
    up_part(1, 2)
    up_part(1, 3)
    middle(downs, 0, 1)
    up_part(0, 1)
    up_part(0, 3)
    back4(0, 0)
    back2(0, 3)
    begin(ups, 0, 1)
    tokens_sent()
    middle(downs, 3, 0)
    token_part(1)
    back3(0, 2)
    back1(1, 1)
    token_part(3)
    token_part(0)
    back1(1, 3)
    middle(downs, 2, 0)
    begin(ups, 1, 1)
    begin(ups, 0, 2)
    back3(0, 3)
    middle(downs, 0, 2)
    middle(downs, 1, 1)
    back2(1, 1)
    token_part(2)
    back1(1, 0)
    middle(ups, 0, 0)
    back1(1, 2)
    back2(1, 0)
    back2(1, 2)
    back3(1, 0)
    down_end(1)
    back3(1, 1)
    middle(downs, 3, 1)
    down_end(3)
    middle(ups, 1, 0)
    middle(ups, 0, 1)
    middle(ups, 0, 2)
    down_end(0)
    back2(1, 3)
    middle(ups, 1, 2)
    back4(0, 2)
    begin(ups, 1, 2)
    middle(downs, 2, 1)
    back4(0, 1)
    middle(downs, 2, 2)
    begin(downs, 2, 2)
    back3(1, 2)
    last(ups, 0)
    middle(ups, 1, 1)
    go(y_return)
    back3(1, 3)
    back4(1, 0)
    back4(1, 2)
    up_end()
    back4(1, 1)
    down_end(2)
    back4(0, 3)
    back4(1, 3)
    for copy in sends:
        copy.wait_send()
    for there, copy in guarded:
        @pl.when(there)
        def _():
            copy.wait_send()


def grouped_body(nz, tokens, expert_ids, gates, up_weight, down_weight, cotangent):
    T, D = tokens.shape
    R = 8 * T
    SU, FF = up_weight.shape[1:]
    SD = down_weight.shape[1]
    H = FF // 2
    N = len(WIDTHS)
    anyspace = pl.BlockSpec(memory_space=pl.ANY)
    vmem = pl.BlockSpec(memory_space=pltpu.VMEM)
    sem = pltpu.SemaphoreType.DMA
    V = pltpu.VMEM

    def pair(*shape):
        return [sem(shape), sem(shape)]

    scratch = [
        V((D, H), BF16), V((H, D), BF16), V((R, D), BF16), V((R, D), BF16),
        V((SU, FF), BF16), V((FF, FF), BF16), V((SU, H), BF16),
        V((8, 8, T), F32), V((R, LANES), F32), V((R, H), F32), V((R, H), F32),
        V((R, H), BF16), V((R, H), BF16), V((D, H), BF16), V((H, D), BF16),
        V((2, 2, nz, SU, H), BF16), V((2, nz, SD, D), BF16), V((SU, H), BF16),
        V((4 * T, D), BF16), V((4 * T, D), BF16), V((2 * T, D), BF16), V((2 * T, D), BF16),
        V((T, D), BF16), V((T, D), BF16),
        sem((4,)),
        *pair(2, 2, nz), *pair(N, 2, nz), *pair(1),
        *pair(2, N), *pair(2, N), *pair(2, N), *pair(2, N), *pair(2, N, 4), *pair(7),
        sem((2, nz)), sem((2, 2, nz)), sem((N, nz)), sem((N, 2, nz)), *pair(1),
        *pair(2, N), *pair(2, N, 3), *pair(2, N, 2),
    ]
    return pl.pallas_call(
        functools.partial(grouped, nz),
        out_shape=(
            jax.ShapeDtypeStruct((T, D), BF16),
            jax.ShapeDtypeStruct((T, D), BF16),
            jax.ShapeDtypeStruct((1, SU, FF), BF16),
            jax.ShapeDtypeStruct((1, SD, D), BF16),
        ),
        in_specs=[anyspace, anyspace, vmem, vmem, anyspace, anyspace],
        out_specs=(vmem, vmem, vmem, vmem),
        scratch_shapes=scratch,
        compiler_params=pltpu.CompilerParams(
            collective_id=0, has_side_effects=True, vmem_limit_bytes=64 * 1024 * 1024 - 262144
        ),
    )(tokens, cotangent, expert_ids.T, gates.T, up_weight, down_weight)


def solution(mesh):
    placed = (
        P(("fsdp", "ep"), None),
        P(("fsdp", "ep"), None),
        P(("fsdp", "ep"), None),
        P("ep", "fsdp", None),
        P("ep", "fsdp", None),
        P(("fsdp", "ep"), None),
    )
    nf, ne = mesh.shape["fsdp"], mesh.shape["ep"]
    run = functools.partial(grouped_body, 4) if (nf, ne) == (8, 4) else body
    return jax.shard_map(
        run,
        mesh=mesh,
        in_specs=placed,
        out_specs=(
            P(("fsdp", "ep"), None),
            P(("fsdp", "ep"), None),
            P("ep", "fsdp", None),
            P("ep", "fsdp", None),
        ),
        check_vma=False,
    )
```

```python
import functools

import jax
import jax.numpy as jnp
from jax import lax
from jax.experimental import pallas as pl
from jax.experimental.pallas import tpu as pltpu
from jax.sharding import PartitionSpec as P

F32 = jnp.float32
BF16 = jnp.bfloat16
MESH = pl.DeviceIdType.MESH
LANES = 128
WIDTHS = (768, 768, 768, 768)
SPLITS = (512, 512, 512, 512)
SHARE = 80
TILE = 768
ROWS = 256


def gelu_parts(pre):
    root = 0.7978845608028654
    inner = root * (pre + 0.044715 * pre * pre * pre)
    tanh_val = jnp.tanh(inner)
    value = 0.5 * pre * (1.0 + tanh_val)
    slope = 0.5 * (1.0 + tanh_val) + 0.5 * pre * (1.0 - tanh_val * tanh_val) * root * (
        1.0 + 3.0 * 0.044715 * pre * pre
    )
    return (value, slope)


def dot(left, right, dims):
    return lax.dot_general(left, right, (dims, ((), ())), preferred_element_type=F32)


NN = ((1,), (0,))
NT = ((1,), (1,))
TN = ((0,), (0,))


def tail_rows(size):
    return max(16, size // 6 // 16 * 16)


def tiles(count, size):
    def run(fn):
        @pl.loop(0, count // size)
        def _(i):
            fn(pl.ds(pl.multiple_of(i * size, size), size))

    return run


def kernel(
    nz, ny, nx,
    tok_in, cot_in, gate_in, up_in, down_in,
    mixed_out, tg_out, ug_out, dg_out,
    up, down, tok, cot, gate, slope, hidden, dpre, upart, dpart,
    ry_u, ry_d, rz_u, rz_d, rt_u, rt_d, ft_u, ft_d, rc_m, rc_t, rx_m, rx_t,
    local_sem, wz_s, wz_r, wt_s, wt_r, wo_s, wo_r, wy_s, wy_r,
    tx_s, tx_r, tc_s, tc_r, g_s, g_r,
    ry_s, ry_r, rz_s, rz_r, rt_s, rt_r, ft_s, ft_r, rc_s, rc_r, rx_s, rx_r,
):
    ne = 2 * nx
    f = lax.axis_index("fsdp")
    e = lax.axis_index("ep")
    z, y = lax.div(f, ny), lax.rem(f, ny)
    x, c = lax.div(e, 2), lax.rem(e, 2)
    T = tok_in.shape[0]
    D = tok_in.shape[1]
    R = ne * T
    FF = up.shape[1]

    def zp(k):
        return lax.rem(z + k + nz, nz)

    def inside(zz):
        return (zz >= 0) & (zz < nz)

    def yp(j):
        return lax.rem(y + j + ny, ny)

    def xp(k):
        return lax.rem(x + k + nx, nx)

    def fdev(zz, yy):
        return {"fsdp": zz * ny + yy}

    def edev(xx, cc):
        return {"ep": xx * 2 + cc}

    def rows(ref, index, size):
        return ref.at[pl.ds(pl.multiple_of(index * size, size), size)]

    def remote(src, dst, ss, rs, dev):
        return pltpu.make_async_remote_copy(
            src_ref=src, dst_ref=dst, send_sem=ss, recv_sem=rs,
            device_id=dev, device_id_type=MESH,
        )

    sends = []
    guarded = []

    def send_when(there, copies):
        @pl.when(there)
        def _():
            for copy in copies:
                copy.start()

        guarded.append((there, copies))


    def send(src, dst, ss, rs, dev):
        copy = remote(src, dst, ss, rs, dev)
        copy.start()
        sends.append(copy)
        return copy

    barrier = pltpu.get_barrier_semaphore()
    peers = [fdev(zp(k), y) for k in range(1, nz)]
    peers += [fdev(z, yp(j)) for j in range(1, ny)]
    peers += [{"ep": lax.rem(e + i, ne)} for i in range(1, ne)]
    for dev in peers:
        pl.semaphore_signal(barrier, inc=1, device_id=dev, device_id_type=MESH)
    locals_ = []
    for i, (src, dst) in enumerate((
        (up_in.at[0], rows(up, f, up_in.shape[1])),
        (down_in.at[0], rows(down, f, down_in.shape[1])),
        (tok_in, rows(tok, e, T)),
        (cot_in, rows(cot, e, T)),
    )):
        copy = pltpu.make_async_copy(src, dst, local_sem.at[i])
        copy.start()
        locals_.append(copy)
    rows(gate, e, T)[...] = gate_in[e]
    pl.semaphore_wait(barrier, len(peers))

    weights = ((up_in, up), (down_in, down))

    def span(ref, index, size, begin, count):
        return ref.at[pl.ds(pl.multiple_of(index * size + begin, 16), count)]

    def chain(w, sgn, b, src=None):
        full = weights[w][1]
        size = weights[w][0].shape[1]
        block = rows(full, b * ny + y, size)
        way = (1 - sgn) // 2
        return remote(block if src is None else src, block, wz_s.at[w, way, b],
                      wz_r.at[w, way, b], fdev(zp(sgn), y))

    def chain_tail(w, sgn, b, j):
        full = weights[w][1]
        size = weights[w][0].shape[1]
        q = tail_rows(size)
        block = span(full, b * ny + yp(-j), size, size - q, q)
        way = (1 - sgn) // 2
        return remote(block, block, wt_s.at[w, way, b, j - 1], wt_r.at[w, way, b, j - 1],
                      fdev(zp(sgn), y))

    def across(w, b, yy, j):
        full = weights[w][1]
        size = weights[w][0].shape[1]
        block = span(full, b * ny + yy, size, 0, size - tail_rows(size))
        return remote(block, block, wy_s.at[w, b, j - 1], wy_r.at[w, b, j - 1], fdev(z, yp(j)))

    def own_across(w, yy, j, src=None):
        full = weights[w][1]
        size = weights[w][0].shape[1]
        block = rows(full, z * ny + yy, size)
        return remote(block if src is None else src, block, wo_s.at[w, j - 1], wo_r.at[w, j - 1],
                      fdev(z, yp(j)))

    def weight_start(w):
        src = weights[w][0].at[0]
        for sgn in (1, -1):
            send_when(inside(z + sgn), [chain(w, sgn, z, src)])
        for j in range(1, ny):
            copy = own_across(w, y, j, src)
            copy.start()
            sends.append(copy)

    def tail_start(w):
        for j in range(1, ny):
            own_across(w, yp(-j), j).wait_recv()
        for sgn in (1, -1):
            send_when(inside(z + sgn), [chain_tail(w, sgn, z, j) for j in range(1, ny)])

    def hop(w, s):
        for sgn in (1, -1):
            b = zp(-sgn * s)
            there = inside(z - sgn * s)

            @pl.when(there)
            def _():
                chain(w, sgn, b).wait_recv()

            send_when(there & inside(z + sgn), [chain(w, sgn, b)])
            send_when(there, [across(w, b, y, j) for j in range(1, ny)])

    def hop_tail(w, s):
        for sgn in (1, -1):
            b = zp(-sgn * s)
            there = inside(z - sgn * s)

            @pl.when(there)
            def _():
                for j in range(1, ny):
                    chain_tail(w, sgn, b, j).wait_recv()

            send_when(there & inside(z + sgn), [chain_tail(w, sgn, b, j) for j in range(1, ny)])

    def weight_wait(w):
        locals_[w].wait()
        for k in range(1, nz):
            for j in range(1, ny):
                across(w, zp(k), yp(-j), j).wait_recv()

    acts = ((tok_in, tok), (cot_in, cot))

    def act_start(w):
        src, full = acts[w]
        for k in range(1, nx):
            send(src, rows(full, e, T), tx_s.at[w, k - 1], tx_r.at[w, k - 1], edev(xp(k), c))
        send(src, rows(full, e, T), tc_s.at[w, 0], tc_r.at[w, 0], edev(x, 1 - c))

    def act_forward(w):
        src, full = acts[w]
        started = []
        for k in range(1, nx):
            block = rows(full, xp(-k) * 2 + c, T)
            remote(block, block, tx_s.at[w, k - 1], tx_r.at[w, k - 1],
                   edev(xp(k), c)).wait_recv()
            copy = remote(block, block, tc_s.at[w, k], tc_r.at[w, k], edev(x, 1 - c))
            copy.start()
            started.append(copy)
        return started

    def act_wait(w):
        src, full = acts[w]
        locals_[2 + w].wait()
        for k in range(nx):
            block = rows(full, xp(-k) * 2 + 1 - c, T)
            remote(block, block, tc_s.at[w, k], tc_r.at[w, k], edev(x, 1 - c)).wait_recv()

    weight_start(0)
    act_start(0)
    for i in range(1, ne):
        other = lax.rem(e + i, ne)
        send(gate_in.at[other], rows(gate, e, T), g_s.at[i - 1], g_r.at[i - 1], {"ep": other})
    act_start(1)
    hop(0, 1)
    tok_forwards = act_forward(0)
    tail_start(0)
    hop(0, 2)
    hop_tail(0, 1)
    hop(0, 3)
    weight_start(1)
    hop_tail(0, 2)
    hop_tail(0, 3)
    cot_forwards = act_forward(1)

    act_wait(1)
    for copy in cot_forwards:
        copy.wait_send()
    for i in range(1, ne):
        block = rows(gate, lax.rem(e - i + ne, ne), T)
        remote(block, block, g_s.at[i - 1], g_r.at[i - 1], {"ep": lax.rem(e + i, ne)}).wait_recv()

    @tiles(R, 16)
    def _(r):
        cot[r, :] = (cot[r, :].astype(F32) * gate[r, 0:1]).astype(BF16)

    act_wait(0)
    hop(1, 1)
    tail_start(1)
    weight_wait(0)

    @tiles(FF, 256)
    def _(n):
        slope[:, n] = dot(tok[...], up[:, n], NN)

    hop(1, 2)
    hop_tail(1, 1)

    @tiles(R, 16)
    def _(r):
        value, grad = gelu_parts(slope[r, :])
        hidden[r, :] = value.astype(BF16)
        slope[r, :] = grad

    @tiles(D, 512)
    def _(n):
        dpart[:, n] = dot(hidden[...], cot[:, n], TN).astype(BF16)

    parts = ((upart, ry_u, rz_u, rt_u, ft_u, ug_out), (dpart, ry_d, rz_d, rt_d, ft_d, dg_out))

    flip = lax.div(z, 2)
    near = z + flip * (3 - 2 * z)
    order = [d + flip * (3 - 2 * d) for d in (near * 0 + 3, 2 - 2 * near, 1 + near, near)]

    def give(w, d, yy, j):
        part, ry = parts[w][:2]
        size = parts[w][-1].shape[1]
        return remote(span(part, d * ny + yy, size, 0, size - tail_rows(size)),
                      ry.at[(j - 1) * nz + d], ry_s.at[w, d, j - 1], ry_r.at[w, d, j - 1],
                      fdev(z, yp(j)))

    def run_block(w, way, d, nxt):
        part, ry, rz = parts[w][:3]
        size = parts[w][-1].shape[1]
        return remote(rows(part, d * ny + y, size), rz.at[way, d], rz_s.at[w, d],
                      rz_r.at[w, way, d], fdev(nxt, y))

    def run_tail(w, way, d, nxt, j):
        part, rt = parts[w][0], parts[w][3]
        size = parts[w][-1].shape[1]
        q = tail_rows(size)
        return remote(span(part, d * ny + yp(j), size, size - q, q), rt.at[way, d, j - 1],
                      rt_s.at[w, d, j - 1], rt_r.at[w, way, d, j - 1], fdev(nxt, y))

    def last_tail(w, j):
        part, ft = parts[w][0], parts[w][4]
        size = parts[w][-1].shape[1]
        q = tail_rows(size)
        return remote(span(part, z * ny + yp(j), size, size - q, q), ft.at[j - 1],
                      ft_s.at[w, j - 1], ft_r.at[w, j - 1], fdev(z, yp(j)))

    def part_start(w):
        for d in order:
            for j in range(1, ny):
                copy = give(w, d, yp(j), j)
                copy.start()
                sends.append(copy)

    def add(part, start, count, others):
        @tiles(count, 16)
        def _(r):
            at = pl.ds(pl.multiple_of(start + r.start, 16), 16)
            total = part[at, :].astype(F32)
            for other in others:
                total += other[r, :].astype(F32)
            part[at, :] = total.astype(BF16)

    def pair(w, d):
        part, ry = parts[w][:2]
        size = parts[w][-1].shape[1]
        for j in range(1, ny):
            give(w, d, y, j).wait_recv()
        add(part, (d * ny + y) * size, size - tail_rows(size),
            [ry.at[(j - 1) * nz + d] for j in range(1, ny)])

    def run(w, p):
        part, ry, rz, rt = parts[w][:4]
        size = parts[w][-1].shape[1]
        q = tail_rows(size)
        d = order[p]
        way = jnp.where(d > z, 0, 1)
        sgn = 1 - 2 * way
        nxt = z + sgn
        pair(w, d)

        @pl.when(inside(z - sgn))
        def _():
            run_block(w, way, d, nxt).wait_recv()
            for j in range(1, ny):
                run_tail(w, way, d, nxt, j).wait_recv()
            add(part, (d * ny + y) * size, size, [rz.at[way, d]])
            for j in range(1, ny):
                add(part, (d * ny + yp(j)) * size + size - q, q, [rt.at[way, d, j - 1]])

        copies = [run_block(w, way, d, nxt)]
        copies += [run_tail(w, way, d, nxt, j) for j in range(1, ny)]
        for copy in copies:
            copy.start()
            sends.append(copy)

    def part_last(w):
        part, ry, rz, rt = parts[w][:4]
        size = parts[w][-1].shape[1]
        q = tail_rows(size)
        pair(w, z)
        for way in range(2):
            sgn = 1 - 2 * way

            @pl.when(inside(z - sgn))
            def _():
                for j in range(1, ny):
                    run_tail(w, way, z, zp(1), j).wait_recv()
                    add(part, (z * ny + yp(j)) * size + size - q, q, [rt.at[way, z, j - 1]])

        for j in range(1, ny):
            copy = last_tail(w, j)
            copy.start()
            sends.append(copy)
        for way in range(2):
            sgn = 1 - 2 * way

            @pl.when(inside(z - sgn))
            def _():
                run_block(w, way, z, zp(1)).wait_recv()
                add(part, (z * ny + y) * size, size, [rz.at[way, z]])

    def part_end(w):
        part, ry, rz, rt, ft, out = parts[w]
        size = out.shape[1]
        q = tail_rows(size)
        for j in range(1, ny):
            last_tail(w, j).wait_recv()
        add(part, (z * ny + y) * size + size - q, q, [ft.at[j - 1] for j in range(1, ny)])

        @tiles(size, 16)
        def _(r):
            out[0, r, :] = part[pl.ds(pl.multiple_of(f * size + r.start, 16), 16), :]

    backs = ((cot, rc_m, rx_m, mixed_out), (tok, rc_t, rx_t, tg_out))

    def back_start(w):
        full, rc, rx, out = backs[w]
        for k in range(nx):
            k = (k + 1) % nx
            send(rows(full, xp(k) * 2 + 1 - c, T), rc.at[k], rc_s.at[w, k], rc_r.at[w, k],
                 edev(x, 1 - c))

    def back_pair(w):
        full, rc, rx, out = backs[w]
        for k in range(nx):
            k = (k + 1) % nx
            index = xp(k) * 2 + c
            slot = rc.at[k]
            remote(slot, slot, rc_s.at[w, k], rc_r.at[w, k], edev(x, 1 - c)).wait_recv()

            @tiles(T, 16)
            def _(r):
                at = pl.ds(pl.multiple_of(index * T + r.start, 16), 16)
                full[at, :] = (full[at, :].astype(F32) + rc[k, r, :].astype(F32)).astype(BF16)

            if k:
                send(rows(full, index, T), rx.at[k - 1], rx_s.at[w, k - 1], rx_r.at[w, k - 1],
                     edev(xp(k), c))

    def back_end(w):
        full, rc, rx, out = backs[w]
        for k in range(1, nx):
            slot = rx.at[k - 1]
            remote(slot, slot, rx_s.at[w, k - 1], rx_r.at[w, k - 1], edev(xp(k), c)).wait_recv()

        @tiles(T, 16)
        def _(r):
            at = pl.ds(pl.multiple_of(e * T + r.start, 16), 16)
            total = full[at, :].astype(F32)
            for k in range(1, nx):
                total += rx[k - 1, r, :].astype(F32)
            out[r, :] = total.astype(BF16)

    hop(1, 3)
    hop_tail(1, 2)
    part_start(1)
    hop_tail(1, 3)
    weight_wait(1)

    @tiles(FF, 256)
    def _(n):
        dpre[:, n] = (dot(cot[...], down[n, :], NT) * slope[:, n]).astype(BF16)

    run(1, 0)

    @tiles(D, 384)
    def _(n):
        upart[n, :] = dot(tok[:, n], dpre[...], TN).astype(BF16)

    part_start(0)
    run(1, 1)

    @tiles(D, 512)
    def _(n):
        cot[:, n] = (dot(hidden[...], down[:, n], NN) * gate[:, 0:1]).astype(BF16)

    back_start(0)
    run(1, 2)
    for copy in tok_forwards:
        copy.wait_send()

    @tiles(D, 512)
    def _(n):
        tok[:, n] = dot(dpre[...], up[n, :], NT).astype(BF16)

    back_start(1)
    back_pair(0)
    back_pair(1)
    run(0, 0)
    part_last(1)
    back_end(0)
    run(0, 1)
    back_end(1)
    part_end(1)
    run(0, 2)
    part_last(0)
    part_end(0)
    for copy in sends:
        copy.wait_send()
    for there, copies in guarded:
        @pl.when(there)
        def _():
            for copy in copies:
                copy.wait_send()


def body(tokens, expert_ids, gates, up_weight, down_weight, cotangent):
    nf, ne = lax.axis_size("fsdp"), lax.axis_size("ep")
    nz = 4
    ny, nx = nf // nz, ne // 2
    T, D = tokens.shape
    R = ne * T
    su, FF = up_weight.shape[1:]
    sd = down_weight.shape[1]
    chosen = expert_ids[None] == jnp.arange(ne, dtype=jnp.int32)[:, None, None]
    dense = jnp.sum(jnp.where(chosen, gates[None], 0.0), axis=2)
    gcols = jnp.broadcast_to(dense[:, :, None], (ne, T, LANES))
    qu, qd = (tail_rows(size) for size in (su, sd))
    anyspace = pl.BlockSpec(memory_space=pl.ANY)
    vmem = pl.BlockSpec(memory_space=pltpu.VMEM)
    sem = pltpu.SemaphoreType.DMA
    V = pltpu.VMEM
    scratch = [
        V((D, FF), BF16), V((FF, D), BF16), V((R, D), BF16), V((R, D), BF16),
        V((R, LANES), F32), V((R, FF), F32), V((R, FF), BF16), V((R, FF), BF16),
        V((D, FF), BF16), V((FF, D), BF16),
        V(((ny - 1) * nz, su - qu, FF), BF16), V(((ny - 1) * nz, sd - qd, D), BF16),
        V((2, nz, su, FF), BF16), V((2, nz, sd, D), BF16),
        V((2, nz, ny - 1, qu, FF), BF16), V((2, nz, ny - 1, qd, D), BF16),
        V((ny - 1, qu, FF), BF16), V((ny - 1, qd, D), BF16),
        V((nx, T, D), BF16), V((nx, T, D), BF16),
        V((nx - 1, T, D), BF16), V((nx - 1, T, D), BF16),
        sem((4,)),
        sem((2, 2, nz)), sem((2, 2, nz)),
        sem((2, 2, nz, ny - 1)), sem((2, 2, nz, ny - 1)),
        sem((2, ny - 1)), sem((2, ny - 1)),
        sem((2, nz, ny - 1)), sem((2, nz, ny - 1)),
        sem((2, nx - 1)), sem((2, nx - 1)),
        sem((2, nx)), sem((2, nx)),
        sem((ne - 1,)), sem((ne - 1,)),
        sem((2, nz, ny - 1)), sem((2, nz, ny - 1)),
        sem((2, nz)), sem((2, 2, nz)),
        sem((2, nz, ny - 1)), sem((2, 2, nz, ny - 1)),
        sem((2, ny - 1)), sem((2, ny - 1)),
        sem((2, nx)), sem((2, nx)),
        sem((2, nx - 1)), sem((2, nx - 1)),
    ]
    return pl.pallas_call(
        functools.partial(kernel, nz, ny, nx),
        out_shape=(
            jax.ShapeDtypeStruct((T, D), BF16),
            jax.ShapeDtypeStruct((T, D), BF16),
            jax.ShapeDtypeStruct((1, su, FF), BF16),
            jax.ShapeDtypeStruct((1, sd, D), BF16),
        ),
        in_specs=[anyspace, anyspace, vmem, anyspace, anyspace],
        out_specs=(vmem, vmem, vmem, vmem),
        scratch_shapes=scratch,
        compiler_params=pltpu.CompilerParams(
            collective_id=0, has_side_effects=True, vmem_limit_bytes=64 * 1024 * 1024 - 262144
        ),
    )(tokens, cotangent, gcols, up_weight, down_weight)


def grouped(nz, *refs):
    (tok_in, cot_in, ids_in, gate_in, up_in, down_in,
     mixed_out, tg_out, ug_out, dg_out,
     up, down, tok, cot, upl, perm, uex, gd, gcol, slope, dh, hidden, dpre, upart, dpart,
     rz_u, rz_d, yrecv, rc_m, rc_t, r2_m, r2_t, r3_m, r3_t,
     local_sem, us, ur, ds_s, ds_r, yx_s, yx_r, tx_s, tx_r, ty_s, ty_r, fx_s, fx_r, fy_s, fy_r,
     tc_s, tc_r, g_s, g_r, ru_s, ru_r, rd_s, rd_r, yg_s, yg_r, b1_s, b1_r, b2_s, b2_r, b3_s, b3_r) = refs
    f = lax.axis_index("fsdp")
    e = lax.axis_index("ep")
    z, y = lax.div(f, 2), lax.rem(f, 2)
    x, c = lax.div(e, 2), lax.rem(e, 2)
    T, D = tok_in.shape
    SU, FF = up_in.shape[1:]
    SD = down_in.shape[1]
    G3 = nz * SD
    H = FF // 2
    R = 8 * T
    N = len(WIDTHS)
    begins = [D * sum(WIDTHS[:n]) // sum(WIDTHS) for n in range(N + 1)]

    def inside(zz):
        return (zz >= 0) & (zz < nz)

    def zp(k):
        return lax.rem(z + k + nz, nz)

    def zdev(zz):
        return {"fsdp": lax.rem(zz + nz, nz) * 2 + y}

    ydev = {"fsdp": z * 2 + 1 - y}
    xdev = {"ep": (1 - x) * 2 + c}
    cdev = {"ep": x * 2 + 1 - c}

    def blk(yy, xx, cc):
        return cc * 4 + yy * 2 + xx

    me = blk(y, x, c)

    def rows(index, size):
        return pl.ds(pl.multiple_of(index * size, size), size)

    def lanes(index, size):
        return pl.ds(pl.multiple_of(index * size, size), size)

    def cols(n):
        return pl.ds(begins[n], begins[n + 1] - begins[n])

    def cols_a(n):
        return pl.ds(begins[n], SPLITS[n])

    def cols_b(n):
        return pl.ds(begins[n] + SPLITS[n], begins[n + 1] - begins[n] - SPLITS[n])

    units = (pl.ds(0, 2 * G3), pl.ds(2 * G3, G3))
    sets = (pl.ds(0, 2), pl.ds(2, 1))

    def remote(src, dst, ss, rs, dev):
        return pltpu.make_async_remote_copy(
            src_ref=src, dst_ref=dst, send_sem=ss, recv_sem=rs,
            device_id=dev, device_id_type=MESH,
        )

    sends = []
    guarded = []

    def go(copy, keep=sends):
        copy.start()
        keep.append(copy)

    def go_when(there, copy):
        @pl.when(there)
        def _():
            copy.start()

        guarded.append((there, copy))

    barrier = pltpu.get_barrier_semaphore()
    offsets = [(i // 4, i // 2 % 2, i % 2) for i in range(1, 8)]

    def gdev(dy, dx, dc):
        yy = 1 - y if dy else y
        xx = 1 - x if dx else x
        cc = 1 - c if dc else c
        return yy, xx, cc

    peers = [{"fsdp": zp(k) * 2 + y, "ep": e} for k in range(1, nz)]
    for offset in offsets:
        yy, xx, cc = gdev(*offset)
        peers.append({"fsdp": z * 2 + yy, "ep": xx * 2 + cc})
    for dev in peers:
        pl.semaphore_signal(barrier, inc=1, device_id=dev, device_id_type=MESH)
    locals_ = []
    for i, (src, dst) in enumerate((
        (up_in.at[0], upl),
        (down_in, down.at[:, rows(z, SD)]),
        (tok_in, tok.at[rows(me, T)]),
        (cot_in, cot.at[rows(me, T)]),
    )):
        copy = pltpu.make_async_copy(src, dst, local_sem.at[i])
        copy.start()
        locals_.append(copy)

    expert = lax.broadcasted_iota(jnp.int32, (8, T), 0)
    gd[me] = jnp.where(ids_in[0:1, :] == expert, gate_in[0:1, :], 0.0) + jnp.where(
        ids_in[1:2, :] == expert, gate_in[1:2, :], 0.0)

    @pl.loop(0, 6 * nz)
    def _(i):
        half, third, zz = lax.div(i, 3 * nz), lax.rem(lax.div(i, nz), 3), lax.rem(i, nz)
        column = lax.broadcasted_iota(jnp.int32, (SD, FF), 1)
        first = SD * (3 * (2 * zz + half) + third)
        unit = lax.broadcasted_iota(jnp.int32, (SD, FF), 0) + first
        perm[rows(i, SD), :] = jnp.where(column == unit, 1.0, 0.0).astype(BF16)

    pl.semaphore_wait(barrier, len(peers))

    def permute_up():
        locals_[0].wait()
        up[rows(f, SU), :] = dot(upl[...], perm[rows(y, H), :], NT).astype(BF16)
        uex[...] = dot(upl[...], perm[rows(1 - y, H), :], NT).astype(BF16)
        locals_[1].wait()

    def sub(p):
        return y if p % 2 == 0 else 1 - y

    def chain_u(p, sgn, b):
        block = up.at[rows(2 * b + sub(p), SU), units[p // 2]]
        way = (1 - sgn) // 2
        return remote(block, block, us.at[p, way, b], ur.at[p, way, b], zdev(z + sgn))

    def chain_d(n, sgn, b):
        block = down.at[:, rows(b, SD), cols(n)]
        way = (1 - sgn) // 2
        return remote(block, block, ds_s.at[n, way, b], ds_r.at[n, way, b], zdev(z + sgn))

    def own_start(chain, n):
        for sgn in (1, -1):
            go_when(inside(z + sgn), chain(n, sgn, z))

    def hop(chain, n, s):
        for sgn in (1, -1):
            b = zp(-sgn * s)
            there = inside(z - sgn * s)

            @pl.when(there)
            def _():
                chain(n, sgn, b).wait_recv()

            go_when(there & inside(z + sgn), chain(n, sgn, b))

    y_exchange = [remote(uex.at[:, units[g]], up.at[rows(f, SU), units[g]], yx_s.at[g], yx_r.at[g], ydev)
                  for g in range(2)]

    acts = ((tok_in, tok), (cot_in, cot))
    forwards = ([[] for _ in range(N)], [[] for _ in range(N)])

    def act_own(w, n):
        src, full = acts[w]
        there = full.at[rows(me, T), cols(n)]
        go(remote(src.at[:, cols(n)], there, tx_s.at[w, n], tx_r.at[w, n], xdev))
        go(remote(src.at[:, cols(n)], there, ty_s.at[w, n], ty_r.at[w, n], ydev))
        go(remote(src.at[:, cols(n)], there, tc_s.at[w, n, 0], tc_r.at[w, n, 0], cdev))

    def high_rows(b):
        return pl.ds(pl.multiple_of(b * T, 16), SHARE)

    def low_rows(b):
        return pl.ds(pl.multiple_of(b * T + SHARE, 16), T - SHARE)

    def act_fwd(w, n):
        full = acts[w][1]
        keep = forwards[w][n]
        bx, by = blk(y, 1 - x, c), blk(1 - y, x, c)
        here = full.at[rows(bx, T), cols(n)]
        part = full.at[low_rows(bx), cols(n)]
        remote(here, here, tx_s.at[w, n], tx_r.at[w, n], xdev).wait_recv()
        go(remote(part, part, fy_s.at[w, n], fy_r.at[w, n], ydev), keep)
        go(remote(here, here, tc_s.at[w, n, 1], tc_r.at[w, n, 1], cdev), keep)
        here = full.at[rows(by, T), cols(n)]
        part = full.at[high_rows(by), cols(n)]
        remote(here, here, ty_s.at[w, n], ty_r.at[w, n], ydev).wait_recv()
        go(remote(part, part, fx_s.at[w, n], fx_r.at[w, n], xdev), keep)
        go(remote(here, here, tc_s.at[w, n, 2], tc_r.at[w, n, 2], cdev), keep)

    def act_diag(w, n):
        full = acts[w][1]
        bd = blk(1 - y, 1 - x, c)
        low = full.at[high_rows(bd), cols(n)]
        high = full.at[low_rows(bd), cols(n)]
        here = full.at[rows(bd, T), cols(n)]
        remote(low, low, fx_s.at[w, n], fx_r.at[w, n], xdev).wait_recv()
        remote(high, high, fy_s.at[w, n], fy_r.at[w, n], ydev).wait_recv()
        go(remote(here, here, tc_s.at[w, n, 3], tc_r.at[w, n, 3], cdev), forwards[w][n])

    def act_done(w, n):
        full = acts[w][1]
        others = ((y, x), (y, 1 - x), (1 - y, x), (1 - y, 1 - x))
        for k, (yy, xx) in enumerate(others):
            here = full.at[rows(blk(yy, xx, 1 - c), T), cols(n)]
            remote(here, here, tc_s.at[w, n, k], tc_r.at[w, n, k], cdev).wait_recv()

    def gates_start():
        for i, offset in enumerate(offsets):
            yy, xx, cc = gdev(*offset)
            go(remote(gd.at[me], gd.at[me], g_s.at[i], g_r.at[i],
                      {"fsdp": z * 2 + yy, "ep": xx * 2 + cc}))

    def gates_done():
        for i, offset in enumerate(offsets):
            yy, xx, cc = gdev(*offset)
            here = gd.at[blk(yy, xx, cc)]
            remote(here, here, g_s.at[i], g_r.at[i],
                   {"fsdp": z * 2 + yy, "ep": xx * 2 + cc}).wait_recv()

        @pl.loop(0, 8)
        def _(b):
            mine = lax.broadcasted_iota(jnp.int32, (8, T), 0) == e
            row = jnp.sum(jnp.where(mine, gd[b], 0.0), axis=0, keepdims=True)
            eye = lax.broadcasted_iota(jnp.int32, (T, T), 0) == lax.broadcasted_iota(
                jnp.int32, (T, T), 1)
            column = jnp.sum(jnp.where(eye, row, 0.0), axis=1, keepdims=True)
            gcol[rows(b, T), :] = jnp.broadcast_to(column, (T, LANES))

    flip = lax.div(z, 2)
    near = z + flip * (3 - 2 * z)
    order = [d + flip * (3 - 2 * d) for d in (near * 0 + 3, 2 - 2 * near, 1 + near, near)]
    is_end = near == 0

    def pre_step(g, s):
        plane = order[3 - s]
        u = units[g]
        if g == 0 and s == 0:
            locals_[2].wait()
            locals_[3].wait()

        @tiles(R, 256)
        def _(r):
            part = dot(tok[r, lanes(plane, 2 * SU)], up[rows(plane, 2 * SU), u], NN)
            if s == 0:
                slope[r, u] = part
            elif s < nz - 1:
                slope[r, u] += part
            else:
                value, grad = gelu_parts(slope[r, u] + part)
                hidden[r, u] = (value * gcol[r, 0:1]).astype(BF16)
                slope[r, u] = grad * gcol[r, 0:1]

    def tokens_sent():
        for copies in forwards[0]:
            for copy in copies:
                copy.wait_send()

    def chunk_tiles(n):
        size = TILE

        def run(fn):
            @pl.loop(0, (begins[n + 1] - begins[n]) // size)
            def _(i):
                fn(pl.ds(pl.multiple_of(begins[n] + i * size, size), size))

        return run

    def down_part(g, n):
        @chunk_tiles(n)
        def _(t):
            part = dot(hidden[:, units[g]], cot[:, t], TN).astype(BF16)
            dpart[sets[g], :, t] = part.reshape(2 - g, G3, TILE)

    def back_hidden(n):
        @tiles(R, 256)
        def _(r):
            part = dot(cot[r, cols(n)], down[:, :, cols(n)].reshape(H, begins[n + 1] - begins[n]), NT)
            if n == 0:
                dh[r, :] = part
            elif n < N - 1:
                dh[r, :] += part
            else:
                dpre[r, :] = ((dh[r, :] + part) * slope[r, :]).astype(BF16)

    def mixed_part(n):
        for copy in forwards[1][n]:
            copy.wait_send()

        @chunk_tiles(n)
        def _(t):
            @tiles(R, ROWS)
            def _(r):
                cot[r, t] = dot(hidden[r, :], down[:, :, t].reshape(H, TILE), NN).astype(BF16)

    def token_part(n):
        @chunk_tiles(n)
        def _(t):
            @tiles(R, ROWS)
            def _(r):
                tok[r, t] = dot(dpre[r, :], up[t, :], NT).astype(BF16)

    def up_part(q, pos):
        at = rows(2 * order[pos] + (1 - sub(q)), SU)
        upart[at, :] = dot(tok[:, at], dpre[...], TN).astype(BF16)

    def send_down(m, d, way, nxt):
        g, n = m // N, m % N
        return remote(dpart.at[sets[g], rows(d, SD), cols(n)], rz_d.at[way, d, sets[g], :, cols(n)],
                      rd_s.at[m, d], rd_r.at[m, way, d], zdev(nxt))

    def send_up(q, d, way, nxt):
        return remote(upart.at[rows(2 * d + (1 - sub(q)), SU)], rz_u.at[q, way, d],
                      ru_s.at[q, d], ru_r.at[q, way, d], zdev(nxt))

    def add_down(m, d, way):
        g, n = m // N, m % N

        @tiles(SD, 16)
        def _(r):
            at = pl.ds(pl.multiple_of(d * SD + r.start, 16), 16)
            dpart[sets[g], at, cols(n)] = (dpart[sets[g], at, cols(n)].astype(F32)
                                           + rz_d[way, d, sets[g], r, cols(n)].astype(F32)).astype(BF16)

    def add_up(q, d, way):
        @tiles(SU, 32)
        def _(r):
            at = pl.ds(pl.multiple_of((2 * d + (1 - sub(q))) * SU + r.start, 32), 32)
            upart[at, :] = (upart[at, :].astype(F32)
                            + rz_u[q, way, d, r, :].astype(F32)).astype(BF16)

    downs, ups = (send_down, add_down), (send_up, add_up)

    def course(pos):
        d = order[pos]
        way = jnp.where(d > z, 0, 1)
        return d, way, z + 1 - 2 * way

    def begin(kind, n, pos):
        d, way, nxt = course(pos)
        go_when(is_end, kind[0](n, d, way, nxt))

    def middle(kind, n, pos):
        d, way, nxt = course(pos)
        copy = kind[0](n, d, way, nxt)

        @pl.when(jnp.logical_not(is_end))
        def _():
            copy.wait_recv()
            kind[1](n, d, way)
            copy.start()

        guarded.append((jnp.logical_not(is_end), copy))

    def last(kind, n):
        for way in range(2):
            @pl.when(inside(z - 1 + 2 * way))
            def _():
                kind[0](n, z, way, zp(1)).wait_recv()
                kind[1](n, z, way)

    def down_end(m):
        g, n = m // N, m % N
        last(downs, m)
        dg_out[sets[g], :, cols(n)] = dpart[sets[g], rows(z, SD), cols(n)]

    other_up = upart.at[rows(2 * z + 1 - y, SU)]
    y_return = remote(other_up, yrecv, yg_s.at[0], yg_r.at[0], ydev)

    def up_end():
        last(ups, 1)
        y_return.wait_recv()
        ug_out[0] = (dot(upart[rows(f, SU), :], perm[rows(y, H), :], NN)
                     + dot(yrecv[...], perm[rows(1 - y, H), :], NN)).astype(BF16)

    backs = ((cot, rc_m, r2_m, r3_m, mixed_out), (tok, rc_t, r2_t, r3_t, tg_out))
    G = 4 * T

    def back1(w, n):
        full, rc = backs[w][:2]
        go(remote(full.at[rows(1 - c, G), cols(n)], rc.at[:, cols(n)],
                  b1_s.at[w, n], b1_r.at[w, n], cdev))

    def back2(w, n):
        full, rc, r2 = backs[w][:3]
        here = rc.at[:, cols(n)]
        remote(here, here, b1_s.at[w, n], b1_r.at[w, n], cdev).wait_recv()

        @tiles(G, 16)
        def _(r):
            at = pl.ds(pl.multiple_of(c * G + r.start, 16), 16)
            full[at, cols(n)] = (full[at, cols(n)].astype(F32)
                                 + rc[r, cols(n)].astype(F32)).astype(BF16)

        for yy in range(2):
            go(remote(full.at[rows(blk(yy, 1 - x, c), T), cols_a(n)],
                      r2.at[pl.ds(yy * T, T), cols_a(n)],
                      b2_s.at[w, n, yy], b2_r.at[w, n, yy], xdev))
        go(remote(full.at[rows(c * 2 + 1 - y, 2 * T), cols_b(n)], r2.at[:, cols_b(n)],
                  b2_s.at[w, n, 2], b2_r.at[w, n, 2], ydev))

    def back3(w, n):
        full, rc, r2, r3 = backs[w][:4]
        for yy in range(2):
            here = r2.at[pl.ds(yy * T, T), cols_a(n)]
            remote(here, here, b2_s.at[w, n, yy], b2_r.at[w, n, yy], xdev).wait_recv()
        here = r2.at[:, cols_b(n)]
        remote(here, here, b2_s.at[w, n, 2], b2_r.at[w, n, 2], ydev).wait_recv()
        ba, bb = blk(1 - y, x, c), blk(y, 1 - x, c)

        @tiles(T, 16)
        def _(r):
            at = pl.ds(pl.multiple_of(ba * T + r.start, 16), 16)
            there = pl.ds(pl.multiple_of((1 - y) * T + r.start, 16), 16)
            full[at, cols_a(n)] = (full[at, cols_a(n)].astype(F32)
                                   + r2[there, cols_a(n)].astype(F32)).astype(BF16)
            at = pl.ds(pl.multiple_of(bb * T + r.start, 16), 16)
            there = pl.ds(pl.multiple_of((1 - x) * T + r.start, 16), 16)
            full[at, cols_b(n)] = (full[at, cols_b(n)].astype(F32)
                                   + r2[there, cols_b(n)].astype(F32)).astype(BF16)

        go(remote(full.at[rows(ba, T), cols_a(n)], r3.at[:, cols_a(n)],
                  b3_s.at[w, n, 0], b3_r.at[w, n, 0], ydev))
        go(remote(full.at[rows(bb, T), cols_b(n)], r3.at[:, cols_b(n)],
                  b3_s.at[w, n, 1], b3_r.at[w, n, 1], xdev))

    def back4(w, n):
        full, rc, r2, r3, out = backs[w]
        for k, (span, dev) in enumerate(((cols_a(n), ydev), (cols_b(n), xdev))):
            here = r3.at[:, span]
            remote(here, here, b3_s.at[w, n, k], b3_r.at[w, n, k], dev).wait_recv()

        @tiles(T, 16)
        def _(r):
            at = pl.ds(pl.multiple_of(me * T + r.start, 16), 16)
            for span, lane in ((cols_a(n), y), (cols_b(n), x)):
                there = pl.ds(pl.multiple_of(lane * T + r.start, 16), 16)
                out[r, span] = (full[at, span].astype(F32) + r2[there, span].astype(F32)
                                + r3[r, span].astype(F32)).astype(BF16)

    permute_up()
    own_start(chain_d, 0)
    go(y_exchange[0])
    own_start(chain_u, 0)
    act_own(0, 0)
    act_own(0, 1)
    act_own(0, 2)
    go(y_exchange[1])
    y_exchange[0].wait_recv()
    own_start(chain_u, 1)
    gates_start()
    hop(chain_u, 0, 1)
    act_own(1, 2)
    own_start(chain_u, 2)
    act_own(0, 3)
    hop(chain_u, 1, 1)
    y_exchange[1].wait_recv()
    act_fwd(0, 1)
    own_start(chain_u, 3)
    hop(chain_u, 0, 2)
    act_fwd(0, 2)
    hop(chain_u, 2, 1)
    act_fwd(0, 0)
    hop(chain_u, 3, 1)
    act_fwd(0, 3)
    hop(chain_u, 1, 2)
    gates_done()
    act_diag(0, 1)
    act_fwd(1, 2)
    own_start(chain_d, 2)
    hop(chain_d, 0, 1)
    act_diag(0, 2)
    act_own(1, 0)
    act_done(0, 2)
    hop(chain_u, 0, 3)
    act_diag(0, 0)
    act_diag(0, 3)
    act_done(0, 3)
    hop(chain_u, 2, 2)
    act_done(0, 1)
    act_own(1, 1)
    act_done(0, 0)
    hop(chain_u, 3, 2)
    pre_step(0, 0)
    act_diag(1, 2)
    own_start(chain_d, 1)
    hop(chain_u, 1, 3)
    pre_step(0, 1)
    own_start(chain_d, 3)
    pre_step(0, 2)
    act_done(1, 2)
    act_fwd(1, 0)
    pre_step(0, 3)
    down_part(0, 2)
    begin(downs, 0 * N + 2, 1)
    act_fwd(1, 1)
    act_own(1, 3)
    begin(downs, 0 * N + 2, 0)
    begin(downs, 0 * N + 2, 2)
    act_diag(1, 0)
    hop(chain_d, 0, 2)
    pre_step(1, 0)
    act_done(1, 0)
    pre_step(1, 1)
    hop(chain_u, 3, 3)
    down_part(0, 0)
    hop(chain_u, 2, 3)
    begin(downs, 0 * N + 0, 0)
    pre_step(1, 2)
    act_diag(1, 1)
    pre_step(1, 3)
    act_done(1, 1)
    begin(downs, 0 * N + 0, 2)
    down_part(1, 0)
    hop(chain_d, 1, 1)
    down_part(1, 1)
    down_part(0, 1)
    begin(downs, 0 * N + 1, 2)
    act_fwd(1, 3)
    begin(downs, 0 * N + 0, 1)
    begin(downs, 0 * N + 1, 0)
    begin(downs, 1 * N + 0, 1)
    hop(chain_d, 0, 3)
    back_hidden(0)
    mixed_part(0)
    back1(0, 0)
    hop(chain_d, 1, 2)
    begin(downs, 1 * N + 0, 2)
    begin(downs, 1 * N + 1, 1)
    begin(downs, 0 * N + 1, 1)
    down_part(1, 2)
    begin(downs, 1 * N + 0, 0)
    hop(chain_d, 2, 1)
    middle(downs, 0 * N + 0, 0)
    act_diag(1, 3)
    back2(0, 0)
    hop(chain_d, 1, 3)
    back_hidden(1)
    mixed_part(1)
    back1(0, 1)
    begin(downs, 1 * N + 2, 0)
    act_done(1, 3)
    down_part(1, 3)
    begin(downs, 1 * N + 3, 2)
    hop(chain_d, 2, 2)
    hop(chain_d, 3, 1)
    down_part(0, 3)
    begin(downs, 1 * N + 3, 1)
    middle(downs, 0 * N + 2, 0)
    middle(downs, 1 * N + 0, 2)
    begin(downs, 0 * N + 3, 0)
    begin(downs, 1 * N + 1, 2)
    back2(0, 1)
    begin(downs, 1 * N + 3, 0)
    middle(downs, 1 * N + 1, 2)
    hop(chain_d, 2, 3)
    begin(downs, 1 * N + 2, 2)
    back_hidden(2)
    middle(downs, 1 * N + 0, 0)
    begin(downs, 0 * N + 3, 1)
    mixed_part(2)
    back1(0, 2)
    middle(downs, 0 * N + 1, 2)
    hop(chain_d, 3, 2)
    back3(0, 0)
    middle(downs, 0 * N + 1, 0)
    middle(downs, 0 * N + 0, 2)
    begin(downs, 1 * N + 1, 0)
    back2(0, 2)
    back3(0, 1)
    hop(chain_d, 3, 3)
    back_hidden(3)
    up_part(0, 0)
    begin(ups, 0, 0)
    mixed_part(3)
    back1(0, 3)
    up_part(0, 1)
    middle(downs, 0 * N + 3, 0)
    up_part(1, 1)
    up_part(1, 0)
    up_part(0, 2)
    up_part(1, 2)
    middle(downs, 1 * N + 2, 0)
    back2(0, 3)
    middle(downs, 1 * N + 1, 0)
    up_part(1, 3)
    up_part(0, 3)
    middle(downs, 0 * N + 1, 1)
    tokens_sent()
    begin(ups, 1, 0)
    middle(downs, 1 * N + 3, 0)
    token_part(1)
    back1(1, 1)
    back3(0, 2)
    token_part(0)
    begin(ups, 0, 1)
    middle(downs, 0 * N + 0, 1)
    middle(ups, 0, 0)
    begin(ups, 0, 2)
    back2(1, 1)
    token_part(2)
    down_end(0 * N + 0)
    back1(1, 0)
    middle(downs, 0 * N + 3, 1)
    middle(downs, 1 * N + 3, 1)
    begin(ups, 1, 1)
    middle(downs, 0 * N + 2, 1)
    back3(0, 3)
    back1(1, 2)
    middle(ups, 1, 0)
    back2(1, 0)
    token_part(3)
    middle(downs, 1 * N + 2, 1)
    back4(0, 0)
    back1(1, 3)
    back2(1, 2)
    middle(ups, 0, 1)
    back2(1, 3)
    middle(downs, 1 * N + 0, 1)
    middle(ups, 0, 2)
    middle(downs, 0 * N + 2, 2)
    back3(1, 1)
    middle(downs, 0 * N + 3, 2)
    middle(downs, 1 * N + 3, 2)
    begin(downs, 1 * N + 2, 1)
    back3(1, 0)
    middle(downs, 1 * N + 1, 1)
    last(ups, 0)
    go(y_return)
    down_end(1 * N + 0)
    middle(ups, 1, 1)
    middle(ups, 1, 2)
    middle(downs, 1 * N + 2, 2)
    back4(0, 1)
    back3(1, 2)
    back4(0, 2)
    begin(ups, 1, 2)
    back3(1, 3)
    begin(downs, 0 * N + 3, 2)
    down_end(1 * N + 1)
    back4(0, 3)
    down_end(1 * N + 3)
    down_end(0 * N + 2)
    up_end()
    back4(1, 0)
    down_end(0 * N + 1)
    down_end(1 * N + 2)
    back4(1, 2)
    back4(1, 1)
    down_end(0 * N + 3)
    back4(1, 3)
    for copy in sends:
        copy.wait_send()
    for there, copy in guarded:
        @pl.when(there)
        def _():
            copy.wait_send()


def settle(*refs):
    sources, results, held, arrived, done = refs[:4], refs[4:8], refs[8:12], refs[12], refs[13]
    ins = [pltpu.make_async_copy(a, b, arrived.at[i]) for i, (a, b) in enumerate(zip(sources, held))]
    outs = [pltpu.make_async_copy(a, b, done.at[i]) for i, (a, b) in enumerate(zip(held, results))]
    for copy in ins:
        copy.start()
    for arrival, copy in zip(ins, outs):
        arrival.wait()
        copy.start()
    for copy in outs:
        copy.wait()


def grouped_body(nz, tokens, expert_ids, gates, up_weight, down_weight, cotangent):
    T, D = tokens.shape
    R = 8 * T
    SU, FF = up_weight.shape[1:]
    SD = down_weight.shape[1] // 3
    H = FF // 2
    N = len(WIDTHS)
    anyspace = pl.BlockSpec(memory_space=pl.ANY)
    vmem = pl.BlockSpec(memory_space=pltpu.VMEM)
    sem = pltpu.SemaphoreType.DMA
    V = pltpu.VMEM

    def pair(*shape):
        return [sem(shape), sem(shape)]

    scratch = [
        V((D, H), BF16), V((3, nz * SD, D), BF16), V((R, D), BF16), V((R, D), BF16),
        V((SU, FF), BF16), V((FF, FF), BF16), V((SU, H), BF16),
        V((8, 8, T), F32), V((R, LANES), F32), V((R, H), F32), V((R, H), F32),
        V((R, H), BF16), V((R, H), BF16), V((D, H), BF16), V((3, nz * SD, D), BF16),
        V((2, 2, nz, SU, H), BF16), V((2, nz, 3, SD, D), BF16), V((SU, H), BF16),
        V((4 * T, D), BF16), V((4 * T, D), BF16), V((2 * T, D), BF16), V((2 * T, D), BF16),
        V((T, D), BF16), V((T, D), BF16),
        sem((4,)),
        *pair(4, 2, nz), *pair(N, 2, nz), *pair(2),
        *pair(2, N), *pair(2, N), *pair(2, N), *pair(2, N), *pair(2, N, 4), *pair(7),
        sem((2, nz)), sem((2, 2, nz)), sem((2 * N, nz)), sem((2 * N, 2, nz)), *pair(1),
        *pair(2, N), *pair(2, N, 3), *pair(2, N, 2),
    ]
    outs = pl.pallas_call(
        functools.partial(grouped, nz),
        out_shape=(
            jax.ShapeDtypeStruct((T, D), BF16),
            jax.ShapeDtypeStruct((T, D), BF16),
            jax.ShapeDtypeStruct((1, SU, FF), BF16),
            jax.ShapeDtypeStruct((3, SD, D), BF16),
        ),
        in_specs=[anyspace, anyspace, vmem, vmem, anyspace, anyspace],
        out_specs=(vmem, vmem, vmem, vmem),
        scratch_shapes=scratch,
        compiler_params=pltpu.CompilerParams(
            collective_id=0, has_side_effects=True, vmem_limit_bytes=64 * 1024 * 1024 - 262144
        ),
    )(tokens, cotangent, expert_ids.T, gates.T, up_weight, down_weight.reshape(3, SD, D))
    outs = pl.pallas_call(
        settle,
        out_shape=tuple(jax.ShapeDtypeStruct(out.shape, out.dtype) for out in outs),
        in_specs=[anyspace] * 4,
        out_specs=(anyspace,) * 4,
        scratch_shapes=[V(out.shape, BF16) for out in outs] + [sem((4,)), sem((4,))],
    )(*outs)
    return *outs[:3], outs[3].reshape(down_weight.shape)


def solution(mesh):
    placed = (
        P(("fsdp", "ep"), None),
        P(("fsdp", "ep"), None),
        P(("fsdp", "ep"), None),
        P("ep", "fsdp", None),
        P("ep", "fsdp", None),
        P(("fsdp", "ep"), None),
    )
    nf, ne = mesh.shape["fsdp"], mesh.shape["ep"]
    run = functools.partial(grouped_body, 4) if (nf, ne) == (8, 4) else body
    return jax.shard_map(
        run,
        mesh=mesh,
        in_specs=placed,
        out_specs=(
            P(("fsdp", "ep"), None),
            P(("fsdp", "ep"), None),
            P("ep", "fsdp", None),
            P("ep", "fsdp", None),
        ),
        check_vma=False,
    )
```

```python
import functools

import jax
import jax.numpy as jnp
from jax import lax
from jax.experimental import pallas as pl
from jax.experimental.pallas import tpu as pltpu
from jax.sharding import PartitionSpec as P

F32 = jnp.float32
BF16 = jnp.bfloat16
MESH = pl.DeviceIdType.MESH
LANES = 128
WIDTHS = (768, 768, 768, 768)
SPLITS = (512, 512, 512, 512)
SHARE = 80
TILE = 768
ROWS = 256


def gelu_parts(pre):
    root = 0.7978845608028654
    inner = root * (pre + 0.044715 * pre * pre * pre)
    tanh_val = jnp.tanh(inner)
    value = 0.5 * pre * (1.0 + tanh_val)
    slope = 0.5 * (1.0 + tanh_val) + 0.5 * pre * (1.0 - tanh_val * tanh_val) * root * (
        1.0 + 3.0 * 0.044715 * pre * pre
    )
    return (value, slope)


def dot(left, right, dims):
    return lax.dot_general(left, right, (dims, ((), ())), preferred_element_type=F32)


NN = ((1,), (0,))
NT = ((1,), (1,))
TN = ((0,), (0,))


def tail_rows(size):
    return max(16, size // 6 // 16 * 16)


def tiles(count, size):
    def run(fn):
        @pl.loop(0, count // size)
        def _(i):
            fn(pl.ds(pl.multiple_of(i * size, size), size))

    return run


def kernel(
    nz, ny, nx,
    tok_in, cot_in, gate_in, up_in, down_in,
    mixed_out, tg_out, ug_out, dg_out,
    up, down, tok, cot, gate, slope, hidden, dpre, upart, dpart,
    ry_u, ry_d, rz_u, rz_d, rt_u, rt_d, ft_u, ft_d, rc_m, rc_t, rx_m, rx_t,
    local_sem, wz_s, wz_r, wt_s, wt_r, wo_s, wo_r, wy_s, wy_r,
    tx_s, tx_r, tc_s, tc_r, g_s, g_r,
    ry_s, ry_r, rz_s, rz_r, rt_s, rt_r, ft_s, ft_r, rc_s, rc_r, rx_s, rx_r,
):
    ne = 2 * nx
    f = lax.axis_index("fsdp")
    e = lax.axis_index("ep")
    z, y = lax.div(f, ny), lax.rem(f, ny)
    x, c = lax.div(e, 2), lax.rem(e, 2)
    T = tok_in.shape[0]
    D = tok_in.shape[1]
    R = ne * T
    FF = up.shape[1]

    def zp(k):
        return lax.rem(z + k + nz, nz)

    def inside(zz):
        return (zz >= 0) & (zz < nz)

    def yp(j):
        return lax.rem(y + j + ny, ny)

    def xp(k):
        return lax.rem(x + k + nx, nx)

    def fdev(zz, yy):
        return {"fsdp": zz * ny + yy}

    def edev(xx, cc):
        return {"ep": xx * 2 + cc}

    def rows(ref, index, size):
        return ref.at[pl.ds(pl.multiple_of(index * size, size), size)]

    def remote(src, dst, ss, rs, dev):
        return pltpu.make_async_remote_copy(
            src_ref=src, dst_ref=dst, send_sem=ss, recv_sem=rs,
            device_id=dev, device_id_type=MESH,
        )

    sends = []
    guarded = []

    def send_when(there, copies):
        @pl.when(there)
        def _():
            for copy in copies:
                copy.start()

        guarded.append((there, copies))


    def send(src, dst, ss, rs, dev):
        copy = remote(src, dst, ss, rs, dev)
        copy.start()
        sends.append(copy)
        return copy

    barrier = pltpu.get_barrier_semaphore()
    peers = [fdev(zp(k), y) for k in range(1, nz)]
    peers += [fdev(z, yp(j)) for j in range(1, ny)]
    peers += [{"ep": lax.rem(e + i, ne)} for i in range(1, ne)]
    for dev in peers:
        pl.semaphore_signal(barrier, inc=1, device_id=dev, device_id_type=MESH)
    locals_ = []
    for i, (src, dst) in enumerate((
        (up_in.at[0], rows(up, f, up_in.shape[1])),
        (down_in.at[0], rows(down, f, down_in.shape[1])),
        (tok_in, rows(tok, e, T)),
        (cot_in, rows(cot, e, T)),
    )):
        copy = pltpu.make_async_copy(src, dst, local_sem.at[i])
        copy.start()
        locals_.append(copy)
    rows(gate, e, T)[...] = gate_in[e]
    pl.semaphore_wait(barrier, len(peers))

    weights = ((up_in, up), (down_in, down))

    def span(ref, index, size, begin, count):
        return ref.at[pl.ds(pl.multiple_of(index * size + begin, 16), count)]

    def chain(w, sgn, b, src=None):
        full = weights[w][1]
        size = weights[w][0].shape[1]
        block = rows(full, b * ny + y, size)
        way = (1 - sgn) // 2
        return remote(block if src is None else src, block, wz_s.at[w, way, b],
                      wz_r.at[w, way, b], fdev(zp(sgn), y))

    def chain_tail(w, sgn, b, j):
        full = weights[w][1]
        size = weights[w][0].shape[1]
        q = tail_rows(size)
        block = span(full, b * ny + yp(-j), size, size - q, q)
        way = (1 - sgn) // 2
        return remote(block, block, wt_s.at[w, way, b, j - 1], wt_r.at[w, way, b, j - 1],
                      fdev(zp(sgn), y))

    def across(w, b, yy, j):
        full = weights[w][1]
        size = weights[w][0].shape[1]
        block = span(full, b * ny + yy, size, 0, size - tail_rows(size))
        return remote(block, block, wy_s.at[w, b, j - 1], wy_r.at[w, b, j - 1], fdev(z, yp(j)))

    def own_across(w, yy, j, src=None):
        full = weights[w][1]
        size = weights[w][0].shape[1]
        block = rows(full, z * ny + yy, size)
        return remote(block if src is None else src, block, wo_s.at[w, j - 1], wo_r.at[w, j - 1],
                      fdev(z, yp(j)))

    def weight_start(w):
        src = weights[w][0].at[0]
        for sgn in (1, -1):
            send_when(inside(z + sgn), [chain(w, sgn, z, src)])
        for j in range(1, ny):
            copy = own_across(w, y, j, src)
            copy.start()
            sends.append(copy)

    def tail_start(w):
        for j in range(1, ny):
            own_across(w, yp(-j), j).wait_recv()
        for sgn in (1, -1):
            send_when(inside(z + sgn), [chain_tail(w, sgn, z, j) for j in range(1, ny)])

    def hop(w, s):
        for sgn in (1, -1):
            b = zp(-sgn * s)
            there = inside(z - sgn * s)

            @pl.when(there)
            def _():
                chain(w, sgn, b).wait_recv()

            send_when(there & inside(z + sgn), [chain(w, sgn, b)])
            send_when(there, [across(w, b, y, j) for j in range(1, ny)])

    def hop_tail(w, s):
        for sgn in (1, -1):
            b = zp(-sgn * s)
            there = inside(z - sgn * s)

            @pl.when(there)
            def _():
                for j in range(1, ny):
                    chain_tail(w, sgn, b, j).wait_recv()

            send_when(there & inside(z + sgn), [chain_tail(w, sgn, b, j) for j in range(1, ny)])

    def weight_wait(w):
        locals_[w].wait()
        for k in range(1, nz):
            for j in range(1, ny):
                across(w, zp(k), yp(-j), j).wait_recv()

    acts = ((tok_in, tok), (cot_in, cot))

    def act_start(w):
        src, full = acts[w]
        for k in range(1, nx):
            send(src, rows(full, e, T), tx_s.at[w, k - 1], tx_r.at[w, k - 1], edev(xp(k), c))
        send(src, rows(full, e, T), tc_s.at[w, 0], tc_r.at[w, 0], edev(x, 1 - c))

    def act_forward(w):
        src, full = acts[w]
        started = []
        for k in range(1, nx):
            block = rows(full, xp(-k) * 2 + c, T)
            remote(block, block, tx_s.at[w, k - 1], tx_r.at[w, k - 1],
                   edev(xp(k), c)).wait_recv()
            copy = remote(block, block, tc_s.at[w, k], tc_r.at[w, k], edev(x, 1 - c))
            copy.start()
            started.append(copy)
        return started

    def act_wait(w):
        src, full = acts[w]
        locals_[2 + w].wait()
        for k in range(nx):
            block = rows(full, xp(-k) * 2 + 1 - c, T)
            remote(block, block, tc_s.at[w, k], tc_r.at[w, k], edev(x, 1 - c)).wait_recv()

    weight_start(0)
    act_start(0)
    for i in range(1, ne):
        other = lax.rem(e + i, ne)
        send(gate_in.at[other], rows(gate, e, T), g_s.at[i - 1], g_r.at[i - 1], {"ep": other})
    act_start(1)
    hop(0, 1)
    tok_forwards = act_forward(0)
    tail_start(0)
    hop(0, 2)
    hop_tail(0, 1)
    hop(0, 3)
    weight_start(1)
    hop_tail(0, 2)
    hop_tail(0, 3)
    cot_forwards = act_forward(1)

    act_wait(1)
    for copy in cot_forwards:
        copy.wait_send()
    for i in range(1, ne):
        block = rows(gate, lax.rem(e - i + ne, ne), T)
        remote(block, block, g_s.at[i - 1], g_r.at[i - 1], {"ep": lax.rem(e + i, ne)}).wait_recv()

    @tiles(R, 16)
    def _(r):
        cot[r, :] = (cot[r, :].astype(F32) * gate[r, 0:1]).astype(BF16)

    act_wait(0)
    hop(1, 1)
    tail_start(1)
    weight_wait(0)

    @tiles(FF, 256)
    def _(n):
        slope[:, n] = dot(tok[...], up[:, n], NN)

    hop(1, 2)
    hop_tail(1, 1)

    @tiles(R, 16)
    def _(r):
        value, grad = gelu_parts(slope[r, :])
        hidden[r, :] = value.astype(BF16)
        slope[r, :] = grad

    @tiles(D, 512)
    def _(n):
        dpart[:, n] = dot(hidden[...], cot[:, n], TN).astype(BF16)

    parts = ((upart, ry_u, rz_u, rt_u, ft_u, ug_out), (dpart, ry_d, rz_d, rt_d, ft_d, dg_out))

    flip = lax.div(z, 2)
    near = z + flip * (3 - 2 * z)
    order = [d + flip * (3 - 2 * d) for d in (near * 0 + 3, 2 - 2 * near, 1 + near, near)]

    def give(w, d, yy, j):
        part, ry = parts[w][:2]
        size = parts[w][-1].shape[1]
        return remote(span(part, d * ny + yy, size, 0, size - tail_rows(size)),
                      ry.at[(j - 1) * nz + d], ry_s.at[w, d, j - 1], ry_r.at[w, d, j - 1],
                      fdev(z, yp(j)))

    def run_block(w, way, d, nxt):
        part, ry, rz = parts[w][:3]
        size = parts[w][-1].shape[1]
        return remote(rows(part, d * ny + y, size), rz.at[way, d], rz_s.at[w, d],
                      rz_r.at[w, way, d], fdev(nxt, y))

    def run_tail(w, way, d, nxt, j):
        part, rt = parts[w][0], parts[w][3]
        size = parts[w][-1].shape[1]
        q = tail_rows(size)
        return remote(span(part, d * ny + yp(j), size, size - q, q), rt.at[way, d, j - 1],
                      rt_s.at[w, d, j - 1], rt_r.at[w, way, d, j - 1], fdev(nxt, y))

    def last_tail(w, j):
        part, ft = parts[w][0], parts[w][4]
        size = parts[w][-1].shape[1]
        q = tail_rows(size)
        return remote(span(part, z * ny + yp(j), size, size - q, q), ft.at[j - 1],
                      ft_s.at[w, j - 1], ft_r.at[w, j - 1], fdev(z, yp(j)))

    def part_start(w):
        for d in order:
            for j in range(1, ny):
                copy = give(w, d, yp(j), j)
                copy.start()
                sends.append(copy)

    def add(part, start, count, others):
        @tiles(count, 16)
        def _(r):
            at = pl.ds(pl.multiple_of(start + r.start, 16), 16)
            total = part[at, :].astype(F32)
            for other in others:
                total += other[r, :].astype(F32)
            part[at, :] = total.astype(BF16)

    def pair(w, d):
        part, ry = parts[w][:2]
        size = parts[w][-1].shape[1]
        for j in range(1, ny):
            give(w, d, y, j).wait_recv()
        add(part, (d * ny + y) * size, size - tail_rows(size),
            [ry.at[(j - 1) * nz + d] for j in range(1, ny)])

    def run(w, p):
        part, ry, rz, rt = parts[w][:4]
        size = parts[w][-1].shape[1]
        q = tail_rows(size)
        d = order[p]
        way = jnp.where(d > z, 0, 1)
        sgn = 1 - 2 * way
        nxt = z + sgn
        pair(w, d)

        @pl.when(inside(z - sgn))
        def _():
            run_block(w, way, d, nxt).wait_recv()
            for j in range(1, ny):
                run_tail(w, way, d, nxt, j).wait_recv()
            add(part, (d * ny + y) * size, size, [rz.at[way, d]])
            for j in range(1, ny):
                add(part, (d * ny + yp(j)) * size + size - q, q, [rt.at[way, d, j - 1]])

        copies = [run_block(w, way, d, nxt)]
        copies += [run_tail(w, way, d, nxt, j) for j in range(1, ny)]
        for copy in copies:
            copy.start()
            sends.append(copy)

    def part_last(w):
        part, ry, rz, rt = parts[w][:4]
        size = parts[w][-1].shape[1]
        q = tail_rows(size)
        pair(w, z)
        for way in range(2):
            sgn = 1 - 2 * way

            @pl.when(inside(z - sgn))
            def _():
                for j in range(1, ny):
                    run_tail(w, way, z, zp(1), j).wait_recv()
                    add(part, (z * ny + yp(j)) * size + size - q, q, [rt.at[way, z, j - 1]])

        for j in range(1, ny):
            copy = last_tail(w, j)
            copy.start()
            sends.append(copy)
        for way in range(2):
            sgn = 1 - 2 * way

            @pl.when(inside(z - sgn))
            def _():
                run_block(w, way, z, zp(1)).wait_recv()
                add(part, (z * ny + y) * size, size, [rz.at[way, z]])

    def part_end(w):
        part, ry, rz, rt, ft, out = parts[w]
        size = out.shape[1]
        q = tail_rows(size)
        for j in range(1, ny):
            last_tail(w, j).wait_recv()
        add(part, (z * ny + y) * size + size - q, q, [ft.at[j - 1] for j in range(1, ny)])

        @tiles(size, 16)
        def _(r):
            out[0, r, :] = part[pl.ds(pl.multiple_of(f * size + r.start, 16), 16), :]

    backs = ((cot, rc_m, rx_m, mixed_out), (tok, rc_t, rx_t, tg_out))

    def back_start(w):
        full, rc, rx, out = backs[w]
        for k in range(nx):
            k = (k + 1) % nx
            send(rows(full, xp(k) * 2 + 1 - c, T), rc.at[k], rc_s.at[w, k], rc_r.at[w, k],
                 edev(x, 1 - c))

    def back_pair(w):
        full, rc, rx, out = backs[w]
        for k in range(nx):
            k = (k + 1) % nx
            index = xp(k) * 2 + c
            slot = rc.at[k]
            remote(slot, slot, rc_s.at[w, k], rc_r.at[w, k], edev(x, 1 - c)).wait_recv()

            @tiles(T, 16)
            def _(r):
                at = pl.ds(pl.multiple_of(index * T + r.start, 16), 16)
                full[at, :] = (full[at, :].astype(F32) + rc[k, r, :].astype(F32)).astype(BF16)

            if k:
                send(rows(full, index, T), rx.at[k - 1], rx_s.at[w, k - 1], rx_r.at[w, k - 1],
                     edev(xp(k), c))

    def back_end(w):
        full, rc, rx, out = backs[w]
        for k in range(1, nx):
            slot = rx.at[k - 1]
            remote(slot, slot, rx_s.at[w, k - 1], rx_r.at[w, k - 1], edev(xp(k), c)).wait_recv()

        @tiles(T, 16)
        def _(r):
            at = pl.ds(pl.multiple_of(e * T + r.start, 16), 16)
            total = full[at, :].astype(F32)
            for k in range(1, nx):
                total += rx[k - 1, r, :].astype(F32)
            out[r, :] = total.astype(BF16)

    hop(1, 3)
    hop_tail(1, 2)
    part_start(1)
    hop_tail(1, 3)
    weight_wait(1)

    @tiles(FF, 256)
    def _(n):
        dpre[:, n] = (dot(cot[...], down[n, :], NT) * slope[:, n]).astype(BF16)

    run(1, 0)

    @tiles(D, 384)
    def _(n):
        upart[n, :] = dot(tok[:, n], dpre[...], TN).astype(BF16)

    part_start(0)
    run(1, 1)

    @tiles(D, 512)
    def _(n):
        cot[:, n] = (dot(hidden[...], down[:, n], NN) * gate[:, 0:1]).astype(BF16)

    back_start(0)
    run(1, 2)
    for copy in tok_forwards:
        copy.wait_send()

    @tiles(D, 512)
    def _(n):
        tok[:, n] = dot(dpre[...], up[n, :], NT).astype(BF16)

    back_start(1)
    back_pair(0)
    back_pair(1)
    run(0, 0)
    part_last(1)
    back_end(0)
    run(0, 1)
    back_end(1)
    part_end(1)
    run(0, 2)
    part_last(0)
    part_end(0)
    for copy in sends:
        copy.wait_send()
    for there, copies in guarded:
        @pl.when(there)
        def _():
            for copy in copies:
                copy.wait_send()


def body(tokens, expert_ids, gates, up_weight, down_weight, cotangent):
    nf, ne = lax.axis_size("fsdp"), lax.axis_size("ep")
    nz = 4
    ny, nx = nf // nz, ne // 2
    T, D = tokens.shape
    R = ne * T
    su, FF = up_weight.shape[1:]
    sd = down_weight.shape[1]
    chosen = expert_ids[None] == jnp.arange(ne, dtype=jnp.int32)[:, None, None]
    dense = jnp.sum(jnp.where(chosen, gates[None], 0.0), axis=2)
    gcols = jnp.broadcast_to(dense[:, :, None], (ne, T, LANES))
    qu, qd = (tail_rows(size) for size in (su, sd))
    anyspace = pl.BlockSpec(memory_space=pl.ANY)
    vmem = pl.BlockSpec(memory_space=pltpu.VMEM)
    sem = pltpu.SemaphoreType.DMA
    V = pltpu.VMEM
    scratch = [
        V((D, FF), BF16), V((FF, D), BF16), V((R, D), BF16), V((R, D), BF16),
        V((R, LANES), F32), V((R, FF), F32), V((R, FF), BF16), V((R, FF), BF16),
        V((D, FF), BF16), V((FF, D), BF16),
        V(((ny - 1) * nz, su - qu, FF), BF16), V(((ny - 1) * nz, sd - qd, D), BF16),
        V((2, nz, su, FF), BF16), V((2, nz, sd, D), BF16),
        V((2, nz, ny - 1, qu, FF), BF16), V((2, nz, ny - 1, qd, D), BF16),
        V((ny - 1, qu, FF), BF16), V((ny - 1, qd, D), BF16),
        V((nx, T, D), BF16), V((nx, T, D), BF16),
        V((nx - 1, T, D), BF16), V((nx - 1, T, D), BF16),
        sem((4,)),
        sem((2, 2, nz)), sem((2, 2, nz)),
        sem((2, 2, nz, ny - 1)), sem((2, 2, nz, ny - 1)),
        sem((2, ny - 1)), sem((2, ny - 1)),
        sem((2, nz, ny - 1)), sem((2, nz, ny - 1)),
        sem((2, nx - 1)), sem((2, nx - 1)),
        sem((2, nx)), sem((2, nx)),
        sem((ne - 1,)), sem((ne - 1,)),
        sem((2, nz, ny - 1)), sem((2, nz, ny - 1)),
        sem((2, nz)), sem((2, 2, nz)),
        sem((2, nz, ny - 1)), sem((2, 2, nz, ny - 1)),
        sem((2, ny - 1)), sem((2, ny - 1)),
        sem((2, nx)), sem((2, nx)),
        sem((2, nx - 1)), sem((2, nx - 1)),
    ]
    return pl.pallas_call(
        functools.partial(kernel, nz, ny, nx),
        out_shape=(
            jax.ShapeDtypeStruct((T, D), BF16),
            jax.ShapeDtypeStruct((T, D), BF16),
            jax.ShapeDtypeStruct((1, su, FF), BF16),
            jax.ShapeDtypeStruct((1, sd, D), BF16),
        ),
        in_specs=[anyspace, anyspace, vmem, anyspace, anyspace],
        out_specs=(vmem, vmem, vmem, vmem),
        scratch_shapes=scratch,
        compiler_params=pltpu.CompilerParams(
            collective_id=0, has_side_effects=True, vmem_limit_bytes=64 * 1024 * 1024 - 262144
        ),
    )(tokens, cotangent, gcols, up_weight, down_weight)


def grouped(nz, *refs):
    (tok_in, cot_in, ids_in, gate_in, up_in, down_in,
     mixed_out, tg_out, ug_out, dg_out,
     up, down, tok, cot, upl, perm, uex, gd, gcol, slope, dh, hidden, dpre, upart, dpart,
     rz_u, rz_d, yrecv, rc_m, rc_t, r2_m, r2_t, r3_m, r3_t,
     local_sem, us, ur, ds_s, ds_r, yx_s, yx_r, tx_s, tx_r, ty_s, ty_r, fx_s, fx_r, fy_s, fy_r,
     tc_s, tc_r, g_s, g_r, ru_s, ru_r, rd_s, rd_r, yg_s, yg_r, b1_s, b1_r, b2_s, b2_r, b3_s, b3_r,
     ids, gate, ob, od, ou) = refs
    f = lax.axis_index("fsdp")
    e = lax.axis_index("ep")
    z, y = lax.div(f, 2), lax.rem(f, 2)
    x, c = lax.div(e, 2), lax.rem(e, 2)
    T, D = tok_in.shape
    SU, FF = up_in.shape[1:]
    SD = down_in.shape[1]
    G3 = nz * SD
    H = FF // 2
    R = 8 * T
    N = len(WIDTHS)
    begins = [D * sum(WIDTHS[:n]) // sum(WIDTHS) for n in range(N + 1)]

    def inside(zz):
        return (zz >= 0) & (zz < nz)

    def zp(k):
        return lax.rem(z + k + nz, nz)

    def zdev(zz):
        return {"fsdp": lax.rem(zz + nz, nz) * 2 + y}

    ydev = {"fsdp": z * 2 + 1 - y}
    xdev = {"ep": (1 - x) * 2 + c}
    cdev = {"ep": x * 2 + 1 - c}

    def blk(yy, xx, cc):
        return cc * 4 + yy * 2 + xx

    me = blk(y, x, c)

    def rows(index, size):
        return pl.ds(pl.multiple_of(index * size, size), size)

    def lanes(index, size):
        return pl.ds(pl.multiple_of(index * size, size), size)

    def cols(n):
        return pl.ds(begins[n], begins[n + 1] - begins[n])

    def cols_a(n):
        return pl.ds(begins[n], SPLITS[n])

    def cols_b(n):
        return pl.ds(begins[n] + SPLITS[n], begins[n + 1] - begins[n] - SPLITS[n])

    units = (pl.ds(0, 2 * G3), pl.ds(2 * G3, G3))
    sets = (pl.ds(0, 2), pl.ds(2, 1))

    def remote(src, dst, ss, rs, dev):
        return pltpu.make_async_remote_copy(
            src_ref=src, dst_ref=dst, send_sem=ss, recv_sem=rs,
            device_id=dev, device_id_type=MESH,
        )

    sends = []
    guarded = []

    def go(copy, keep=sends):
        copy.start()
        keep.append(copy)

    def go_when(there, copy):
        @pl.when(there)
        def _():
            copy.start()

        guarded.append((there, copy))

    barrier = pltpu.get_barrier_semaphore()
    offsets = [(i // 4, i // 2 % 2, i % 2) for i in range(1, 8)]

    def gdev(dy, dx, dc):
        yy = 1 - y if dy else y
        xx = 1 - x if dx else x
        cc = 1 - c if dc else c
        return yy, xx, cc

    for sgn in (1, -1):
        @pl.when(inside(z + sgn))
        def _():
            pl.semaphore_signal(barrier, inc=1, device_id=zdev(z + sgn), device_id_type=MESH)

    for offset in offsets:
        yy, xx, cc = gdev(*offset)
        pl.semaphore_signal(barrier, inc=1, device_id={"fsdp": z * 2 + yy, "ep": xx * 2 + cc},
                            device_id_type=MESH)
    locals_ = []
    for i, (src, dst) in enumerate((
        (up_in.at[0], upl),
        (down_in, down.at[:, rows(z, SD)]),
        (tok_in, tok.at[rows(me, T)]),
        (cot_in, cot.at[rows(me, T)]),
        (ids_in, ids),
        (gate_in, gate),
    )):
        copy = pltpu.make_async_copy(src, dst, local_sem.at[i])
        copy.start()
        locals_.append(copy)

    near = z + lax.div(z, 2) * (3 - 2 * z)
    pl.semaphore_wait(barrier, len(offsets) + 1 + jnp.minimum(near, 1))

    def permute_up():
        @pl.loop(0, 6 * nz)
        def _(i):
            half, third, zz = lax.div(i, 3 * nz), lax.rem(lax.div(i, nz), 3), lax.rem(i, nz)
            column = lax.broadcasted_iota(jnp.int32, (SD, FF), 1)
            first = SD * (3 * (2 * zz + half) + third)
            unit = lax.broadcasted_iota(jnp.int32, (SD, FF), 0) + first
            perm[rows(i, SD), :] = jnp.where(column == unit, 1.0, 0.0).astype(BF16)

        locals_[0].wait()
        up[rows(f, SU), :] = dot(upl[...], perm[rows(y, H), :], NT).astype(BF16)
        uex[...] = dot(upl[...], perm[rows(1 - y, H), :], NT).astype(BF16)

    def sub(p):
        return y if p % 2 == 0 else 1 - y

    def chain_u(p, sgn, b, own=False):
        block = up.at[rows(2 * b + sub(p), SU), units[p // 2]]
        way = (1 - sgn) // 2
        return remote(block, block, us.at[p, way, b], ur.at[p, way, b], zdev(z + sgn))

    def chain_d(n, sgn, b, own=False):
        block = down.at[:, rows(b, SD), cols(n)]
        way = (1 - sgn) // 2
        return remote(down_in.at[:, :, cols(n)] if own else block, block, ds_s.at[n, way, b], ds_r.at[n, way, b], zdev(z + sgn))

    def own_start(chain, n):
        for sgn in (1, -1):
            go_when(inside(z + sgn), chain(n, sgn, z, True))

    def hop(chain, n, s):
        for sgn in (1, -1):
            b = zp(-sgn * s)
            there = inside(z - sgn * s)

            @pl.when(there)
            def _():
                chain(n, sgn, b).wait_recv()

            go_when(there & inside(z + sgn), chain(n, sgn, b))

    y_exchange = [remote(uex.at[:, units[g]], up.at[rows(f, SU), units[g]], yx_s.at[g], yx_r.at[g], ydev)
                  for g in range(2)]

    acts = ((tok_in, tok), (cot_in, cot))
    forwards = ([[] for _ in range(N)], [[] for _ in range(N)])

    def act_own(w, n):
        src, full = acts[w]
        there = full.at[rows(me, T), cols(n)]
        go(remote(src.at[:, cols(n)], there, tx_s.at[w, n], tx_r.at[w, n], xdev))
        go(remote(src.at[:, cols(n)], there, ty_s.at[w, n], ty_r.at[w, n], ydev))
        go(remote(src.at[:, cols(n)], there, tc_s.at[w, n, 0], tc_r.at[w, n, 0], cdev))

    def high_rows(b):
        return pl.ds(pl.multiple_of(b * T, 16), SHARE)

    def low_rows(b):
        return pl.ds(pl.multiple_of(b * T + SHARE, 16), T - SHARE)

    def act_fwd(w, n):
        full = acts[w][1]
        keep = forwards[w][n]
        bx, by = blk(y, 1 - x, c), blk(1 - y, x, c)
        here = full.at[rows(bx, T), cols(n)]
        part = full.at[low_rows(bx), cols(n)]
        remote(here, here, tx_s.at[w, n], tx_r.at[w, n], xdev).wait_recv()
        go(remote(part, part, fy_s.at[w, n], fy_r.at[w, n], ydev), keep)
        go(remote(here, here, tc_s.at[w, n, 1], tc_r.at[w, n, 1], cdev), keep)
        here = full.at[rows(by, T), cols(n)]
        part = full.at[high_rows(by), cols(n)]
        remote(here, here, ty_s.at[w, n], ty_r.at[w, n], ydev).wait_recv()
        go(remote(part, part, fx_s.at[w, n], fx_r.at[w, n], xdev), keep)
        go(remote(here, here, tc_s.at[w, n, 2], tc_r.at[w, n, 2], cdev), keep)

    def act_diag(w, n):
        full = acts[w][1]
        bd = blk(1 - y, 1 - x, c)
        low = full.at[high_rows(bd), cols(n)]
        high = full.at[low_rows(bd), cols(n)]
        here = full.at[rows(bd, T), cols(n)]
        remote(low, low, fx_s.at[w, n], fx_r.at[w, n], xdev).wait_recv()
        remote(high, high, fy_s.at[w, n], fy_r.at[w, n], ydev).wait_recv()
        go(remote(here, here, tc_s.at[w, n, 3], tc_r.at[w, n, 3], cdev), forwards[w][n])

    def act_done(w, n):
        full = acts[w][1]
        others = ((y, x), (y, 1 - x), (1 - y, x), (1 - y, 1 - x))
        for k, (yy, xx) in enumerate(others):
            here = full.at[rows(blk(yy, xx, 1 - c), T), cols(n)]
            remote(here, here, tc_s.at[w, n, k], tc_r.at[w, n, k], cdev).wait_recv()

    def gates_start():
        locals_[4].wait()
        locals_[5].wait()
        expert = lax.broadcasted_iota(jnp.int32, (8, T), 0)
        gd[me] = jnp.where(ids[0:1, :] == expert, gate[0:1, :], 0.0) + jnp.where(
            ids[1:2, :] == expert, gate[1:2, :], 0.0)
        for i, offset in enumerate(offsets):
            yy, xx, cc = gdev(*offset)
            go(remote(gd.at[me], gd.at[me], g_s.at[i], g_r.at[i],
                      {"fsdp": z * 2 + yy, "ep": xx * 2 + cc}))

    def gates_done():
        for i, offset in enumerate(offsets):
            yy, xx, cc = gdev(*offset)
            here = gd.at[blk(yy, xx, cc)]
            remote(here, here, g_s.at[i], g_r.at[i],
                   {"fsdp": z * 2 + yy, "ep": xx * 2 + cc}).wait_recv()

        @pl.loop(0, 8)
        def _(b):
            mine = lax.broadcasted_iota(jnp.int32, (8, T), 0) == e
            row = jnp.sum(jnp.where(mine, gd[b], 0.0), axis=0, keepdims=True)
            eye = lax.broadcasted_iota(jnp.int32, (T, T), 0) == lax.broadcasted_iota(
                jnp.int32, (T, T), 1)
            column = jnp.sum(jnp.where(eye, row, 0.0), axis=1, keepdims=True)
            gcol[rows(b, T), :] = jnp.broadcast_to(column, (T, LANES))

    flip = lax.div(z, 2)
    near = z + flip * (3 - 2 * z)
    order = [d + flip * (3 - 2 * d) for d in (near * 0 + 3, 2 - 2 * near, 1 + near, near)]
    is_end = near == 0

    def pre_step(g, s):
        plane = order[3 - s]
        u = units[g]
        if g == 0 and s == 0:
            locals_[2].wait()
            locals_[3].wait()

        @tiles(R, 256)
        def _(r):
            part = dot(tok[r, lanes(plane, 2 * SU)], up[rows(plane, 2 * SU), u], NN)
            if s == 0:
                slope[r, u] = part
            elif s < nz - 1:
                slope[r, u] += part
            else:
                value, grad = gelu_parts(slope[r, u] + part)
                hidden[r, u] = (value * gcol[r, 0:1]).astype(BF16)
                slope[r, u] = grad * gcol[r, 0:1]

    def tokens_sent():
        for copies in forwards[0]:
            for copy in copies:
                copy.wait_send()

    def chunk_tiles(n):
        size = TILE

        def run(fn):
            @pl.loop(0, (begins[n + 1] - begins[n]) // size)
            def _(i):
                fn(pl.ds(pl.multiple_of(begins[n] + i * size, size), size))

        return run

    def down_part(g, n):
        @chunk_tiles(n)
        def _(t):
            part = dot(hidden[:, units[g]], cot[:, t], TN).astype(BF16)
            dpart[sets[g], :, t] = part.reshape(2 - g, G3, TILE)

    def back_hidden(n):
        if n == 0:
            locals_[1].wait()

        @tiles(R, 256)
        def _(r):
            part = dot(cot[r, cols(n)], down[:, :, cols(n)].reshape(H, begins[n + 1] - begins[n]), NT)
            if n == 0:
                dh[r, :] = part
            elif n < N - 1:
                dh[r, :] += part
            else:
                dpre[r, :] = ((dh[r, :] + part) * slope[r, :]).astype(BF16)

    def mixed_part(n):
        for copy in forwards[1][n]:
            copy.wait_send()

        @chunk_tiles(n)
        def _(t):
            @tiles(R, ROWS)
            def _(r):
                cot[r, t] = dot(hidden[r, :], down[:, :, t].reshape(H, TILE), NN).astype(BF16)

    def token_part(n):
        @chunk_tiles(n)
        def _(t):
            @tiles(R, ROWS)
            def _(r):
                tok[r, t] = dot(dpre[r, :], up[t, :], NT).astype(BF16)

    def up_part(q, pos):
        at = rows(2 * order[pos] + (1 - sub(q)), SU)
        upart[at, :] = dot(tok[:, at], dpre[...], TN).astype(BF16)

    def send_down(m, d, way, nxt):
        g, n = m // N, m % N
        return remote(dpart.at[sets[g], rows(d, SD), cols(n)], rz_d.at[way, d, sets[g], :, cols(n)],
                      rd_s.at[m, d], rd_r.at[m, way, d], zdev(nxt))

    def send_up(q, d, way, nxt):
        return remote(upart.at[rows(2 * d + (1 - sub(q)), SU)], rz_u.at[q, way, d],
                      ru_s.at[q, d], ru_r.at[q, way, d], zdev(nxt))

    def add_down(m, d, way):
        g, n = m // N, m % N

        @tiles(SD, 16)
        def _(r):
            at = pl.ds(pl.multiple_of(d * SD + r.start, 16), 16)
            dpart[sets[g], at, cols(n)] = (dpart[sets[g], at, cols(n)].astype(F32)
                                           + rz_d[way, d, sets[g], r, cols(n)].astype(F32)).astype(BF16)

    def add_up(q, d, way):
        @tiles(SU, 32)
        def _(r):
            at = pl.ds(pl.multiple_of((2 * d + (1 - sub(q))) * SU + r.start, 32), 32)
            upart[at, :] = (upart[at, :].astype(F32)
                            + rz_u[q, way, d, r, :].astype(F32)).astype(BF16)

    downs, ups = (send_down, add_down), (send_up, add_up)

    def course(pos):
        d = order[pos]
        way = jnp.where(d > z, 0, 1)
        return d, way, z + 1 - 2 * way

    def begin(kind, n, pos):
        d, way, nxt = course(pos)
        go_when(is_end, kind[0](n, d, way, nxt))

    def middle(kind, n, pos):
        d, way, nxt = course(pos)
        copy = kind[0](n, d, way, nxt)

        @pl.when(jnp.logical_not(is_end))
        def _():
            copy.wait_recv()
            kind[1](n, d, way)
            copy.start()

        guarded.append((jnp.logical_not(is_end), copy))

    def last(kind, n):
        for way in range(2):
            @pl.when(inside(z - 1 + 2 * way))
            def _():
                kind[0](n, z, way, zp(1)).wait_recv()
                kind[1](n, z, way)

    results = []

    def result(src, dst, done):
        copy = pltpu.make_async_copy(src, dst, done)
        copy.start()
        results.append(copy)

    def down_end(m):
        g, n = m // N, m % N
        last(downs, m)
        result(dpart.at[sets[g], rows(z, SD), cols(n)], dg_out.at[sets[g], :, cols(n)], od.at[m])

    other_up = upart.at[rows(2 * z + 1 - y, SU)]
    y_return = remote(other_up, yrecv, yg_s.at[0], yg_r.at[0], ydev)

    def up_end():
        last(ups, 1)
        y_return.wait_recv()
        upl[...] = (dot(upart[rows(f, SU), :], perm[rows(y, H), :], NN)
                     + dot(yrecv[...], perm[rows(1 - y, H), :], NN)).astype(BF16)
        result(upl, ug_out.at[0], ou.at[0])

    backs = ((cot, rc_m, r2_m, r3_m, mixed_out), (tok, rc_t, r2_t, r3_t, tg_out))
    G = 4 * T

    def back1(w, n):
        full, rc = backs[w][:2]
        go(remote(full.at[rows(1 - c, G), cols(n)], rc.at[:, cols(n)],
                  b1_s.at[w, n], b1_r.at[w, n], cdev))

    def back2(w, n):
        full, rc, r2 = backs[w][:3]
        here = rc.at[:, cols(n)]
        remote(here, here, b1_s.at[w, n], b1_r.at[w, n], cdev).wait_recv()

        @tiles(G, 16)
        def _(r):
            at = pl.ds(pl.multiple_of(c * G + r.start, 16), 16)
            full[at, cols(n)] = (full[at, cols(n)].astype(F32)
                                 + rc[r, cols(n)].astype(F32)).astype(BF16)

        for yy in range(2):
            go(remote(full.at[rows(blk(yy, 1 - x, c), T), cols_a(n)],
                      r2.at[pl.ds(yy * T, T), cols_a(n)],
                      b2_s.at[w, n, yy], b2_r.at[w, n, yy], xdev))
        go(remote(full.at[rows(c * 2 + 1 - y, 2 * T), cols_b(n)], r2.at[:, cols_b(n)],
                  b2_s.at[w, n, 2], b2_r.at[w, n, 2], ydev))

    def back3(w, n):
        full, rc, r2, r3 = backs[w][:4]
        for yy in range(2):
            here = r2.at[pl.ds(yy * T, T), cols_a(n)]
            remote(here, here, b2_s.at[w, n, yy], b2_r.at[w, n, yy], xdev).wait_recv()
        here = r2.at[:, cols_b(n)]
        remote(here, here, b2_s.at[w, n, 2], b2_r.at[w, n, 2], ydev).wait_recv()
        ba, bb = blk(1 - y, x, c), blk(y, 1 - x, c)

        @tiles(T, 16)
        def _(r):
            at = pl.ds(pl.multiple_of(ba * T + r.start, 16), 16)
            there = pl.ds(pl.multiple_of((1 - y) * T + r.start, 16), 16)
            full[at, cols_a(n)] = (full[at, cols_a(n)].astype(F32)
                                   + r2[there, cols_a(n)].astype(F32)).astype(BF16)
            at = pl.ds(pl.multiple_of(bb * T + r.start, 16), 16)
            there = pl.ds(pl.multiple_of((1 - x) * T + r.start, 16), 16)
            full[at, cols_b(n)] = (full[at, cols_b(n)].astype(F32)
                                   + r2[there, cols_b(n)].astype(F32)).astype(BF16)

        go(remote(full.at[rows(ba, T), cols_a(n)], r3.at[:, cols_a(n)],
                  b3_s.at[w, n, 0], b3_r.at[w, n, 0], ydev))
        go(remote(full.at[rows(bb, T), cols_b(n)], r3.at[:, cols_b(n)],
                  b3_s.at[w, n, 1], b3_r.at[w, n, 1], xdev))

    def back4(w, n):
        full, rc, r2, r3, out = backs[w]
        for k, (span, dev) in enumerate(((cols_a(n), ydev), (cols_b(n), xdev))):
            here = r3.at[:, span]
            remote(here, here, b3_s.at[w, n, k], b3_r.at[w, n, k], dev).wait_recv()

        @tiles(T, 16)
        def _(r):
            at = pl.ds(pl.multiple_of(me * T + r.start, 16), 16)
            for span, lane in ((cols_a(n), y), (cols_b(n), x)):
                there = pl.ds(pl.multiple_of(lane * T + r.start, 16), 16)
                full[at, span] = (full[at, span].astype(F32) + r2[there, span].astype(F32)
                                + r3[r, span].astype(F32)).astype(BF16)

        result(full.at[rows(me, T), cols(n)], out.at[:, cols(n)], ob.at[w, n])

    gates_start()
    own_start(chain_d, 0)
    act_own(0, 2)
    own_start(chain_d, 1)
    permute_up()
    go(y_exchange[0])
    act_own(0, 0)
    hop(chain_d, 0, 1)
    act_own(0, 3)
    own_start(chain_u, 0)
    y_exchange[0].wait_recv()
    act_own(0, 1)
    own_start(chain_u, 1)
    hop(chain_u, 0, 1)
    act_own(1, 1)
    hop(chain_u, 1, 1)
    own_start(chain_u, 2)
    act_fwd(0, 3)
    act_fwd(0, 2)
    act_fwd(0, 0)
    gates_done()
    act_fwd(0, 1)
    go(y_exchange[1])
    act_fwd(1, 1)
    act_own(1, 0)
    hop(chain_u, 0, 2)
    act_own(1, 2)
    hop(chain_u, 1, 2)
    hop(chain_u, 2, 1)
    act_diag(0, 2)
    act_diag(0, 3)
    act_diag(0, 1)
    act_done(0, 3)
    act_done(0, 2)
    act_diag(0, 0)
    hop(chain_u, 0, 3)
    y_exchange[1].wait_recv()
    act_done(0, 0)
    act_done(0, 1)
    own_start(chain_d, 2)
    pre_step(0, 0)
    pre_step(0, 1)
    own_start(chain_u, 3)
    hop(chain_u, 1, 3)
    act_diag(1, 1)
    pre_step(1, 0)
    pre_step(0, 2)
    hop(chain_d, 0, 2)
    own_start(chain_d, 3)
    act_done(1, 1)
    pre_step(0, 3)
    act_fwd(1, 0)
    down_part(0, 1)
    begin(downs, 0 * N + 1, 2)
    hop(chain_u, 3, 1)
    begin(downs, 0 * N + 1, 1)
    act_fwd(1, 2)
    hop(chain_u, 2, 2)
    act_diag(1, 0)
    begin(downs, 0 * N + 1, 0)
    pre_step(1, 1)
    act_own(1, 3)
    act_done(1, 0)
    down_part(0, 0)
    act_diag(1, 2)
    begin(downs, 0 * N + 0, 2)
    hop(chain_d, 0, 3)
    back_hidden(0)
    act_done(1, 2)
    down_part(0, 2)
    begin(downs, 0 * N + 0, 1)
    begin(downs, 0 * N + 2, 0)
    begin(downs, 0 * N + 0, 0)
    hop(chain_u, 3, 2)
    hop(chain_u, 2, 3)
    hop(chain_d, 1, 1)
    begin(downs, 0 * N + 2, 1)
    begin(downs, 0 * N + 2, 2)
    pre_step(1, 2)
    act_fwd(1, 3)
    hop(chain_u, 3, 3)
    pre_step(1, 3)
    down_part(1, 0)
    mixed_part(0)
    back1(0, 0)
    hop(chain_d, 1, 2)
    begin(downs, 1 * N + 0, 0)
    begin(downs, 1 * N + 0, 2)
    down_part(1, 2)
    down_part(1, 1)
    begin(downs, 1 * N + 1, 0)
    begin(downs, 1 * N + 0, 1)
    act_diag(1, 3)
    begin(downs, 1 * N + 2, 0)
    hop(chain_d, 2, 1)
    back2(0, 0)
    hop(chain_d, 1, 3)
    act_done(1, 3)
    back_hidden(1)
    mixed_part(1)
    back1(0, 1)
    down_part(1, 3)
    begin(downs, 1 * N + 3, 0)
    hop(chain_d, 2, 2)
    hop(chain_d, 3, 1)
    down_part(0, 3)
    begin(downs, 0 * N + 3, 0)
    begin(downs, 1 * N + 2, 1)
    middle(downs, 0 * N + 1, 2)
    back2(0, 1)
    hop(chain_d, 2, 3)
    middle(downs, 0 * N + 1, 0)
    middle(downs, 0 * N + 2, 2)
    begin(downs, 1 * N + 1, 2)
    begin(downs, 1 * N + 1, 1)
    back_hidden(2)
    mixed_part(2)
    back1(0, 2)
    begin(downs, 0 * N + 3, 2)
    back3(0, 0)
    middle(downs, 0 * N + 0, 0)
    hop(chain_d, 3, 2)
    middle(downs, 1 * N + 1, 0)
    begin(downs, 0 * N + 3, 1)
    middle(downs, 0 * N + 0, 2)
    begin(downs, 1 * N + 3, 1)
    middle(downs, 1 * N + 2, 0)
    back2(0, 2)
    back3(0, 1)
    hop(chain_d, 3, 3)
    back_hidden(3)
    up_part(0, 0)
    begin(ups, 0, 0)
    mixed_part(3)
    middle(downs, 1 * N + 3, 0)
    middle(downs, 0 * N + 3, 0)
    back1(0, 3)
    up_part(0, 3)
    up_part(1, 0)
    middle(downs, 0 * N + 3, 2)
    up_part(1, 3)
    middle(downs, 1 * N + 1, 1)
    up_part(1, 2)
    up_part(0, 1)
    middle(downs, 1 * N + 0, 2)
    back2(0, 3)
    up_part(1, 1)
    up_part(0, 2)
    begin(ups, 0, 1)
    middle(downs, 1 * N + 0, 0)
    middle(downs, 0 * N + 1, 1)
    tokens_sent()
    token_part(1)
    middle(downs, 0 * N + 0, 1)
    back1(1, 1)
    middle(downs, 1 * N + 3, 2)
    back3(0, 2)
    token_part(3)
    middle(downs, 0 * N + 2, 0)
    back2(1, 1)
    middle(downs, 1 * N + 3, 1)
    begin(ups, 1, 0)
    middle(downs, 1 * N + 1, 2)
    middle(ups, 0, 0)
    token_part(2)
    back3(0, 3)
    back1(1, 3)
    back1(1, 2)
    begin(ups, 0, 2)
    token_part(0)
    back2(1, 3)
    begin(ups, 1, 1)
    back4(0, 1)
    back1(1, 0)
    middle(downs, 1 * N + 0, 1)
    middle(downs, 0 * N + 3, 1)
    middle(ups, 0, 2)
    back2(1, 2)
    middle(ups, 0, 1)
    back2(1, 0)
    middle(ups, 1, 0)
    middle(downs, 1 * N + 2, 2)
    begin(ups, 1, 2)
    back3(1, 1)
    begin(downs, 1 * N + 2, 2)
    down_end(1 * N + 1)
    back3(1, 3)
    middle(downs, 0 * N + 2, 1)
    down_end(0 * N + 0)
    last(ups, 0)
    back4(0, 2)
    go(y_return)
    back3(1, 2)
    back4(0, 0)
    middle(downs, 1 * N + 2, 1)
    down_end(0 * N + 2)
    down_end(0 * N + 1)
    down_end(1 * N + 0)
    middle(ups, 1, 2)
    middle(ups, 1, 1)
    begin(downs, 1 * N + 3, 2)
    back3(1, 0)
    back4(1, 3)
    back4(1, 2)
    back4(0, 3)
    back4(1, 1)
    down_end(0 * N + 3)
    up_end()
    down_end(1 * N + 2)
    down_end(1 * N + 3)
    back4(1, 0)
    for copy in sends:
        copy.wait_send()
    for copy in results:
        copy.wait()
    for there, copy in guarded:
        @pl.when(there)
        def _():
            copy.wait_send()


def settle(*refs):
    sources, results, held, arrived, done = refs[:4], refs[4:8], refs[8:12], refs[12], refs[13]
    ins = [pltpu.make_async_copy(a, b, arrived.at[i]) for i, (a, b) in enumerate(zip(sources, held))]
    outs = [pltpu.make_async_copy(a, b, done.at[i]) for i, (a, b) in enumerate(zip(held, results))]
    for copy in ins:
        copy.start()
    for arrival, copy in zip(ins, outs):
        arrival.wait()
        copy.start()
    for copy in outs:
        copy.wait()


def grouped_body(nz, tokens, expert_ids, gates, up_weight, down_weight, cotangent):
    T, D = tokens.shape
    R = 8 * T
    SU, FF = up_weight.shape[1:]
    SD = down_weight.shape[1] // 3
    H = FF // 2
    N = len(WIDTHS)
    anyspace = pl.BlockSpec(memory_space=pl.ANY)
    sem = pltpu.SemaphoreType.DMA
    V = pltpu.VMEM

    def pair(*shape):
        return [sem(shape), sem(shape)]

    scratch = [
        V((D, H), BF16), V((3, nz * SD, D), BF16), V((R, D), BF16), V((R, D), BF16),
        V((SU, FF), BF16), V((FF, FF), BF16), V((SU, H), BF16),
        V((8, 8, T), F32), V((R, LANES), F32), V((R, H), F32), V((R, H), F32),
        V((R, H), BF16), V((R, H), BF16), V((D, H), BF16), V((3, nz * SD, D), BF16),
        V((2, 2, nz, SU, H), BF16), V((2, nz, 3, SD, D), BF16), V((SU, H), BF16),
        V((4 * T, D), BF16), V((4 * T, D), BF16), V((2 * T, D), BF16), V((2 * T, D), BF16),
        V((T, D), BF16), V((T, D), BF16),
        sem((6,)),
        *pair(4, 2, nz), *pair(N, 2, nz), *pair(2),
        *pair(2, N), *pair(2, N), *pair(2, N), *pair(2, N), *pair(2, N, 4), *pair(7),
        sem((2, nz)), sem((2, 2, nz)), sem((2 * N, nz)), sem((2 * N, 2, nz)), *pair(1),
        *pair(2, N), *pair(2, N, 3), *pair(2, N, 2),
        V((2, T), jnp.int32), V((2, T), F32), sem((2, N)), sem((2 * N,)), sem((1,)),
    ]
    outs = pl.pallas_call(
        functools.partial(grouped, nz),
        out_shape=(
            jax.ShapeDtypeStruct((T, D), BF16),
            jax.ShapeDtypeStruct((T, D), BF16),
            jax.ShapeDtypeStruct((1, SU, FF), BF16),
            jax.ShapeDtypeStruct((3, SD, D), BF16),
        ),
        in_specs=[anyspace] * 6,
        out_specs=(anyspace,) * 4,
        scratch_shapes=scratch,
        compiler_params=pltpu.CompilerParams(
            collective_id=0, has_side_effects=True, vmem_limit_bytes=64 * 1024 * 1024 - 262144
        ),
    )(tokens, cotangent, expert_ids.T, gates.T, up_weight, down_weight.reshape(3, SD, D))
    outs = pl.pallas_call(
        settle,
        out_shape=tuple(jax.ShapeDtypeStruct(out.shape, out.dtype) for out in outs),
        in_specs=[anyspace] * 4,
        out_specs=(anyspace,) * 4,
        scratch_shapes=[V(out.shape, BF16) for out in outs] + [sem((4,)), sem((4,))],
    )(*outs)
    return *outs[:3], outs[3].reshape(down_weight.shape)


def solution(mesh):
    placed = (
        P(("fsdp", "ep"), None),
        P(("fsdp", "ep"), None),
        P(("fsdp", "ep"), None),
        P("ep", "fsdp", None),
        P("ep", "fsdp", None),
        P(("fsdp", "ep"), None),
    )
    nf, ne = mesh.shape["fsdp"], mesh.shape["ep"]
    run = functools.partial(grouped_body, 4) if (nf, ne) == (8, 4) else body
    return jax.shard_map(
        run,
        mesh=mesh,
        in_specs=placed,
        out_specs=(
            P(("fsdp", "ep"), None),
            P(("fsdp", "ep"), None),
            P("ep", "fsdp", None),
            P("ep", "fsdp", None),
        ),
        check_vma=False,
    )
```

```python
import functools

import jax
import jax.numpy as jnp
from jax import lax
from jax.experimental import pallas as pl
from jax.experimental.pallas import tpu as pltpu
from jax.sharding import PartitionSpec as P

F32 = jnp.float32
BF16 = jnp.bfloat16
MESH = pl.DeviceIdType.MESH
LANES = 128
WIDTHS = (768, 768, 768, 768)
SPLITS = (512, 512, 512, 512)
SHARE = 80
TILE = 768
ROWS = 256


def gelu_parts(pre):
    root = 0.7978845608028654
    inner = root * (pre + 0.044715 * pre * pre * pre)
    tanh_val = jnp.tanh(inner)
    value = 0.5 * pre * (1.0 + tanh_val)
    slope = 0.5 * (1.0 + tanh_val) + 0.5 * pre * (1.0 - tanh_val * tanh_val) * root * (
        1.0 + 3.0 * 0.044715 * pre * pre
    )
    return (value, slope)


def dot(left, right, dims):
    return lax.dot_general(left, right, (dims, ((), ())), preferred_element_type=F32)


NN = ((1,), (0,))
NT = ((1,), (1,))
TN = ((0,), (0,))


def tail_rows(size):
    return max(16, size // 6 // 16 * 16)


def tiles(count, size):
    def run(fn):
        @pl.loop(0, count // size)
        def _(i):
            fn(pl.ds(pl.multiple_of(i * size, size), size))

    return run


def kernel(
    nz, ny, nx,
    tok_in, cot_in, gate_in, up_in, down_in,
    mixed_out, tg_out, ug_out, dg_out,
    up, down, tok, cot, gate, slope, hidden, dpre, upart, dpart,
    ry_u, ry_d, rz_u, rz_d, rt_u, rt_d, ft_u, ft_d, rc_m, rc_t, rx_m, rx_t,
    local_sem, wz_s, wz_r, wt_s, wt_r, wo_s, wo_r, wy_s, wy_r,
    tx_s, tx_r, tc_s, tc_r, g_s, g_r,
    ry_s, ry_r, rz_s, rz_r, rt_s, rt_r, ft_s, ft_r, rc_s, rc_r, rx_s, rx_r,
):
    ne = 2 * nx
    f = lax.axis_index("fsdp")
    e = lax.axis_index("ep")
    z, y = lax.div(f, ny), lax.rem(f, ny)
    x, c = lax.div(e, 2), lax.rem(e, 2)
    T = tok_in.shape[0]
    D = tok_in.shape[1]
    R = ne * T
    FF = up.shape[1]

    def zp(k):
        return lax.rem(z + k + nz, nz)

    def inside(zz):
        return (zz >= 0) & (zz < nz)

    def yp(j):
        return lax.rem(y + j + ny, ny)

    def xp(k):
        return lax.rem(x + k + nx, nx)

    def fdev(zz, yy):
        return {"fsdp": zz * ny + yy}

    def edev(xx, cc):
        return {"ep": xx * 2 + cc}

    def rows(ref, index, size):
        return ref.at[pl.ds(pl.multiple_of(index * size, size), size)]

    def remote(src, dst, ss, rs, dev):
        return pltpu.make_async_remote_copy(
            src_ref=src, dst_ref=dst, send_sem=ss, recv_sem=rs,
            device_id=dev, device_id_type=MESH,
        )

    sends = []
    guarded = []

    def send_when(there, copies):
        @pl.when(there)
        def _():
            for copy in copies:
                copy.start()

        guarded.append((there, copies))


    def send(src, dst, ss, rs, dev):
        copy = remote(src, dst, ss, rs, dev)
        copy.start()
        sends.append(copy)
        return copy

    barrier = pltpu.get_barrier_semaphore()
    peers = [fdev(zp(k), y) for k in range(1, nz)]
    peers += [fdev(z, yp(j)) for j in range(1, ny)]
    peers += [{"ep": lax.rem(e + i, ne)} for i in range(1, ne)]
    for dev in peers:
        pl.semaphore_signal(barrier, inc=1, device_id=dev, device_id_type=MESH)
    locals_ = []
    for i, (src, dst) in enumerate((
        (up_in.at[0], rows(up, f, up_in.shape[1])),
        (down_in.at[0], rows(down, f, down_in.shape[1])),
        (tok_in, rows(tok, e, T)),
        (cot_in, rows(cot, e, T)),
    )):
        copy = pltpu.make_async_copy(src, dst, local_sem.at[i])
        copy.start()
        locals_.append(copy)
    rows(gate, e, T)[...] = gate_in[e]
    pl.semaphore_wait(barrier, len(peers))

    weights = ((up_in, up), (down_in, down))

    def span(ref, index, size, begin, count):
        return ref.at[pl.ds(pl.multiple_of(index * size + begin, 16), count)]

    def chain(w, sgn, b, src=None):
        full = weights[w][1]
        size = weights[w][0].shape[1]
        block = rows(full, b * ny + y, size)
        way = (1 - sgn) // 2
        return remote(block if src is None else src, block, wz_s.at[w, way, b],
                      wz_r.at[w, way, b], fdev(zp(sgn), y))

    def chain_tail(w, sgn, b, j):
        full = weights[w][1]
        size = weights[w][0].shape[1]
        q = tail_rows(size)
        block = span(full, b * ny + yp(-j), size, size - q, q)
        way = (1 - sgn) // 2
        return remote(block, block, wt_s.at[w, way, b, j - 1], wt_r.at[w, way, b, j - 1],
                      fdev(zp(sgn), y))

    def across(w, b, yy, j):
        full = weights[w][1]
        size = weights[w][0].shape[1]
        block = span(full, b * ny + yy, size, 0, size - tail_rows(size))
        return remote(block, block, wy_s.at[w, b, j - 1], wy_r.at[w, b, j - 1], fdev(z, yp(j)))

    def own_across(w, yy, j, src=None):
        full = weights[w][1]
        size = weights[w][0].shape[1]
        block = rows(full, z * ny + yy, size)
        return remote(block if src is None else src, block, wo_s.at[w, j - 1], wo_r.at[w, j - 1],
                      fdev(z, yp(j)))

    def weight_start(w):
        src = weights[w][0].at[0]
        for sgn in (1, -1):
            send_when(inside(z + sgn), [chain(w, sgn, z, src)])
        for j in range(1, ny):
            copy = own_across(w, y, j, src)
            copy.start()
            sends.append(copy)

    def tail_start(w):
        for j in range(1, ny):
            own_across(w, yp(-j), j).wait_recv()
        for sgn in (1, -1):
            send_when(inside(z + sgn), [chain_tail(w, sgn, z, j) for j in range(1, ny)])

    def hop(w, s):
        for sgn in (1, -1):
            b = zp(-sgn * s)
            there = inside(z - sgn * s)

            @pl.when(there)
            def _():
                chain(w, sgn, b).wait_recv()

            send_when(there & inside(z + sgn), [chain(w, sgn, b)])
            send_when(there, [across(w, b, y, j) for j in range(1, ny)])

    def hop_tail(w, s):
        for sgn in (1, -1):
            b = zp(-sgn * s)
            there = inside(z - sgn * s)

            @pl.when(there)
            def _():
                for j in range(1, ny):
                    chain_tail(w, sgn, b, j).wait_recv()

            send_when(there & inside(z + sgn), [chain_tail(w, sgn, b, j) for j in range(1, ny)])

    def weight_wait(w):
        locals_[w].wait()
        for k in range(1, nz):
            for j in range(1, ny):
                across(w, zp(k), yp(-j), j).wait_recv()

    acts = ((tok_in, tok), (cot_in, cot))

    def act_start(w):
        src, full = acts[w]
        for k in range(1, nx):
            send(src, rows(full, e, T), tx_s.at[w, k - 1], tx_r.at[w, k - 1], edev(xp(k), c))
        send(src, rows(full, e, T), tc_s.at[w, 0], tc_r.at[w, 0], edev(x, 1 - c))

    def act_forward(w):
        src, full = acts[w]
        started = []
        for k in range(1, nx):
            block = rows(full, xp(-k) * 2 + c, T)
            remote(block, block, tx_s.at[w, k - 1], tx_r.at[w, k - 1],
                   edev(xp(k), c)).wait_recv()
            copy = remote(block, block, tc_s.at[w, k], tc_r.at[w, k], edev(x, 1 - c))
            copy.start()
            started.append(copy)
        return started

    def act_wait(w):
        src, full = acts[w]
        locals_[2 + w].wait()
        for k in range(nx):
            block = rows(full, xp(-k) * 2 + 1 - c, T)
            remote(block, block, tc_s.at[w, k], tc_r.at[w, k], edev(x, 1 - c)).wait_recv()

    weight_start(0)
    act_start(0)
    for i in range(1, ne):
        other = lax.rem(e + i, ne)
        send(gate_in.at[other], rows(gate, e, T), g_s.at[i - 1], g_r.at[i - 1], {"ep": other})
    act_start(1)
    hop(0, 1)
    tok_forwards = act_forward(0)
    tail_start(0)
    hop(0, 2)
    hop_tail(0, 1)
    hop(0, 3)
    weight_start(1)
    hop_tail(0, 2)
    hop_tail(0, 3)
    cot_forwards = act_forward(1)

    act_wait(1)
    for copy in cot_forwards:
        copy.wait_send()
    for i in range(1, ne):
        block = rows(gate, lax.rem(e - i + ne, ne), T)
        remote(block, block, g_s.at[i - 1], g_r.at[i - 1], {"ep": lax.rem(e + i, ne)}).wait_recv()

    @tiles(R, 16)
    def _(r):
        cot[r, :] = (cot[r, :].astype(F32) * gate[r, 0:1]).astype(BF16)

    act_wait(0)
    hop(1, 1)
    tail_start(1)
    weight_wait(0)

    @tiles(FF, 256)
    def _(n):
        slope[:, n] = dot(tok[...], up[:, n], NN)

    hop(1, 2)
    hop_tail(1, 1)

    @tiles(R, 16)
    def _(r):
        value, grad = gelu_parts(slope[r, :])
        hidden[r, :] = value.astype(BF16)
        slope[r, :] = grad

    @tiles(D, 512)
    def _(n):
        dpart[:, n] = dot(hidden[...], cot[:, n], TN).astype(BF16)

    parts = ((upart, ry_u, rz_u, rt_u, ft_u, ug_out), (dpart, ry_d, rz_d, rt_d, ft_d, dg_out))

    flip = lax.div(z, 2)
    near = z + flip * (3 - 2 * z)
    order = [d + flip * (3 - 2 * d) for d in (near * 0 + 3, 2 - 2 * near, 1 + near, near)]

    def give(w, d, yy, j):
        part, ry = parts[w][:2]
        size = parts[w][-1].shape[1]
        return remote(span(part, d * ny + yy, size, 0, size - tail_rows(size)),
                      ry.at[(j - 1) * nz + d], ry_s.at[w, d, j - 1], ry_r.at[w, d, j - 1],
                      fdev(z, yp(j)))

    def run_block(w, way, d, nxt):
        part, ry, rz = parts[w][:3]
        size = parts[w][-1].shape[1]
        return remote(rows(part, d * ny + y, size), rz.at[way, d], rz_s.at[w, d],
                      rz_r.at[w, way, d], fdev(nxt, y))

    def run_tail(w, way, d, nxt, j):
        part, rt = parts[w][0], parts[w][3]
        size = parts[w][-1].shape[1]
        q = tail_rows(size)
        return remote(span(part, d * ny + yp(j), size, size - q, q), rt.at[way, d, j - 1],
                      rt_s.at[w, d, j - 1], rt_r.at[w, way, d, j - 1], fdev(nxt, y))

    def last_tail(w, j):
        part, ft = parts[w][0], parts[w][4]
        size = parts[w][-1].shape[1]
        q = tail_rows(size)
        return remote(span(part, z * ny + yp(j), size, size - q, q), ft.at[j - 1],
                      ft_s.at[w, j - 1], ft_r.at[w, j - 1], fdev(z, yp(j)))

    def part_start(w):
        for d in order:
            for j in range(1, ny):
                copy = give(w, d, yp(j), j)
                copy.start()
                sends.append(copy)

    def add(part, start, count, others):
        @tiles(count, 16)
        def _(r):
            at = pl.ds(pl.multiple_of(start + r.start, 16), 16)
            total = part[at, :].astype(F32)
            for other in others:
                total += other[r, :].astype(F32)
            part[at, :] = total.astype(BF16)

    def pair(w, d):
        part, ry = parts[w][:2]
        size = parts[w][-1].shape[1]
        for j in range(1, ny):
            give(w, d, y, j).wait_recv()
        add(part, (d * ny + y) * size, size - tail_rows(size),
            [ry.at[(j - 1) * nz + d] for j in range(1, ny)])

    def run(w, p):
        part, ry, rz, rt = parts[w][:4]
        size = parts[w][-1].shape[1]
        q = tail_rows(size)
        d = order[p]
        way = jnp.where(d > z, 0, 1)
        sgn = 1 - 2 * way
        nxt = z + sgn
        pair(w, d)

        @pl.when(inside(z - sgn))
        def _():
            run_block(w, way, d, nxt).wait_recv()
            for j in range(1, ny):
                run_tail(w, way, d, nxt, j).wait_recv()
            add(part, (d * ny + y) * size, size, [rz.at[way, d]])
            for j in range(1, ny):
                add(part, (d * ny + yp(j)) * size + size - q, q, [rt.at[way, d, j - 1]])

        copies = [run_block(w, way, d, nxt)]
        copies += [run_tail(w, way, d, nxt, j) for j in range(1, ny)]
        for copy in copies:
            copy.start()
            sends.append(copy)

    def part_last(w):
        part, ry, rz, rt = parts[w][:4]
        size = parts[w][-1].shape[1]
        q = tail_rows(size)
        pair(w, z)
        for way in range(2):
            sgn = 1 - 2 * way

            @pl.when(inside(z - sgn))
            def _():
                for j in range(1, ny):
                    run_tail(w, way, z, zp(1), j).wait_recv()
                    add(part, (z * ny + yp(j)) * size + size - q, q, [rt.at[way, z, j - 1]])

        for j in range(1, ny):
            copy = last_tail(w, j)
            copy.start()
            sends.append(copy)
        for way in range(2):
            sgn = 1 - 2 * way

            @pl.when(inside(z - sgn))
            def _():
                run_block(w, way, z, zp(1)).wait_recv()
                add(part, (z * ny + y) * size, size, [rz.at[way, z]])

    def part_end(w):
        part, ry, rz, rt, ft, out = parts[w]
        size = out.shape[1]
        q = tail_rows(size)
        for j in range(1, ny):
            last_tail(w, j).wait_recv()
        add(part, (z * ny + y) * size + size - q, q, [ft.at[j - 1] for j in range(1, ny)])

        @tiles(size, 16)
        def _(r):
            out[0, r, :] = part[pl.ds(pl.multiple_of(f * size + r.start, 16), 16), :]

    backs = ((cot, rc_m, rx_m, mixed_out), (tok, rc_t, rx_t, tg_out))

    def back_start(w):
        full, rc, rx, out = backs[w]
        for k in range(nx):
            k = (k + 1) % nx
            send(rows(full, xp(k) * 2 + 1 - c, T), rc.at[k], rc_s.at[w, k], rc_r.at[w, k],
                 edev(x, 1 - c))

    def back_pair(w):
        full, rc, rx, out = backs[w]
        for k in range(nx):
            k = (k + 1) % nx
            index = xp(k) * 2 + c
            slot = rc.at[k]
            remote(slot, slot, rc_s.at[w, k], rc_r.at[w, k], edev(x, 1 - c)).wait_recv()

            @tiles(T, 16)
            def _(r):
                at = pl.ds(pl.multiple_of(index * T + r.start, 16), 16)
                full[at, :] = (full[at, :].astype(F32) + rc[k, r, :].astype(F32)).astype(BF16)

            if k:
                send(rows(full, index, T), rx.at[k - 1], rx_s.at[w, k - 1], rx_r.at[w, k - 1],
                     edev(xp(k), c))

    def back_end(w):
        full, rc, rx, out = backs[w]
        for k in range(1, nx):
            slot = rx.at[k - 1]
            remote(slot, slot, rx_s.at[w, k - 1], rx_r.at[w, k - 1], edev(xp(k), c)).wait_recv()

        @tiles(T, 16)
        def _(r):
            at = pl.ds(pl.multiple_of(e * T + r.start, 16), 16)
            total = full[at, :].astype(F32)
            for k in range(1, nx):
                total += rx[k - 1, r, :].astype(F32)
            out[r, :] = total.astype(BF16)

    hop(1, 3)
    hop_tail(1, 2)
    part_start(1)
    hop_tail(1, 3)
    weight_wait(1)

    @tiles(FF, 256)
    def _(n):
        dpre[:, n] = (dot(cot[...], down[n, :], NT) * slope[:, n]).astype(BF16)

    run(1, 0)

    @tiles(D, 384)
    def _(n):
        upart[n, :] = dot(tok[:, n], dpre[...], TN).astype(BF16)

    part_start(0)
    run(1, 1)

    @tiles(D, 512)
    def _(n):
        cot[:, n] = (dot(hidden[...], down[:, n], NN) * gate[:, 0:1]).astype(BF16)

    back_start(0)
    run(1, 2)
    for copy in tok_forwards:
        copy.wait_send()

    @tiles(D, 512)
    def _(n):
        tok[:, n] = dot(dpre[...], up[n, :], NT).astype(BF16)

    back_start(1)
    back_pair(0)
    back_pair(1)
    run(0, 0)
    part_last(1)
    back_end(0)
    run(0, 1)
    back_end(1)
    part_end(1)
    run(0, 2)
    part_last(0)
    part_end(0)
    for copy in sends:
        copy.wait_send()
    for there, copies in guarded:
        @pl.when(there)
        def _():
            for copy in copies:
                copy.wait_send()


def body(tokens, expert_ids, gates, up_weight, down_weight, cotangent):
    nf, ne = lax.axis_size("fsdp"), lax.axis_size("ep")
    nz = 4
    ny, nx = nf // nz, ne // 2
    T, D = tokens.shape
    R = ne * T
    su, FF = up_weight.shape[1:]
    sd = down_weight.shape[1]
    chosen = expert_ids[None] == jnp.arange(ne, dtype=jnp.int32)[:, None, None]
    dense = jnp.sum(jnp.where(chosen, gates[None], 0.0), axis=2)
    gcols = jnp.broadcast_to(dense[:, :, None], (ne, T, LANES))
    qu, qd = (tail_rows(size) for size in (su, sd))
    anyspace = pl.BlockSpec(memory_space=pl.ANY)
    vmem = pl.BlockSpec(memory_space=pltpu.VMEM)
    sem = pltpu.SemaphoreType.DMA
    V = pltpu.VMEM
    scratch = [
        V((D, FF), BF16), V((FF, D), BF16), V((R, D), BF16), V((R, D), BF16),
        V((R, LANES), F32), V((R, FF), F32), V((R, FF), BF16), V((R, FF), BF16),
        V((D, FF), BF16), V((FF, D), BF16),
        V(((ny - 1) * nz, su - qu, FF), BF16), V(((ny - 1) * nz, sd - qd, D), BF16),
        V((2, nz, su, FF), BF16), V((2, nz, sd, D), BF16),
        V((2, nz, ny - 1, qu, FF), BF16), V((2, nz, ny - 1, qd, D), BF16),
        V((ny - 1, qu, FF), BF16), V((ny - 1, qd, D), BF16),
        V((nx, T, D), BF16), V((nx, T, D), BF16),
        V((nx - 1, T, D), BF16), V((nx - 1, T, D), BF16),
        sem((4,)),
        sem((2, 2, nz)), sem((2, 2, nz)),
        sem((2, 2, nz, ny - 1)), sem((2, 2, nz, ny - 1)),
        sem((2, ny - 1)), sem((2, ny - 1)),
        sem((2, nz, ny - 1)), sem((2, nz, ny - 1)),
        sem((2, nx - 1)), sem((2, nx - 1)),
        sem((2, nx)), sem((2, nx)),
        sem((ne - 1,)), sem((ne - 1,)),
        sem((2, nz, ny - 1)), sem((2, nz, ny - 1)),
        sem((2, nz)), sem((2, 2, nz)),
        sem((2, nz, ny - 1)), sem((2, 2, nz, ny - 1)),
        sem((2, ny - 1)), sem((2, ny - 1)),
        sem((2, nx)), sem((2, nx)),
        sem((2, nx - 1)), sem((2, nx - 1)),
    ]
    return pl.pallas_call(
        functools.partial(kernel, nz, ny, nx),
        out_shape=(
            jax.ShapeDtypeStruct((T, D), BF16),
            jax.ShapeDtypeStruct((T, D), BF16),
            jax.ShapeDtypeStruct((1, su, FF), BF16),
            jax.ShapeDtypeStruct((1, sd, D), BF16),
        ),
        in_specs=[anyspace, anyspace, vmem, anyspace, anyspace],
        out_specs=(vmem, vmem, vmem, vmem),
        scratch_shapes=scratch,
        compiler_params=pltpu.CompilerParams(
            collective_id=0, has_side_effects=True, vmem_limit_bytes=64 * 1024 * 1024 - 262144
        ),
    )(tokens, cotangent, gcols, up_weight, down_weight)


def grouped(nz, *refs):
    (tok_in, cot_in, ids_in, gate_in, up_in, down_in,
     mixed_out, tg_out, ug_out, dg_out,
     up, down, tok, cot, upl, perm, uex, gd, gcol, slope, dh, hidden, dpre, upart, dpart,
     rz_u, rz_d, yrecv, rc_m, rc_t, r2_m, r2_t, r3_m, r3_t,
     local_sem, us, ur, ds_s, ds_r, yx_s, yx_r, tx_s, tx_r, ty_s, ty_r, fx_s, fx_r, fy_s, fy_r,
     tc_s, tc_r, g_s, g_r, ru_s, ru_r, rd_s, rd_r, yg_s, yg_r, b1_s, b1_r, b2_s, b2_r, b3_s, b3_r,
     ids, gate, ob, od, ou) = refs
    f = lax.axis_index("fsdp")
    e = lax.axis_index("ep")
    z, y = lax.div(f, 2), lax.rem(f, 2)
    x, c = lax.div(e, 2), lax.rem(e, 2)
    T, D = tok_in.shape
    SU, FF = up_in.shape[1:]
    SD = down_in.shape[1]
    G3 = nz * SD
    H = FF // 2
    R = 8 * T
    N = len(WIDTHS)
    begins = [D * sum(WIDTHS[:n]) // sum(WIDTHS) for n in range(N + 1)]

    def inside(zz):
        return (zz >= 0) & (zz < nz)

    def zp(k):
        return lax.rem(z + k + nz, nz)

    def zdev(zz):
        return {"fsdp": lax.rem(zz + nz, nz) * 2 + y}

    ydev = {"fsdp": z * 2 + 1 - y}
    xdev = {"ep": (1 - x) * 2 + c}
    cdev = {"ep": x * 2 + 1 - c}

    def blk(yy, xx, cc):
        return cc * 4 + yy * 2 + xx

    me = blk(y, x, c)

    def rows(index, size):
        return pl.ds(pl.multiple_of(index * size, size), size)

    def lanes(index, size):
        return pl.ds(pl.multiple_of(index * size, size), size)

    def cols(n):
        return pl.ds(begins[n], begins[n + 1] - begins[n])

    def cols_a(n):
        return pl.ds(begins[n], SPLITS[n])

    def cols_b(n):
        return pl.ds(begins[n] + SPLITS[n], begins[n + 1] - begins[n] - SPLITS[n])

    units = (pl.ds(0, 2 * G3), pl.ds(2 * G3, G3))
    sets = (pl.ds(0, 2), pl.ds(2, 1))

    def remote(src, dst, ss, rs, dev):
        return pltpu.make_async_remote_copy(
            src_ref=src, dst_ref=dst, send_sem=ss, recv_sem=rs,
            device_id=dev, device_id_type=MESH,
        )

    sends = []
    guarded = {}

    def go(copy, keep=sends):
        copy.start()
        keep.append(copy)

    def keep_when(key, there, copy):
        guarded.setdefault(key, (there, []))[1].append(copy)

    def go_when(key, there, copy):
        @pl.when(there)
        def _():
            copy.start()

        keep_when(key, there, copy)

    def taken():
        started = (list(sends), dict(guarded))
        sends.clear()
        guarded.clear()
        return started

    def drain(started):
        for copy in started[0]:
            copy.wait_send()
        for there, copies in started[1].values():
            @pl.when(there)
            def _():
                for copy in copies:
                    copy.wait_send()

    barrier = pltpu.get_barrier_semaphore()
    offsets = [(i // 4, i // 2 % 2, i % 2) for i in range(1, 8)]

    def gdev(dy, dx, dc):
        yy = 1 - y if dy else y
        xx = 1 - x if dx else x
        cc = 1 - c if dc else c
        return yy, xx, cc

    for sgn in (1, -1):
        @pl.when(inside(z + sgn))
        def _():
            pl.semaphore_signal(barrier, inc=1, device_id=zdev(z + sgn), device_id_type=MESH)

    for offset in offsets:
        yy, xx, cc = gdev(*offset)
        pl.semaphore_signal(barrier, inc=1, device_id={"fsdp": z * 2 + yy, "ep": xx * 2 + cc},
                            device_id_type=MESH)
    locals_ = []
    for i, (src, dst) in enumerate((
        (up_in.at[0], upl),
        (down_in, down.at[:, rows(z, SD)]),
        (tok_in, tok.at[rows(me, T)]),
        (cot_in, cot.at[rows(me, T)]),
        (ids_in, ids),
        (gate_in, gate),
    )):
        copy = pltpu.make_async_copy(src, dst, local_sem.at[i])
        copy.start()
        locals_.append(copy)

    near = z + lax.div(z, 2) * (3 - 2 * z)
    pl.semaphore_wait(barrier, len(offsets) + 1 + jnp.minimum(near, 1))

    def permute_up():
        @pl.loop(0, 6 * nz)
        def _(i):
            half, third, zz = lax.div(i, 3 * nz), lax.rem(lax.div(i, nz), 3), lax.rem(i, nz)
            column = lax.broadcasted_iota(jnp.int32, (SD, FF), 1)
            first = SD * (3 * (2 * zz + half) + third)
            unit = lax.broadcasted_iota(jnp.int32, (SD, FF), 0) + first
            perm[rows(i, SD), :] = jnp.where(column == unit, 1.0, 0.0).astype(BF16)

        locals_[0].wait()
        up[rows(f, SU), :] = dot(upl[...], perm[rows(y, H), :], NT).astype(BF16)
        uex[...] = dot(upl[...], perm[rows(1 - y, H), :], NT).astype(BF16)

    def sub(p):
        return y if p % 2 == 0 else 1 - y

    def chain_u(p, sgn, b, own=False):
        block = up.at[rows(2 * b + sub(p), SU), units[p // 2]]
        way = (1 - sgn) // 2
        return remote(block, block, us.at[p, way, b], ur.at[p, way, b], zdev(z + sgn))

    def chain_d(n, sgn, b, own=False):
        block = down.at[:, rows(b, SD), cols(n)]
        way = (1 - sgn) // 2
        return remote(down_in.at[:, :, cols(n)] if own else block, block, ds_s.at[n, way, b], ds_r.at[n, way, b], zdev(z + sgn))

    def own_start(chain, n):
        for sgn in (1, -1):
            go_when((sgn, 0), inside(z + sgn), chain(n, sgn, z, True))

    def hop(chain, n, s):
        for sgn in (1, -1):
            b = zp(-sgn * s)
            there = inside(z - sgn * s)

            @pl.when(there)
            def _():
                chain(n, sgn, b).wait_recv()

            go_when((sgn, s), there & inside(z + sgn), chain(n, sgn, b))

    y_exchange = [remote(uex.at[:, units[g]], up.at[rows(f, SU), units[g]], yx_s.at[g], yx_r.at[g], ydev)
                  for g in range(2)]

    acts = ((tok_in, tok), (cot_in, cot))
    forwards = ([[] for _ in range(N)], [[] for _ in range(N)])

    def act_own(w, n):
        src, full = acts[w]
        there = full.at[rows(me, T), cols(n)]
        go(remote(src.at[:, cols(n)], there, tx_s.at[w, n], tx_r.at[w, n], xdev))
        go(remote(src.at[:, cols(n)], there, ty_s.at[w, n], ty_r.at[w, n], ydev))
        go(remote(src.at[:, cols(n)], there, tc_s.at[w, n, 0], tc_r.at[w, n, 0], cdev))

    def high_rows(b):
        return pl.ds(pl.multiple_of(b * T, 16), SHARE)

    def low_rows(b):
        return pl.ds(pl.multiple_of(b * T + SHARE, 16), T - SHARE)

    def act_fwd(w, n):
        full = acts[w][1]
        keep = forwards[w][n]
        bx, by = blk(y, 1 - x, c), blk(1 - y, x, c)
        here = full.at[rows(bx, T), cols(n)]
        part = full.at[low_rows(bx), cols(n)]
        remote(here, here, tx_s.at[w, n], tx_r.at[w, n], xdev).wait_recv()
        go(remote(part, part, fy_s.at[w, n], fy_r.at[w, n], ydev), keep)
        go(remote(here, here, tc_s.at[w, n, 1], tc_r.at[w, n, 1], cdev), keep)
        here = full.at[rows(by, T), cols(n)]
        part = full.at[high_rows(by), cols(n)]
        remote(here, here, ty_s.at[w, n], ty_r.at[w, n], ydev).wait_recv()
        go(remote(part, part, fx_s.at[w, n], fx_r.at[w, n], xdev), keep)
        go(remote(here, here, tc_s.at[w, n, 2], tc_r.at[w, n, 2], cdev), keep)

    def act_diag(w, n):
        full = acts[w][1]
        bd = blk(1 - y, 1 - x, c)
        low = full.at[high_rows(bd), cols(n)]
        high = full.at[low_rows(bd), cols(n)]
        here = full.at[rows(bd, T), cols(n)]
        remote(low, low, fx_s.at[w, n], fx_r.at[w, n], xdev).wait_recv()
        remote(high, high, fy_s.at[w, n], fy_r.at[w, n], ydev).wait_recv()
        go(remote(here, here, tc_s.at[w, n, 3], tc_r.at[w, n, 3], cdev), forwards[w][n])

    def act_done(w, n):
        full = acts[w][1]
        others = ((y, x), (y, 1 - x), (1 - y, x), (1 - y, 1 - x))
        for k, (yy, xx) in enumerate(others):
            here = full.at[rows(blk(yy, xx, 1 - c), T), cols(n)]
            remote(here, here, tc_s.at[w, n, k], tc_r.at[w, n, k], cdev).wait_recv()

    def gates_start():
        locals_[4].wait()
        locals_[5].wait()
        expert = lax.broadcasted_iota(jnp.int32, (8, T), 0)
        gd[me] = jnp.where(ids[0:1, :] == expert, gate[0:1, :], 0.0) + jnp.where(
            ids[1:2, :] == expert, gate[1:2, :], 0.0)
        for i, offset in enumerate(offsets):
            yy, xx, cc = gdev(*offset)
            go(remote(gd.at[me], gd.at[me], g_s.at[i], g_r.at[i],
                      {"fsdp": z * 2 + yy, "ep": xx * 2 + cc}))

    def gates_done():
        for i, offset in enumerate(offsets):
            yy, xx, cc = gdev(*offset)
            here = gd.at[blk(yy, xx, cc)]
            remote(here, here, g_s.at[i], g_r.at[i],
                   {"fsdp": z * 2 + yy, "ep": xx * 2 + cc}).wait_recv()

        @pl.loop(0, 8)
        def _(b):
            mine = lax.broadcasted_iota(jnp.int32, (8, T), 0) == e
            row = jnp.sum(jnp.where(mine, gd[b], 0.0), axis=0, keepdims=True)
            eye = lax.broadcasted_iota(jnp.int32, (T, T), 0) == lax.broadcasted_iota(
                jnp.int32, (T, T), 1)
            column = jnp.sum(jnp.where(eye, row, 0.0), axis=1, keepdims=True)
            gcol[rows(b, T), :] = jnp.broadcast_to(column, (T, LANES))

    flip = lax.div(z, 2)
    near = z + flip * (3 - 2 * z)
    order = [d + flip * (3 - 2 * d) for d in (near * 0 + 3, 2 - 2 * near, 1 + near, near)]
    is_end = near == 0

    def pre_step(g, s):
        plane = order[3 - s]
        u = units[g]
        if g == 0 and s == 0:
            locals_[2].wait()
            locals_[3].wait()

        @tiles(R, 256)
        def _(r):
            part = dot(tok[r, lanes(plane, 2 * SU)], up[rows(plane, 2 * SU), u], NN)
            if s == 0:
                slope[r, u] = part
            elif s < nz - 1:
                slope[r, u] += part
            else:
                value, grad = gelu_parts(slope[r, u] + part)
                hidden[r, u] = (value * gcol[r, 0:1]).astype(BF16)
                slope[r, u] = grad * gcol[r, 0:1]

    def tokens_sent():
        for copies in forwards[0]:
            for copy in copies:
                copy.wait_send()

    def chunk_tiles(n):
        size = TILE

        def run(fn):
            @pl.loop(0, (begins[n + 1] - begins[n]) // size)
            def _(i):
                fn(pl.ds(pl.multiple_of(begins[n] + i * size, size), size))

        return run

    def down_part(g, n):
        @chunk_tiles(n)
        def _(t):
            part = dot(hidden[:, units[g]], cot[:, t], TN).astype(BF16)
            dpart[sets[g], :, t] = part.reshape(2 - g, G3, TILE)

    def back_hidden(n):
        if n == 0:
            locals_[1].wait()

        @tiles(R, 256)
        def _(r):
            part = dot(cot[r, cols(n)], down[:, :, cols(n)].reshape(H, begins[n + 1] - begins[n]), NT)
            if n == 0:
                dh[r, :] = part
            elif n < N - 1:
                dh[r, :] += part
            else:
                dpre[r, :] = ((dh[r, :] + part) * slope[r, :]).astype(BF16)

    def mixed_part(n):
        for copy in forwards[1][n]:
            copy.wait_send()

        @chunk_tiles(n)
        def _(t):
            @tiles(R, ROWS)
            def _(r):
                cot[r, t] = dot(hidden[r, :], down[:, :, t].reshape(H, TILE), NN).astype(BF16)

    def token_part(n):
        @chunk_tiles(n)
        def _(t):
            @tiles(R, ROWS)
            def _(r):
                tok[r, t] = dot(dpre[r, :], up[t, :], NT).astype(BF16)

    def up_part(q, pos):
        at = rows(2 * order[pos] + (1 - sub(q)), SU)
        upart[at, :] = dot(tok[:, at], dpre[...], TN).astype(BF16)

    def send_down(m, d, way, nxt):
        g, n = m // N, m % N
        return remote(dpart.at[sets[g], rows(d, SD), cols(n)], rz_d.at[way, d, sets[g], :, cols(n)],
                      rd_s.at[m, d], rd_r.at[m, way, d], zdev(nxt))

    def send_up(q, d, way, nxt):
        return remote(upart.at[rows(2 * d + (1 - sub(q)), SU)], rz_u.at[q, way, d],
                      ru_s.at[q, d], ru_r.at[q, way, d], zdev(nxt))

    def add_down(m, d, way):
        g, n = m // N, m % N

        @tiles(SD, 16)
        def _(r):
            at = pl.ds(pl.multiple_of(d * SD + r.start, 16), 16)
            dpart[sets[g], at, cols(n)] = (dpart[sets[g], at, cols(n)].astype(F32)
                                           + rz_d[way, d, sets[g], r, cols(n)].astype(F32)).astype(BF16)

    def add_up(q, d, way):
        @tiles(SU, 32)
        def _(r):
            at = pl.ds(pl.multiple_of((2 * d + (1 - sub(q))) * SU + r.start, 32), 32)
            upart[at, :] = (upart[at, :].astype(F32)
                            + rz_u[q, way, d, r, :].astype(F32)).astype(BF16)

    downs, ups = (send_down, add_down), (send_up, add_up)

    def course(pos):
        d = order[pos]
        way = jnp.where(d > z, 0, 1)
        return d, way, z + 1 - 2 * way

    def begin(kind, n, pos):
        d, way, nxt = course(pos)
        go_when("end", is_end, kind[0](n, d, way, nxt))

    def middle(kind, n, pos):
        d, way, nxt = course(pos)
        copy = kind[0](n, d, way, nxt)

        @pl.when(jnp.logical_not(is_end))
        def _():
            copy.wait_recv()
            kind[1](n, d, way)
            copy.start()

        keep_when("middle", jnp.logical_not(is_end), copy)

    def last(kind, n):
        for way in range(2):
            @pl.when(inside(z - 1 + 2 * way))
            def _():
                kind[0](n, z, way, zp(1)).wait_recv()
                kind[1](n, z, way)

    results = []

    def result(src, dst, done):
        copy = pltpu.make_async_copy(src, dst, done)
        copy.start()
        results.append(copy)

    def down_end(m):
        g, n = m // N, m % N
        last(downs, m)
        result(dpart.at[sets[g], rows(z, SD), cols(n)], dg_out.at[sets[g], :, cols(n)], od.at[m])

    other_up = upart.at[rows(2 * z + 1 - y, SU)]
    y_return = remote(other_up, yrecv, yg_s.at[0], yg_r.at[0], ydev)

    def up_end():
        last(ups, 1)
        y_return.wait_recv()
        upl[...] = (dot(upart[rows(f, SU), :], perm[rows(y, H), :], NN)
                     + dot(yrecv[...], perm[rows(1 - y, H), :], NN)).astype(BF16)
        result(upl, ug_out.at[0], ou.at[0])

    backs = ((cot, rc_m, r2_m, r3_m, mixed_out), (tok, rc_t, r2_t, r3_t, tg_out))
    G = 4 * T

    def back1(w, n):
        full, rc = backs[w][:2]
        go(remote(full.at[rows(1 - c, G), cols(n)], rc.at[:, cols(n)],
                  b1_s.at[w, n], b1_r.at[w, n], cdev))

    def back2(w, n):
        full, rc, r2 = backs[w][:3]
        here = rc.at[:, cols(n)]
        remote(here, here, b1_s.at[w, n], b1_r.at[w, n], cdev).wait_recv()

        @tiles(G, 16)
        def _(r):
            at = pl.ds(pl.multiple_of(c * G + r.start, 16), 16)
            full[at, cols(n)] = (full[at, cols(n)].astype(F32)
                                 + rc[r, cols(n)].astype(F32)).astype(BF16)

        for yy in range(2):
            go(remote(full.at[rows(blk(yy, 1 - x, c), T), cols_a(n)],
                      r2.at[pl.ds(yy * T, T), cols_a(n)],
                      b2_s.at[w, n, yy], b2_r.at[w, n, yy], xdev))
        go(remote(full.at[rows(c * 2 + 1 - y, 2 * T), cols_b(n)], r2.at[:, cols_b(n)],
                  b2_s.at[w, n, 2], b2_r.at[w, n, 2], ydev))

    def back3(w, n):
        full, rc, r2, r3 = backs[w][:4]
        for yy in range(2):
            here = r2.at[pl.ds(yy * T, T), cols_a(n)]
            remote(here, here, b2_s.at[w, n, yy], b2_r.at[w, n, yy], xdev).wait_recv()
        here = r2.at[:, cols_b(n)]
        remote(here, here, b2_s.at[w, n, 2], b2_r.at[w, n, 2], ydev).wait_recv()
        ba, bb = blk(1 - y, x, c), blk(y, 1 - x, c)

        @tiles(T, 16)
        def _(r):
            at = pl.ds(pl.multiple_of(ba * T + r.start, 16), 16)
            there = pl.ds(pl.multiple_of((1 - y) * T + r.start, 16), 16)
            full[at, cols_a(n)] = (full[at, cols_a(n)].astype(F32)
                                   + r2[there, cols_a(n)].astype(F32)).astype(BF16)
            at = pl.ds(pl.multiple_of(bb * T + r.start, 16), 16)
            there = pl.ds(pl.multiple_of((1 - x) * T + r.start, 16), 16)
            full[at, cols_b(n)] = (full[at, cols_b(n)].astype(F32)
                                   + r2[there, cols_b(n)].astype(F32)).astype(BF16)

        go(remote(full.at[rows(ba, T), cols_a(n)], r3.at[:, cols_a(n)],
                  b3_s.at[w, n, 0], b3_r.at[w, n, 0], ydev))
        go(remote(full.at[rows(bb, T), cols_b(n)], r3.at[:, cols_b(n)],
                  b3_s.at[w, n, 1], b3_r.at[w, n, 1], xdev))

    def back4(w, n):
        full, rc, r2, r3, out = backs[w]
        for k, (span, dev) in enumerate(((cols_a(n), ydev), (cols_b(n), xdev))):
            here = r3.at[:, span]
            remote(here, here, b3_s.at[w, n, k], b3_r.at[w, n, k], dev).wait_recv()

        @tiles(T, 16)
        def _(r):
            at = pl.ds(pl.multiple_of(me * T + r.start, 16), 16)
            for span, lane in ((cols_a(n), y), (cols_b(n), x)):
                there = pl.ds(pl.multiple_of(lane * T + r.start, 16), 16)
                full[at, span] = (full[at, span].astype(F32) + r2[there, span].astype(F32)
                                + r3[r, span].astype(F32)).astype(BF16)

        result(full.at[rows(me, T), cols(n)], out.at[:, cols(n)], ob.at[w, n])

    own_start(chain_d, 1)
    act_own(0, 2)
    own_start(chain_d, 0)
    permute_up()
    go(y_exchange[0])
    own_start(chain_u, 2)
    own_start(chain_u, 0)
    act_own(0, 1)
    go(y_exchange[1])
    act_own(0, 0)
    y_exchange[0].wait_recv()
    act_own(0, 3)
    gates_start()
    own_start(chain_u, 1)
    hop(chain_u, 2, 1)
    act_fwd(0, 2)
    y_exchange[1].wait_recv()
    own_start(chain_u, 3)
    act_fwd(0, 1)
    act_own(1, 3)
    hop(chain_u, 1, 1)
    hop(chain_u, 0, 1)
    act_fwd(0, 3)
    hop(chain_u, 1, 2)
    act_fwd(0, 0)
    gates_done()
    act_diag(0, 2)
    act_fwd(1, 3)
    hop(chain_u, 3, 1)
    hop(chain_u, 0, 2)
    act_own(1, 1)
    hop(chain_u, 2, 2)
    act_own(1, 0)
    hop(chain_u, 1, 3)
    act_diag(0, 1)
    act_diag(0, 0)
    act_diag(0, 3)
    hop(chain_u, 3, 2)
    hop(chain_d, 0, 1)
    act_done(0, 2)
    own_start(chain_d, 2)
    act_done(0, 0)
    own_start(chain_d, 3)
    act_diag(1, 3)
    act_done(0, 1)
    act_done(0, 3)
    pre_step(0, 0)
    pre_step(0, 1)
    pre_step(0, 2)
    act_done(1, 3)
    act_fwd(1, 1)
    hop(chain_u, 0, 3)
    pre_step(0, 3)
    down_part(0, 3)
    begin(downs, 0 * N + 3, 1)
    begin(downs, 0 * N + 3, 2)
    hop(chain_u, 3, 3)
    act_fwd(1, 0)
    pre_step(1, 0)
    pre_step(1, 1)
    act_diag(1, 1)
    act_own(1, 2)
    hop(chain_u, 2, 3)
    begin(downs, 0 * N + 3, 0)
    hop(chain_d, 0, 2)
    act_done(1, 1)
    down_part(0, 1)
    hop(chain_d, 1, 1)
    begin(downs, 0 * N + 1, 2)
    pre_step(1, 2)
    act_diag(1, 0)
    pre_step(1, 3)
    down_part(1, 1)
    act_done(1, 0)
    down_part(1, 0)
    begin(downs, 0 * N + 1, 0)
    begin(downs, 1 * N + 0, 0)
    begin(downs, 1 * N + 0, 1)
    begin(downs, 1 * N + 1, 1)
    down_part(0, 0)
    act_fwd(1, 2)
    begin(downs, 1 * N + 1, 2)
    begin(downs, 1 * N + 1, 0)
    begin(downs, 0 * N + 1, 1)
    begin(downs, 0 * N + 0, 0)
    hop(chain_d, 0, 3)
    back_hidden(0)
    mixed_part(0)
    back1(0, 0)
    hop(chain_d, 1, 2)
    down_part(1, 3)
    hop(chain_d, 2, 1)
    begin(downs, 1 * N + 3, 0)
    act_diag(1, 2)
    begin(downs, 1 * N + 3, 2)
    begin(downs, 0 * N + 0, 1)
    back2(0, 0)
    act_done(1, 2)
    hop(chain_d, 1, 3)
    back_hidden(1)
    mixed_part(1)
    back1(0, 1)
    begin(downs, 1 * N + 3, 1)
    middle(downs, 0 * N + 3, 2)
    hop(chain_d, 2, 2)
    down_part(1, 2)
    hop(chain_d, 3, 1)
    middle(downs, 0 * N + 1, 0)
    begin(downs, 1 * N + 2, 0)
    down_part(0, 2)
    begin(downs, 0 * N + 2, 2)
    begin(downs, 0 * N + 2, 1)
    back2(0, 1)
    hop(chain_d, 2, 3)
    middle(downs, 0 * N + 0, 0)
    back_hidden(2)
    mixed_part(2)
    back1(0, 2)
    begin(downs, 0 * N + 2, 0)
    hop(chain_d, 3, 2)
    middle(downs, 0 * N + 3, 0)
    back3(0, 0)
    begin(downs, 1 * N + 2, 2)
    middle(downs, 1 * N + 1, 0)
    begin(downs, 1 * N + 0, 2)
    middle(downs, 1 * N + 1, 2)
    begin(downs, 1 * N + 2, 1)
    middle(downs, 1 * N + 3, 2)
    back2(0, 2)
    hop(chain_d, 3, 3)
    early = taken()
    back_hidden(3)
    up_part(0, 0)
    middle(downs, 0 * N + 1, 2)
    begin(ups, 0, 0)
    mixed_part(3)
    back1(0, 3)
    back3(0, 1)
    up_part(1, 2)
    middle(downs, 1 * N + 0, 0)
    up_part(0, 3)
    up_part(0, 2)
    up_part(0, 1)
    back2(0, 3)
    up_part(1, 1)
    up_part(1, 3)
    middle(downs, 0 * N + 3, 1)
    up_part(1, 0)
    middle(downs, 1 * N + 2, 0)
    middle(downs, 0 * N + 2, 2)
    middle(downs, 1 * N + 3, 0)
    tokens_sent()
    begin(ups, 0, 1)
    token_part(3)
    back1(1, 3)
    middle(downs, 0 * N + 2, 0)
    back3(0, 2)
    middle(downs, 1 * N + 2, 1)
    token_part(1)
    back2(1, 3)
    middle(ups, 0, 0)
    middle(downs, 0 * N + 0, 1)
    token_part(0)
    back1(1, 0)
    middle(downs, 1 * N + 0, 1)
    begin(ups, 1, 0)
    back4(0, 0)
    begin(ups, 0, 2)
    back3(0, 3)
    middle(downs, 1 * N + 2, 2)
    back1(1, 1)
    middle(downs, 1 * N + 1, 1)
    middle(downs, 1 * N + 0, 2)
    token_part(2)
    back2(1, 0)
    down_end(1 * N + 1)
    middle(ups, 0, 2)
    back1(1, 2)
    middle(downs, 1 * N + 3, 1)
    begin(ups, 1, 1)
    back2(1, 1)
    back4(0, 1)
    back3(1, 3)
    middle(downs, 0 * N + 1, 1)
    begin(ups, 1, 2)
    back4(0, 3)
    middle(ups, 0, 1)
    back2(1, 2)
    back3(1, 0)
    down_end(1 * N + 3)
    begin(downs, 0 * N + 0, 2)
    middle(ups, 1, 0)
    down_end(0 * N + 1)
    middle(downs, 0 * N + 0, 2)
    last(ups, 0)
    down_end(1 * N + 2)
    middle(downs, 0 * N + 2, 1)
    go(y_return)
    drain(early)
    later = taken()
    back3(1, 1)
    down_end(0 * N + 2)
    back4(0, 2)
    down_end(1 * N + 0)
    middle(ups, 1, 1)
    middle(ups, 1, 2)
    back4(1, 3)
    back3(1, 2)
    down_end(0 * N + 3)
    back4(1, 0)
    back4(1, 1)
    drain(later)
    up_end()
    down_end(0 * N + 0)
    back4(1, 2)
    drain(taken())
    for copy in results:
        copy.wait()


def settle(*refs):
    sources, results, held, arrived, done = refs[:4], refs[4:8], refs[8:12], refs[12], refs[13]
    ins = [pltpu.make_async_copy(a, b, arrived.at[i]) for i, (a, b) in enumerate(zip(sources, held))]
    outs = [pltpu.make_async_copy(a, b, done.at[i]) for i, (a, b) in enumerate(zip(held, results))]
    for copy in ins:
        copy.start()
    for arrival, copy in zip(ins, outs):
        arrival.wait()
        copy.start()
    for copy in outs:
        copy.wait()


def grouped_body(nz, tokens, expert_ids, gates, up_weight, down_weight, cotangent):
    T, D = tokens.shape
    R = 8 * T
    SU, FF = up_weight.shape[1:]
    SD = down_weight.shape[1] // 3
    H = FF // 2
    N = len(WIDTHS)
    anyspace = pl.BlockSpec(memory_space=pl.ANY)
    sem = pltpu.SemaphoreType.DMA
    V = pltpu.VMEM

    def pair(*shape):
        return [sem(shape), sem(shape)]

    scratch = [
        V((D, H), BF16), V((3, nz * SD, D), BF16), V((R, D), BF16), V((R, D), BF16),
        V((SU, FF), BF16), V((FF, FF), BF16), V((SU, H), BF16),
        V((8, 8, T), F32), V((R, LANES), F32), V((R, H), F32), V((R, H), F32),
        V((R, H), BF16), V((R, H), BF16), V((D, H), BF16), V((3, nz * SD, D), BF16),
        V((2, 2, nz, SU, H), BF16), V((2, nz, 3, SD, D), BF16), V((SU, H), BF16),
        V((4 * T, D), BF16), V((4 * T, D), BF16), V((2 * T, D), BF16), V((2 * T, D), BF16),
        V((T, D), BF16), V((T, D), BF16),
        sem((6,)),
        *pair(4, 2, nz), *pair(N, 2, nz), *pair(2),
        *pair(2, N), *pair(2, N), *pair(2, N), *pair(2, N), *pair(2, N, 4), *pair(7),
        sem((2, nz)), sem((2, 2, nz)), sem((2 * N, nz)), sem((2 * N, 2, nz)), *pair(1),
        *pair(2, N), *pair(2, N, 3), *pair(2, N, 2),
        V((2, T), jnp.int32), V((2, T), F32), sem((2, N)), sem((2 * N,)), sem((1,)),
    ]
    outs = pl.pallas_call(
        functools.partial(grouped, nz),
        out_shape=(
            jax.ShapeDtypeStruct((T, D), BF16),
            jax.ShapeDtypeStruct((T, D), BF16),
            jax.ShapeDtypeStruct((1, SU, FF), BF16),
            jax.ShapeDtypeStruct((3, SD, D), BF16),
        ),
        in_specs=[anyspace] * 6,
        out_specs=(anyspace,) * 4,
        scratch_shapes=scratch,
        compiler_params=pltpu.CompilerParams(
            collective_id=0, has_side_effects=True, vmem_limit_bytes=64 * 1024 * 1024 - 262144
        ),
    )(tokens, cotangent, expert_ids.T, gates.T, up_weight, down_weight.reshape(3, SD, D))
    outs = pl.pallas_call(
        settle,
        out_shape=tuple(jax.ShapeDtypeStruct(out.shape, out.dtype) for out in outs),
        in_specs=[anyspace] * 4,
        out_specs=(anyspace,) * 4,
        scratch_shapes=[V(out.shape, BF16) for out in outs] + [sem((4,)), sem((4,))],
    )(*outs)
    return *outs[:3], outs[3].reshape(down_weight.shape)


def solution(mesh):
    placed = (
        P(("fsdp", "ep"), None),
        P(("fsdp", "ep"), None),
        P(("fsdp", "ep"), None),
        P("ep", "fsdp", None),
        P("ep", "fsdp", None),
        P(("fsdp", "ep"), None),
    )
    nf, ne = mesh.shape["fsdp"], mesh.shape["ep"]
    run = functools.partial(grouped_body, 4) if (nf, ne) == (8, 4) else body
    return jax.shard_map(
        run,
        mesh=mesh,
        in_specs=placed,
        out_specs=(
            P(("fsdp", "ep"), None),
            P(("fsdp", "ep"), None),
            P("ep", "fsdp", None),
            P("ep", "fsdp", None),
        ),
        check_vma=False,
    )
```

```python
import functools

import jax
import jax.numpy as jnp
from jax import lax
from jax.experimental import pallas as pl
from jax.experimental.pallas import tpu as pltpu
from jax.sharding import PartitionSpec as P

F32 = jnp.float32
BF16 = jnp.bfloat16
MESH = pl.DeviceIdType.MESH
LANES = 128
WIDTHS = (768, 768, 768, 768)
SPLITS = (512, 512, 512, 512)
SHARE = 80
TILE = 768
ROWS = 256


def gelu_parts(pre):
    root = 0.7978845608028654
    inner = root * (pre + 0.044715 * pre * pre * pre)
    tanh_val = jnp.tanh(inner)
    value = 0.5 * pre * (1.0 + tanh_val)
    slope = 0.5 * (1.0 + tanh_val) + 0.5 * pre * (1.0 - tanh_val * tanh_val) * root * (
        1.0 + 3.0 * 0.044715 * pre * pre
    )
    return (value, slope)


def dot(left, right, dims):
    return lax.dot_general(left, right, (dims, ((), ())), preferred_element_type=F32)


NN = ((1,), (0,))
NT = ((1,), (1,))
TN = ((0,), (0,))


def tail_rows(size):
    return max(16, size // 6 // 16 * 16)


def tiles(count, size):
    def run(fn):
        @pl.loop(0, count // size)
        def _(i):
            fn(pl.ds(pl.multiple_of(i * size, size), size))

    return run


def kernel(
    nz, ny, nx,
    tok_in, cot_in, gate_in, up_in, down_in,
    mixed_out, tg_out, ug_out, dg_out,
    up, down, tok, cot, gate, slope, hidden, dpre, upart, dpart,
    ry_u, ry_d, rz_u, rz_d, rt_u, rt_d, ft_u, ft_d, rc_m, rc_t, rx_m, rx_t,
    local_sem, wz_s, wz_r, wt_s, wt_r, wo_s, wo_r, wy_s, wy_r,
    tx_s, tx_r, tc_s, tc_r, g_s, g_r,
    ry_s, ry_r, rz_s, rz_r, rt_s, rt_r, ft_s, ft_r, rc_s, rc_r, rx_s, rx_r,
):
    ne = 2 * nx
    f = lax.axis_index("fsdp")
    e = lax.axis_index("ep")
    z, y = lax.div(f, ny), lax.rem(f, ny)
    x, c = lax.div(e, 2), lax.rem(e, 2)
    T = tok_in.shape[0]
    D = tok_in.shape[1]
    R = ne * T
    FF = up.shape[1]

    def zp(k):
        return lax.rem(z + k + nz, nz)

    def inside(zz):
        return (zz >= 0) & (zz < nz)

    def yp(j):
        return lax.rem(y + j + ny, ny)

    def xp(k):
        return lax.rem(x + k + nx, nx)

    def fdev(zz, yy):
        return {"fsdp": zz * ny + yy}

    def edev(xx, cc):
        return {"ep": xx * 2 + cc}

    def rows(ref, index, size):
        return ref.at[pl.ds(pl.multiple_of(index * size, size), size)]

    def remote(src, dst, ss, rs, dev):
        return pltpu.make_async_remote_copy(
            src_ref=src, dst_ref=dst, send_sem=ss, recv_sem=rs,
            device_id=dev, device_id_type=MESH,
        )

    sends = []
    guarded = []

    def send_when(there, copies):
        @pl.when(there)
        def _():
            for copy in copies:
                copy.start()

        guarded.append((there, copies))


    def send(src, dst, ss, rs, dev):
        copy = remote(src, dst, ss, rs, dev)
        copy.start()
        sends.append(copy)
        return copy

    barrier = pltpu.get_barrier_semaphore()
    peers = [fdev(zp(k), y) for k in range(1, nz)]
    peers += [fdev(z, yp(j)) for j in range(1, ny)]
    peers += [{"ep": lax.rem(e + i, ne)} for i in range(1, ne)]
    for dev in peers:
        pl.semaphore_signal(barrier, inc=1, device_id=dev, device_id_type=MESH)
    locals_ = []
    for i, (src, dst) in enumerate((
        (up_in.at[0], rows(up, f, up_in.shape[1])),
        (down_in.at[0], rows(down, f, down_in.shape[1])),
        (tok_in, rows(tok, e, T)),
        (cot_in, rows(cot, e, T)),
    )):
        copy = pltpu.make_async_copy(src, dst, local_sem.at[i])
        copy.start()
        locals_.append(copy)
    rows(gate, e, T)[...] = gate_in[e]
    pl.semaphore_wait(barrier, len(peers))

    weights = ((up_in, up), (down_in, down))

    def span(ref, index, size, begin, count):
        return ref.at[pl.ds(pl.multiple_of(index * size + begin, 16), count)]

    def chain(w, sgn, b, src=None):
        full = weights[w][1]
        size = weights[w][0].shape[1]
        block = rows(full, b * ny + y, size)
        way = (1 - sgn) // 2
        return remote(block if src is None else src, block, wz_s.at[w, way, b],
                      wz_r.at[w, way, b], fdev(zp(sgn), y))

    def chain_tail(w, sgn, b, j):
        full = weights[w][1]
        size = weights[w][0].shape[1]
        q = tail_rows(size)
        block = span(full, b * ny + yp(-j), size, size - q, q)
        way = (1 - sgn) // 2
        return remote(block, block, wt_s.at[w, way, b, j - 1], wt_r.at[w, way, b, j - 1],
                      fdev(zp(sgn), y))

    def across(w, b, yy, j):
        full = weights[w][1]
        size = weights[w][0].shape[1]
        block = span(full, b * ny + yy, size, 0, size - tail_rows(size))
        return remote(block, block, wy_s.at[w, b, j - 1], wy_r.at[w, b, j - 1], fdev(z, yp(j)))

    def own_across(w, yy, j, src=None):
        full = weights[w][1]
        size = weights[w][0].shape[1]
        block = rows(full, z * ny + yy, size)
        return remote(block if src is None else src, block, wo_s.at[w, j - 1], wo_r.at[w, j - 1],
                      fdev(z, yp(j)))

    def weight_start(w):
        src = weights[w][0].at[0]
        for sgn in (1, -1):
            send_when(inside(z + sgn), [chain(w, sgn, z, src)])
        for j in range(1, ny):
            copy = own_across(w, y, j, src)
            copy.start()
            sends.append(copy)

    def tail_start(w):
        for j in range(1, ny):
            own_across(w, yp(-j), j).wait_recv()
        for sgn in (1, -1):
            send_when(inside(z + sgn), [chain_tail(w, sgn, z, j) for j in range(1, ny)])

    def hop(w, s):
        for sgn in (1, -1):
            b = zp(-sgn * s)
            there = inside(z - sgn * s)

            @pl.when(there)
            def _():
                chain(w, sgn, b).wait_recv()

            send_when(there & inside(z + sgn), [chain(w, sgn, b)])
            send_when(there, [across(w, b, y, j) for j in range(1, ny)])

    def hop_tail(w, s):
        for sgn in (1, -1):
            b = zp(-sgn * s)
            there = inside(z - sgn * s)

            @pl.when(there)
            def _():
                for j in range(1, ny):
                    chain_tail(w, sgn, b, j).wait_recv()

            send_when(there & inside(z + sgn), [chain_tail(w, sgn, b, j) for j in range(1, ny)])

    def weight_wait(w):
        locals_[w].wait()
        for k in range(1, nz):
            for j in range(1, ny):
                across(w, zp(k), yp(-j), j).wait_recv()

    acts = ((tok_in, tok), (cot_in, cot))

    def act_start(w):
        src, full = acts[w]
        for k in range(1, nx):
            send(src, rows(full, e, T), tx_s.at[w, k - 1], tx_r.at[w, k - 1], edev(xp(k), c))
        send(src, rows(full, e, T), tc_s.at[w, 0], tc_r.at[w, 0], edev(x, 1 - c))

    def act_forward(w):
        src, full = acts[w]
        started = []
        for k in range(1, nx):
            block = rows(full, xp(-k) * 2 + c, T)
            remote(block, block, tx_s.at[w, k - 1], tx_r.at[w, k - 1],
                   edev(xp(k), c)).wait_recv()
            copy = remote(block, block, tc_s.at[w, k], tc_r.at[w, k], edev(x, 1 - c))
            copy.start()
            started.append(copy)
        return started

    def act_wait(w):
        src, full = acts[w]
        locals_[2 + w].wait()
        for k in range(nx):
            block = rows(full, xp(-k) * 2 + 1 - c, T)
            remote(block, block, tc_s.at[w, k], tc_r.at[w, k], edev(x, 1 - c)).wait_recv()

    weight_start(0)
    act_start(0)
    for i in range(1, ne):
        other = lax.rem(e + i, ne)
        send(gate_in.at[other], rows(gate, e, T), g_s.at[i - 1], g_r.at[i - 1], {"ep": other})
    act_start(1)
    hop(0, 1)
    tok_forwards = act_forward(0)
    tail_start(0)
    hop(0, 2)
    hop_tail(0, 1)
    hop(0, 3)
    weight_start(1)
    hop_tail(0, 2)
    hop_tail(0, 3)
    cot_forwards = act_forward(1)

    act_wait(1)
    for copy in cot_forwards:
        copy.wait_send()
    for i in range(1, ne):
        block = rows(gate, lax.rem(e - i + ne, ne), T)
        remote(block, block, g_s.at[i - 1], g_r.at[i - 1], {"ep": lax.rem(e + i, ne)}).wait_recv()

    @tiles(R, 16)
    def _(r):
        cot[r, :] = (cot[r, :].astype(F32) * gate[r, 0:1]).astype(BF16)

    act_wait(0)
    hop(1, 1)
    tail_start(1)
    weight_wait(0)

    @tiles(FF, 256)
    def _(n):
        slope[:, n] = dot(tok[...], up[:, n], NN)

    hop(1, 2)
    hop_tail(1, 1)

    @tiles(R, 16)
    def _(r):
        value, grad = gelu_parts(slope[r, :])
        hidden[r, :] = value.astype(BF16)
        slope[r, :] = grad

    @tiles(D, 512)
    def _(n):
        dpart[:, n] = dot(hidden[...], cot[:, n], TN).astype(BF16)

    parts = ((upart, ry_u, rz_u, rt_u, ft_u, ug_out), (dpart, ry_d, rz_d, rt_d, ft_d, dg_out))

    flip = lax.div(z, 2)
    near = z + flip * (3 - 2 * z)
    order = [d + flip * (3 - 2 * d) for d in (near * 0 + 3, 2 - 2 * near, 1 + near, near)]

    def give(w, d, yy, j):
        part, ry = parts[w][:2]
        size = parts[w][-1].shape[1]
        return remote(span(part, d * ny + yy, size, 0, size - tail_rows(size)),
                      ry.at[(j - 1) * nz + d], ry_s.at[w, d, j - 1], ry_r.at[w, d, j - 1],
                      fdev(z, yp(j)))

    def run_block(w, way, d, nxt):
        part, ry, rz = parts[w][:3]
        size = parts[w][-1].shape[1]
        return remote(rows(part, d * ny + y, size), rz.at[way, d], rz_s.at[w, d],
                      rz_r.at[w, way, d], fdev(nxt, y))

    def run_tail(w, way, d, nxt, j):
        part, rt = parts[w][0], parts[w][3]
        size = parts[w][-1].shape[1]
        q = tail_rows(size)
        return remote(span(part, d * ny + yp(j), size, size - q, q), rt.at[way, d, j - 1],
                      rt_s.at[w, d, j - 1], rt_r.at[w, way, d, j - 1], fdev(nxt, y))

    def last_tail(w, j):
        part, ft = parts[w][0], parts[w][4]
        size = parts[w][-1].shape[1]
        q = tail_rows(size)
        return remote(span(part, z * ny + yp(j), size, size - q, q), ft.at[j - 1],
                      ft_s.at[w, j - 1], ft_r.at[w, j - 1], fdev(z, yp(j)))

    def part_start(w):
        for d in order:
            for j in range(1, ny):
                copy = give(w, d, yp(j), j)
                copy.start()
                sends.append(copy)

    def add(part, start, count, others):
        @tiles(count, 16)
        def _(r):
            at = pl.ds(pl.multiple_of(start + r.start, 16), 16)
            total = part[at, :].astype(F32)
            for other in others:
                total += other[r, :].astype(F32)
            part[at, :] = total.astype(BF16)

    def pair(w, d):
        part, ry = parts[w][:2]
        size = parts[w][-1].shape[1]
        for j in range(1, ny):
            give(w, d, y, j).wait_recv()
        add(part, (d * ny + y) * size, size - tail_rows(size),
            [ry.at[(j - 1) * nz + d] for j in range(1, ny)])

    def run(w, p):
        part, ry, rz, rt = parts[w][:4]
        size = parts[w][-1].shape[1]
        q = tail_rows(size)
        d = order[p]
        way = jnp.where(d > z, 0, 1)
        sgn = 1 - 2 * way
        nxt = z + sgn
        pair(w, d)

        @pl.when(inside(z - sgn))
        def _():
            run_block(w, way, d, nxt).wait_recv()
            for j in range(1, ny):
                run_tail(w, way, d, nxt, j).wait_recv()
            add(part, (d * ny + y) * size, size, [rz.at[way, d]])
            for j in range(1, ny):
                add(part, (d * ny + yp(j)) * size + size - q, q, [rt.at[way, d, j - 1]])

        copies = [run_block(w, way, d, nxt)]
        copies += [run_tail(w, way, d, nxt, j) for j in range(1, ny)]
        for copy in copies:
            copy.start()
            sends.append(copy)

    def part_last(w):
        part, ry, rz, rt = parts[w][:4]
        size = parts[w][-1].shape[1]
        q = tail_rows(size)
        pair(w, z)
        for way in range(2):
            sgn = 1 - 2 * way

            @pl.when(inside(z - sgn))
            def _():
                for j in range(1, ny):
                    run_tail(w, way, z, zp(1), j).wait_recv()
                    add(part, (z * ny + yp(j)) * size + size - q, q, [rt.at[way, z, j - 1]])

        for j in range(1, ny):
            copy = last_tail(w, j)
            copy.start()
            sends.append(copy)
        for way in range(2):
            sgn = 1 - 2 * way

            @pl.when(inside(z - sgn))
            def _():
                run_block(w, way, z, zp(1)).wait_recv()
                add(part, (z * ny + y) * size, size, [rz.at[way, z]])

    def part_end(w):
        part, ry, rz, rt, ft, out = parts[w]
        size = out.shape[1]
        q = tail_rows(size)
        for j in range(1, ny):
            last_tail(w, j).wait_recv()
        add(part, (z * ny + y) * size + size - q, q, [ft.at[j - 1] for j in range(1, ny)])

        @tiles(size, 16)
        def _(r):
            out[0, r, :] = part[pl.ds(pl.multiple_of(f * size + r.start, 16), 16), :]

    backs = ((cot, rc_m, rx_m, mixed_out), (tok, rc_t, rx_t, tg_out))

    def back_start(w):
        full, rc, rx, out = backs[w]
        for k in range(nx):
            k = (k + 1) % nx
            send(rows(full, xp(k) * 2 + 1 - c, T), rc.at[k], rc_s.at[w, k], rc_r.at[w, k],
                 edev(x, 1 - c))

    def back_pair(w):
        full, rc, rx, out = backs[w]
        for k in range(nx):
            k = (k + 1) % nx
            index = xp(k) * 2 + c
            slot = rc.at[k]
            remote(slot, slot, rc_s.at[w, k], rc_r.at[w, k], edev(x, 1 - c)).wait_recv()

            @tiles(T, 16)
            def _(r):
                at = pl.ds(pl.multiple_of(index * T + r.start, 16), 16)
                full[at, :] = (full[at, :].astype(F32) + rc[k, r, :].astype(F32)).astype(BF16)

            if k:
                send(rows(full, index, T), rx.at[k - 1], rx_s.at[w, k - 1], rx_r.at[w, k - 1],
                     edev(xp(k), c))

    def back_end(w):
        full, rc, rx, out = backs[w]
        for k in range(1, nx):
            slot = rx.at[k - 1]
            remote(slot, slot, rx_s.at[w, k - 1], rx_r.at[w, k - 1], edev(xp(k), c)).wait_recv()

        @tiles(T, 16)
        def _(r):
            at = pl.ds(pl.multiple_of(e * T + r.start, 16), 16)
            total = full[at, :].astype(F32)
            for k in range(1, nx):
                total += rx[k - 1, r, :].astype(F32)
            out[r, :] = total.astype(BF16)

    hop(1, 3)
    hop_tail(1, 2)
    part_start(1)
    hop_tail(1, 3)
    weight_wait(1)

    @tiles(FF, 256)
    def _(n):
        dpre[:, n] = (dot(cot[...], down[n, :], NT) * slope[:, n]).astype(BF16)

    run(1, 0)

    @tiles(D, 384)
    def _(n):
        upart[n, :] = dot(tok[:, n], dpre[...], TN).astype(BF16)

    part_start(0)
    run(1, 1)

    @tiles(D, 512)
    def _(n):
        cot[:, n] = (dot(hidden[...], down[:, n], NN) * gate[:, 0:1]).astype(BF16)

    back_start(0)
    run(1, 2)
    for copy in tok_forwards:
        copy.wait_send()

    @tiles(D, 512)
    def _(n):
        tok[:, n] = dot(dpre[...], up[n, :], NT).astype(BF16)

    back_start(1)
    back_pair(0)
    back_pair(1)
    run(0, 0)
    part_last(1)
    back_end(0)
    run(0, 1)
    back_end(1)
    part_end(1)
    run(0, 2)
    part_last(0)
    part_end(0)
    for copy in sends:
        copy.wait_send()
    for there, copies in guarded:
        @pl.when(there)
        def _():
            for copy in copies:
                copy.wait_send()


def body(tokens, expert_ids, gates, up_weight, down_weight, cotangent):
    nf, ne = lax.axis_size("fsdp"), lax.axis_size("ep")
    nz = 4
    ny, nx = nf // nz, ne // 2
    T, D = tokens.shape
    R = ne * T
    su, FF = up_weight.shape[1:]
    sd = down_weight.shape[1]
    chosen = expert_ids[None] == jnp.arange(ne, dtype=jnp.int32)[:, None, None]
    dense = jnp.sum(jnp.where(chosen, gates[None], 0.0), axis=2)
    gcols = jnp.broadcast_to(dense[:, :, None], (ne, T, LANES))
    qu, qd = (tail_rows(size) for size in (su, sd))
    anyspace = pl.BlockSpec(memory_space=pl.ANY)
    vmem = pl.BlockSpec(memory_space=pltpu.VMEM)
    sem = pltpu.SemaphoreType.DMA
    V = pltpu.VMEM
    scratch = [
        V((D, FF), BF16), V((FF, D), BF16), V((R, D), BF16), V((R, D), BF16),
        V((R, LANES), F32), V((R, FF), F32), V((R, FF), BF16), V((R, FF), BF16),
        V((D, FF), BF16), V((FF, D), BF16),
        V(((ny - 1) * nz, su - qu, FF), BF16), V(((ny - 1) * nz, sd - qd, D), BF16),
        V((2, nz, su, FF), BF16), V((2, nz, sd, D), BF16),
        V((2, nz, ny - 1, qu, FF), BF16), V((2, nz, ny - 1, qd, D), BF16),
        V((ny - 1, qu, FF), BF16), V((ny - 1, qd, D), BF16),
        V((nx, T, D), BF16), V((nx, T, D), BF16),
        V((nx - 1, T, D), BF16), V((nx - 1, T, D), BF16),
        sem((4,)),
        sem((2, 2, nz)), sem((2, 2, nz)),
        sem((2, 2, nz, ny - 1)), sem((2, 2, nz, ny - 1)),
        sem((2, ny - 1)), sem((2, ny - 1)),
        sem((2, nz, ny - 1)), sem((2, nz, ny - 1)),
        sem((2, nx - 1)), sem((2, nx - 1)),
        sem((2, nx)), sem((2, nx)),
        sem((ne - 1,)), sem((ne - 1,)),
        sem((2, nz, ny - 1)), sem((2, nz, ny - 1)),
        sem((2, nz)), sem((2, 2, nz)),
        sem((2, nz, ny - 1)), sem((2, 2, nz, ny - 1)),
        sem((2, ny - 1)), sem((2, ny - 1)),
        sem((2, nx)), sem((2, nx)),
        sem((2, nx - 1)), sem((2, nx - 1)),
    ]
    return pl.pallas_call(
        functools.partial(kernel, nz, ny, nx),
        out_shape=(
            jax.ShapeDtypeStruct((T, D), BF16),
            jax.ShapeDtypeStruct((T, D), BF16),
            jax.ShapeDtypeStruct((1, su, FF), BF16),
            jax.ShapeDtypeStruct((1, sd, D), BF16),
        ),
        in_specs=[anyspace, anyspace, vmem, anyspace, anyspace],
        out_specs=(vmem, vmem, vmem, vmem),
        scratch_shapes=scratch,
        compiler_params=pltpu.CompilerParams(
            collective_id=0, has_side_effects=True, vmem_limit_bytes=64 * 1024 * 1024 - 262144
        ),
    )(tokens, cotangent, gcols, up_weight, down_weight)


def grouped(nz, *refs):
    (tok_in, cot_in, ids_in, gate_in, up_in, down_in,
     mixed_out, tg_out, ug_out, dg_out,
     up, down, tok, cot, upl, perm, uex, gd, gcol, slope, dh, hidden, dpre, upart, dpart,
     rz_u, rz_d, yrecv, rc_m, rc_t, r2_m, r2_t, r3_m, r3_t,
     local_sem, us, ur, ds_s, ds_r, yx_s, yx_r, tx_s, tx_r, ty_s, ty_r, fx_s, fx_r, fy_s, fy_r,
     tc_s, tc_r, g_s, g_r, ru_s, ru_r, rd_s, rd_r, yg_s, yg_r, b1_s, b1_r, b2_s, b2_r, b3_s, b3_r,
     ids, gate, ob, od, ou) = refs
    f = lax.axis_index("fsdp")
    e = lax.axis_index("ep")
    z, y = lax.div(f, 2), lax.rem(f, 2)
    x, c = lax.div(e, 2), lax.rem(e, 2)
    T, D = tok_in.shape
    SU, FF = up_in.shape[1:]
    SD = down_in.shape[1]
    G3 = nz * SD
    H = FF // 2
    R = 8 * T
    N = len(WIDTHS)
    begins = [D * sum(WIDTHS[:n]) // sum(WIDTHS) for n in range(N + 1)]

    def inside(zz):
        return (zz >= 0) & (zz < nz)

    def zp(k):
        return lax.rem(z + k + nz, nz)

    def zdev(zz):
        return {"fsdp": lax.rem(zz + nz, nz) * 2 + y}

    ydev = {"fsdp": z * 2 + 1 - y}
    xdev = {"ep": (1 - x) * 2 + c}
    cdev = {"ep": x * 2 + 1 - c}

    def blk(yy, xx, cc):
        return cc * 4 + yy * 2 + xx

    me = blk(y, x, c)

    def rows(index, size):
        return pl.ds(pl.multiple_of(index * size, size), size)

    def lanes(index, size):
        return pl.ds(pl.multiple_of(index * size, size), size)

    def cols(n):
        return pl.ds(begins[n], begins[n + 1] - begins[n])

    def cols_a(n):
        return pl.ds(begins[n], SPLITS[n])

    def cols_b(n):
        return pl.ds(begins[n] + SPLITS[n], begins[n + 1] - begins[n] - SPLITS[n])

    units = (pl.ds(0, 2 * G3), pl.ds(2 * G3, G3))
    sets = (pl.ds(0, 2), pl.ds(2, 1))

    def remote(src, dst, ss, rs, dev):
        return pltpu.make_async_remote_copy(
            src_ref=src, dst_ref=dst, send_sem=ss, recv_sem=rs,
            device_id=dev, device_id_type=MESH,
        )

    sends = []
    guarded = {}

    def go(copy, keep=sends):
        copy.start()
        keep.append(copy)

    def keep_when(key, there, copy):
        guarded.setdefault(key, (there, []))[1].append(copy)

    def go_when(key, there, copy):
        @pl.when(there)
        def _():
            copy.start()

        keep_when(key, there, copy)

    def taken():
        started = (list(sends), dict(guarded))
        sends.clear()
        guarded.clear()
        return started

    def drain(started):
        for copy in started[0]:
            copy.wait_send()
        for there, copies in started[1].values():
            @pl.when(there)
            def _():
                for copy in copies:
                    copy.wait_send()

    barrier = pltpu.get_barrier_semaphore()
    offsets = [(i // 4, i // 2 % 2, i % 2) for i in range(1, 8)]

    def gdev(dy, dx, dc):
        yy = 1 - y if dy else y
        xx = 1 - x if dx else x
        cc = 1 - c if dc else c
        return yy, xx, cc

    for sgn in (1, -1):
        @pl.when(inside(z + sgn))
        def _():
            pl.semaphore_signal(barrier, inc=1, device_id=zdev(z + sgn), device_id_type=MESH)

    for offset in offsets:
        yy, xx, cc = gdev(*offset)
        pl.semaphore_signal(barrier, inc=1, device_id={"fsdp": z * 2 + yy, "ep": xx * 2 + cc},
                            device_id_type=MESH)
    locals_ = []
    for i, (src, dst) in enumerate((
        (up_in.at[0], upl),
        (down_in, down.at[:, rows(z, SD)]),
        (tok_in, tok.at[rows(me, T)]),
        (cot_in, cot.at[rows(me, T)]),
        (ids_in, ids),
        (gate_in, gate),
    )):
        copy = pltpu.make_async_copy(src, dst, local_sem.at[i])
        copy.start()
        locals_.append(copy)

    near = z + lax.div(z, 2) * (3 - 2 * z)
    pl.semaphore_wait(barrier, len(offsets) + 1 + jnp.minimum(near, 1))

    def permute_up():
        @pl.loop(0, 6 * nz)
        def _(i):
            half, third, zz = lax.div(i, 3 * nz), lax.rem(lax.div(i, nz), 3), lax.rem(i, nz)
            column = lax.broadcasted_iota(jnp.int32, (SD, FF), 1)
            first = SD * (3 * (2 * zz + half) + third)
            unit = lax.broadcasted_iota(jnp.int32, (SD, FF), 0) + first
            perm[rows(i, SD), :] = jnp.where(column == unit, 1.0, 0.0).astype(BF16)

        locals_[0].wait()
        up[rows(f, SU), :] = dot(upl[...], perm[rows(y, H), :], NT).astype(BF16)
        uex[...] = dot(upl[...], perm[rows(1 - y, H), :], NT).astype(BF16)

    def sub(p):
        return y if p % 2 == 0 else 1 - y

    def chain_u(p, sgn, b, own=False):
        block = up.at[rows(2 * b + sub(p), SU), units[p // 2]]
        way = (1 - sgn) // 2
        return remote(block, block, us.at[p, way, b], ur.at[p, way, b], zdev(z + sgn))

    def chain_d(n, sgn, b, own=False):
        block = down.at[:, rows(b, SD), cols(n)]
        way = (1 - sgn) // 2
        return remote(down_in.at[:, :, cols(n)] if own else block, block, ds_s.at[n, way, b], ds_r.at[n, way, b], zdev(z + sgn))

    def own_start(chain, n):
        for sgn in (1, -1):
            go_when((sgn, 0), inside(z + sgn), chain(n, sgn, z, True))

    def hop(chain, n, s):
        for sgn in (1, -1):
            b = zp(-sgn * s)
            there = inside(z - sgn * s)

            @pl.when(there)
            def _():
                chain(n, sgn, b).wait_recv()

            go_when((sgn, s), there & inside(z + sgn), chain(n, sgn, b))

    y_exchange = [remote(uex.at[:, units[g]], up.at[rows(f, SU), units[g]], yx_s.at[g], yx_r.at[g], ydev)
                  for g in range(2)]

    acts = ((tok_in, tok), (cot_in, cot))
    forwards = ([[] for _ in range(N)], [[] for _ in range(N)])

    def act_own(w, n):
        src, full = acts[w]
        there = full.at[rows(me, T), cols(n)]
        go(remote(src.at[:, cols(n)], there, tx_s.at[w, n], tx_r.at[w, n], xdev))
        go(remote(src.at[:, cols(n)], there, ty_s.at[w, n], ty_r.at[w, n], ydev))
        go(remote(src.at[:, cols(n)], there, tc_s.at[w, n, 0], tc_r.at[w, n, 0], cdev))

    def high_rows(b):
        return pl.ds(pl.multiple_of(b * T, 16), SHARE)

    def low_rows(b):
        return pl.ds(pl.multiple_of(b * T + SHARE, 16), T - SHARE)

    def act_fwd(w, n):
        full = acts[w][1]
        keep = forwards[w][n]
        bx, by = blk(y, 1 - x, c), blk(1 - y, x, c)
        here = full.at[rows(bx, T), cols(n)]
        part = full.at[low_rows(bx), cols(n)]
        remote(here, here, tx_s.at[w, n], tx_r.at[w, n], xdev).wait_recv()
        go(remote(part, part, fy_s.at[w, n], fy_r.at[w, n], ydev), keep)
        go(remote(here, here, tc_s.at[w, n, 1], tc_r.at[w, n, 1], cdev), keep)
        here = full.at[rows(by, T), cols(n)]
        part = full.at[high_rows(by), cols(n)]
        remote(here, here, ty_s.at[w, n], ty_r.at[w, n], ydev).wait_recv()
        go(remote(part, part, fx_s.at[w, n], fx_r.at[w, n], xdev), keep)
        go(remote(here, here, tc_s.at[w, n, 2], tc_r.at[w, n, 2], cdev), keep)

    def act_diag(w, n):
        full = acts[w][1]
        bd = blk(1 - y, 1 - x, c)
        low = full.at[high_rows(bd), cols(n)]
        high = full.at[low_rows(bd), cols(n)]
        here = full.at[rows(bd, T), cols(n)]
        remote(low, low, fx_s.at[w, n], fx_r.at[w, n], xdev).wait_recv()
        remote(high, high, fy_s.at[w, n], fy_r.at[w, n], ydev).wait_recv()
        go(remote(here, here, tc_s.at[w, n, 3], tc_r.at[w, n, 3], cdev), forwards[w][n])

    def act_done(w, n):
        full = acts[w][1]
        others = ((y, x), (y, 1 - x), (1 - y, x), (1 - y, 1 - x))
        for k, (yy, xx) in enumerate(others):
            here = full.at[rows(blk(yy, xx, 1 - c), T), cols(n)]
            remote(here, here, tc_s.at[w, n, k], tc_r.at[w, n, k], cdev).wait_recv()

    def gates_start():
        locals_[4].wait()
        locals_[5].wait()
        expert = lax.broadcasted_iota(jnp.int32, (8, T), 0)
        gd[me] = jnp.where(ids[0:1, :] == expert, gate[0:1, :], 0.0) + jnp.where(
            ids[1:2, :] == expert, gate[1:2, :], 0.0)
        for i, offset in enumerate(offsets):
            yy, xx, cc = gdev(*offset)
            go(remote(gd.at[me], gd.at[me], g_s.at[i], g_r.at[i],
                      {"fsdp": z * 2 + yy, "ep": xx * 2 + cc}))

    def gates_done():
        for i, offset in enumerate(offsets):
            yy, xx, cc = gdev(*offset)
            here = gd.at[blk(yy, xx, cc)]
            remote(here, here, g_s.at[i], g_r.at[i],
                   {"fsdp": z * 2 + yy, "ep": xx * 2 + cc}).wait_recv()

        @pl.loop(0, 8)
        def _(b):
            mine = lax.broadcasted_iota(jnp.int32, (8, T), 0) == e
            row = jnp.sum(jnp.where(mine, gd[b], 0.0), axis=0, keepdims=True)
            eye = lax.broadcasted_iota(jnp.int32, (T, T), 0) == lax.broadcasted_iota(
                jnp.int32, (T, T), 1)
            column = jnp.sum(jnp.where(eye, row, 0.0), axis=1, keepdims=True)
            gcol[rows(b, T), :] = jnp.broadcast_to(column, (T, LANES))

    flip = lax.div(z, 2)
    near = z + flip * (3 - 2 * z)
    order = [d + flip * (3 - 2 * d) for d in (near * 0 + 3, 2 - 2 * near, 1 + near, near)]
    is_end = near == 0

    def pre_step(g, s):
        plane = order[3 - s]
        u = units[g]
        if g == 0 and s == 0:
            locals_[2].wait()
            locals_[3].wait()

        @tiles(R, 256)
        def _(r):
            part = dot(tok[r, lanes(plane, 2 * SU)], up[rows(plane, 2 * SU), u], NN)
            if s == 0:
                slope[r, u] = part
            elif s < nz - 1:
                slope[r, u] += part
            else:
                value, grad = gelu_parts(slope[r, u] + part)
                hidden[r, u] = (value * gcol[r, 0:1]).astype(BF16)
                slope[r, u] = grad * gcol[r, 0:1]

    def tokens_sent():
        for copies in forwards[0]:
            for copy in copies:
                copy.wait_send()

    def chunk_tiles(n):
        size = TILE

        def run(fn):
            @pl.loop(0, (begins[n + 1] - begins[n]) // size)
            def _(i):
                fn(pl.ds(pl.multiple_of(begins[n] + i * size, size), size))

        return run

    def down_part(g, n):
        @chunk_tiles(n)
        def _(t):
            part = dot(hidden[:, units[g]], cot[:, t], TN).astype(BF16)
            dpart[sets[g], :, t] = part.reshape(2 - g, G3, TILE)

    def back_hidden(n):
        if n == 0:
            locals_[1].wait()

        @tiles(R, 512)
        def _(r):
            part = dot(cot[r, cols(n)], down[:, :, cols(n)].reshape(H, begins[n + 1] - begins[n]), NT)
            if n == 0:
                dh[r, :] = part
            elif n < N - 1:
                dh[r, :] += part
            else:
                dpre[r, :] = ((dh[r, :] + part) * slope[r, :]).astype(BF16)

    def mixed_part(n):
        for copy in forwards[1][n]:
            copy.wait_send()

        @chunk_tiles(n)
        def _(t):
            @tiles(R, ROWS)
            def _(r):
                cot[r, t] = dot(hidden[r, :], down[:, :, t].reshape(H, TILE), NN).astype(BF16)

    def token_part(n):
        @chunk_tiles(n)
        def _(t):
            @tiles(R, ROWS)
            def _(r):
                tok[r, t] = dot(dpre[r, :], up[t, :], NT).astype(BF16)

    def up_part(q, pos):
        at = rows(2 * order[pos] + (1 - sub(q)), SU)
        upart[at, :] = dot(tok[:, at], dpre[...], TN).astype(BF16)

    def send_down(m, d, way, nxt):
        g, n = m // N, m % N
        return remote(dpart.at[sets[g], rows(d, SD), cols(n)], rz_d.at[way, d, sets[g], :, cols(n)],
                      rd_s.at[m, d], rd_r.at[m, way, d], zdev(nxt))

    def send_up(q, d, way, nxt):
        return remote(upart.at[rows(2 * d + (1 - sub(q)), SU)], rz_u.at[q, way, d],
                      ru_s.at[q, d], ru_r.at[q, way, d], zdev(nxt))

    def add_down(m, d, way):
        g, n = m // N, m % N

        @tiles(SD, 16)
        def _(r):
            at = pl.ds(pl.multiple_of(d * SD + r.start, 16), 16)
            dpart[sets[g], at, cols(n)] = (dpart[sets[g], at, cols(n)].astype(F32)
                                           + rz_d[way, d, sets[g], r, cols(n)].astype(F32)).astype(BF16)

    def add_up(q, d, way):
        @tiles(SU, 32)
        def _(r):
            at = pl.ds(pl.multiple_of((2 * d + (1 - sub(q))) * SU + r.start, 32), 32)
            upart[at, :] = (upart[at, :].astype(F32)
                            + rz_u[q, way, d, r, :].astype(F32)).astype(BF16)

    downs, ups = (send_down, add_down), (send_up, add_up)

    def course(pos):
        d = order[pos]
        way = jnp.where(d > z, 0, 1)
        return d, way, z + 1 - 2 * way

    def begin(kind, n, pos):
        d, way, nxt = course(pos)
        go_when("end", is_end, kind[0](n, d, way, nxt))

    def middle(kind, n, pos):
        d, way, nxt = course(pos)
        copy = kind[0](n, d, way, nxt)

        @pl.when(jnp.logical_not(is_end))
        def _():
            copy.wait_recv()
            kind[1](n, d, way)
            copy.start()

        keep_when("middle", jnp.logical_not(is_end), copy)

    def last(kind, n):
        for way in range(2):
            @pl.when(inside(z - 1 + 2 * way))
            def _():
                kind[0](n, z, way, zp(1)).wait_recv()
                kind[1](n, z, way)

    results = []

    def result(src, dst, done):
        copy = pltpu.make_async_copy(src, dst, done)
        copy.start()
        results.append(copy)

    def down_end(m):
        g, n = m // N, m % N
        last(downs, m)
        result(dpart.at[sets[g], rows(z, SD), cols(n)], dg_out.at[sets[g], :, cols(n)], od.at[m])

    other_up = upart.at[rows(2 * z + 1 - y, SU)]
    y_return = remote(other_up, yrecv, yg_s.at[0], yg_r.at[0], ydev)

    def up_end():
        last(ups, 1)
        y_return.wait_recv()
        upl[...] = (dot(upart[rows(f, SU), :], perm[rows(y, H), :], NN)
                     + dot(yrecv[...], perm[rows(1 - y, H), :], NN)).astype(BF16)
        result(upl, ug_out.at[0], ou.at[0])

    backs = ((cot, rc_m, r2_m, r3_m, mixed_out), (tok, rc_t, r2_t, r3_t, tg_out))
    G = 4 * T

    def back1(w, n):
        full, rc = backs[w][:2]
        go(remote(full.at[rows(1 - c, G), cols(n)], rc.at[:, cols(n)],
                  b1_s.at[w, n], b1_r.at[w, n], cdev))

    def back2(w, n):
        full, rc, r2 = backs[w][:3]
        here = rc.at[:, cols(n)]
        remote(here, here, b1_s.at[w, n], b1_r.at[w, n], cdev).wait_recv()

        @tiles(G, 16)
        def _(r):
            at = pl.ds(pl.multiple_of(c * G + r.start, 16), 16)
            full[at, cols(n)] = (full[at, cols(n)].astype(F32)
                                 + rc[r, cols(n)].astype(F32)).astype(BF16)

        for yy in range(2):
            go(remote(full.at[rows(blk(yy, 1 - x, c), T), cols_a(n)],
                      r2.at[pl.ds(yy * T, T), cols_a(n)],
                      b2_s.at[w, n, yy], b2_r.at[w, n, yy], xdev))
        go(remote(full.at[rows(c * 2 + 1 - y, 2 * T), cols_b(n)], r2.at[:, cols_b(n)],
                  b2_s.at[w, n, 2], b2_r.at[w, n, 2], ydev))

    def back3(w, n):
        full, rc, r2, r3 = backs[w][:4]
        for yy in range(2):
            here = r2.at[pl.ds(yy * T, T), cols_a(n)]
            remote(here, here, b2_s.at[w, n, yy], b2_r.at[w, n, yy], xdev).wait_recv()
        here = r2.at[:, cols_b(n)]
        remote(here, here, b2_s.at[w, n, 2], b2_r.at[w, n, 2], ydev).wait_recv()
        ba, bb = blk(1 - y, x, c), blk(y, 1 - x, c)

        @tiles(T, 16)
        def _(r):
            at = pl.ds(pl.multiple_of(ba * T + r.start, 16), 16)
            there = pl.ds(pl.multiple_of((1 - y) * T + r.start, 16), 16)
            full[at, cols_a(n)] = (full[at, cols_a(n)].astype(F32)
                                   + r2[there, cols_a(n)].astype(F32)).astype(BF16)
            at = pl.ds(pl.multiple_of(bb * T + r.start, 16), 16)
            there = pl.ds(pl.multiple_of((1 - x) * T + r.start, 16), 16)
            full[at, cols_b(n)] = (full[at, cols_b(n)].astype(F32)
                                   + r2[there, cols_b(n)].astype(F32)).astype(BF16)

        go(remote(full.at[rows(ba, T), cols_a(n)], r3.at[:, cols_a(n)],
                  b3_s.at[w, n, 0], b3_r.at[w, n, 0], ydev))
        go(remote(full.at[rows(bb, T), cols_b(n)], r3.at[:, cols_b(n)],
                  b3_s.at[w, n, 1], b3_r.at[w, n, 1], xdev))

    def back4(w, n):
        full, rc, r2, r3, out = backs[w]
        for k, (span, dev) in enumerate(((cols_a(n), ydev), (cols_b(n), xdev))):
            here = r3.at[:, span]
            remote(here, here, b3_s.at[w, n, k], b3_r.at[w, n, k], dev).wait_recv()

        @tiles(T, 16)
        def _(r):
            at = pl.ds(pl.multiple_of(me * T + r.start, 16), 16)
            for span, lane in ((cols_a(n), y), (cols_b(n), x)):
                there = pl.ds(pl.multiple_of(lane * T + r.start, 16), 16)
                full[at, span] = (full[at, span].astype(F32) + r2[there, span].astype(F32)
                                + r3[r, span].astype(F32)).astype(BF16)

        result(full.at[rows(me, T), cols(n)], out.at[:, cols(n)], ob.at[w, n])

    own_start(chain_d, 1)
    act_own(0, 2)
    own_start(chain_d, 0)
    permute_up()
    go(y_exchange[0])
    own_start(chain_u, 2)
    own_start(chain_u, 0)
    act_own(0, 1)
    go(y_exchange[1])
    act_own(0, 0)
    y_exchange[0].wait_recv()
    act_own(0, 3)
    gates_start()
    own_start(chain_u, 1)
    hop(chain_u, 2, 1)
    act_fwd(0, 2)
    y_exchange[1].wait_recv()
    own_start(chain_u, 3)
    act_fwd(0, 1)
    act_own(1, 3)
    hop(chain_u, 1, 1)
    hop(chain_u, 0, 1)
    act_fwd(0, 3)
    hop(chain_u, 1, 2)
    act_fwd(0, 0)
    gates_done()
    act_diag(0, 2)
    act_fwd(1, 3)
    hop(chain_u, 3, 1)
    hop(chain_u, 0, 2)
    act_own(1, 1)
    hop(chain_u, 2, 2)
    act_own(1, 0)
    hop(chain_u, 1, 3)
    act_diag(0, 1)
    act_diag(0, 0)
    act_diag(0, 3)
    hop(chain_u, 3, 2)
    hop(chain_d, 0, 1)
    act_done(0, 2)
    own_start(chain_d, 2)
    act_done(0, 0)
    own_start(chain_d, 3)
    act_diag(1, 3)
    act_done(0, 1)
    act_done(0, 3)
    pre_step(0, 0)
    pre_step(0, 1)
    pre_step(0, 2)
    act_done(1, 3)
    act_fwd(1, 1)
    hop(chain_u, 0, 3)
    pre_step(0, 3)
    down_part(0, 3)
    begin(downs, 0 * N + 3, 1)
    begin(downs, 0 * N + 3, 2)
    hop(chain_u, 3, 3)
    act_fwd(1, 0)
    pre_step(1, 0)
    pre_step(1, 1)
    act_diag(1, 1)
    act_own(1, 2)
    hop(chain_u, 2, 3)
    begin(downs, 0 * N + 3, 0)
    hop(chain_d, 0, 2)
    act_done(1, 1)
    down_part(0, 1)
    hop(chain_d, 1, 1)
    begin(downs, 0 * N + 1, 2)
    pre_step(1, 2)
    act_diag(1, 0)
    pre_step(1, 3)
    down_part(1, 1)
    act_done(1, 0)
    down_part(1, 0)
    begin(downs, 0 * N + 1, 0)
    begin(downs, 1 * N + 0, 0)
    begin(downs, 1 * N + 0, 1)
    begin(downs, 1 * N + 1, 1)
    down_part(0, 0)
    act_fwd(1, 2)
    begin(downs, 1 * N + 1, 2)
    begin(downs, 1 * N + 1, 0)
    begin(downs, 0 * N + 1, 1)
    begin(downs, 0 * N + 0, 0)
    hop(chain_d, 0, 3)
    back_hidden(0)
    mixed_part(0)
    back1(0, 0)
    hop(chain_d, 1, 2)
    down_part(1, 3)
    hop(chain_d, 2, 1)
    begin(downs, 1 * N + 3, 0)
    act_diag(1, 2)
    begin(downs, 1 * N + 3, 2)
    begin(downs, 0 * N + 0, 1)
    back2(0, 0)
    act_done(1, 2)
    hop(chain_d, 1, 3)
    back_hidden(1)
    mixed_part(1)
    back1(0, 1)
    begin(downs, 1 * N + 3, 1)
    middle(downs, 0 * N + 3, 2)
    hop(chain_d, 2, 2)
    down_part(1, 2)
    hop(chain_d, 3, 1)
    middle(downs, 0 * N + 1, 0)
    begin(downs, 1 * N + 2, 0)
    down_part(0, 2)
    begin(downs, 0 * N + 2, 2)
    begin(downs, 0 * N + 2, 1)
    back2(0, 1)
    hop(chain_d, 2, 3)
    middle(downs, 0 * N + 0, 0)
    back_hidden(2)
    mixed_part(2)
    back1(0, 2)
    begin(downs, 0 * N + 2, 0)
    hop(chain_d, 3, 2)
    middle(downs, 0 * N + 3, 0)
    back3(0, 0)
    begin(downs, 1 * N + 2, 2)
    middle(downs, 1 * N + 1, 0)
    begin(downs, 1 * N + 0, 2)
    middle(downs, 1 * N + 1, 2)
    begin(downs, 1 * N + 2, 1)
    middle(downs, 1 * N + 3, 2)
    back2(0, 2)
    hop(chain_d, 3, 3)
    early = taken()
    back_hidden(3)
    up_part(0, 0)
    middle(downs, 0 * N + 1, 2)
    begin(ups, 0, 0)
    mixed_part(3)
    back1(0, 3)
    back3(0, 1)
    up_part(1, 2)
    middle(downs, 1 * N + 0, 0)
    up_part(0, 3)
    up_part(0, 2)
    up_part(0, 1)
    back2(0, 3)
    up_part(1, 1)
    up_part(1, 3)
    middle(downs, 0 * N + 3, 1)
    up_part(1, 0)
    middle(downs, 1 * N + 2, 0)
    middle(downs, 0 * N + 2, 2)
    middle(downs, 1 * N + 3, 0)
    tokens_sent()
    begin(ups, 0, 1)
    token_part(3)
    back1(1, 3)
    middle(downs, 0 * N + 2, 0)
    back3(0, 2)
    middle(downs, 1 * N + 2, 1)
    token_part(1)
    back2(1, 3)
    middle(ups, 0, 0)
    middle(downs, 0 * N + 0, 1)
    token_part(0)
    back1(1, 0)
    middle(downs, 1 * N + 0, 1)
    begin(ups, 1, 0)
    back4(0, 0)
    begin(ups, 0, 2)
    back3(0, 3)
    middle(downs, 1 * N + 2, 2)
    back1(1, 1)
    middle(downs, 1 * N + 1, 1)
    middle(downs, 1 * N + 0, 2)
    token_part(2)
    back2(1, 0)
    down_end(1 * N + 1)
    middle(ups, 0, 2)
    back1(1, 2)
    middle(downs, 1 * N + 3, 1)
    begin(ups, 1, 1)
    back2(1, 1)
    back4(0, 1)
    back3(1, 3)
    middle(downs, 0 * N + 1, 1)
    begin(ups, 1, 2)
    back4(0, 3)
    middle(ups, 0, 1)
    back2(1, 2)
    back3(1, 0)
    down_end(1 * N + 3)
    begin(downs, 0 * N + 0, 2)
    middle(ups, 1, 0)
    down_end(0 * N + 1)
    middle(downs, 0 * N + 0, 2)
    last(ups, 0)
    down_end(1 * N + 2)
    middle(downs, 0 * N + 2, 1)
    go(y_return)
    drain(early)
    later = taken()
    back3(1, 1)
    down_end(0 * N + 2)
    back4(0, 2)
    down_end(1 * N + 0)
    middle(ups, 1, 1)
    middle(ups, 1, 2)
    back4(1, 3)
    back3(1, 2)
    down_end(0 * N + 3)
    back4(1, 0)
    back4(1, 1)
    drain(later)
    up_end()
    down_end(0 * N + 0)
    back4(1, 2)
    drain(taken())
    for copy in results:
        copy.wait()


def settle(*refs):
    sources, results, held, arrived, done = refs[:4], refs[4:8], refs[8:12], refs[12], refs[13]
    ins = [pltpu.make_async_copy(a, b, arrived.at[i]) for i, (a, b) in enumerate(zip(sources, held))]
    outs = [pltpu.make_async_copy(a, b, done.at[i]) for i, (a, b) in enumerate(zip(held, results))]
    for copy in ins:
        copy.start()
    for arrival, copy in zip(ins, outs):
        arrival.wait()
        copy.start()
    for copy in outs:
        copy.wait()


def grouped_body(nz, tokens, expert_ids, gates, up_weight, down_weight, cotangent):
    T, D = tokens.shape
    R = 8 * T
    SU, FF = up_weight.shape[1:]
    SD = down_weight.shape[1] // 3
    H = FF // 2
    N = len(WIDTHS)
    anyspace = pl.BlockSpec(memory_space=pl.ANY)
    sem = pltpu.SemaphoreType.DMA
    V = pltpu.VMEM

    def pair(*shape):
        return [sem(shape), sem(shape)]

    scratch = [
        V((D, H), BF16), V((3, nz * SD, D), BF16), V((R, D), BF16), V((R, D), BF16),
        V((SU, FF), BF16), V((FF, FF), BF16), V((SU, H), BF16),
        V((8, 8, T), F32), V((R, LANES), F32), V((R, H), F32), V((R, H), F32),
        V((R, H), BF16), V((R, H), BF16), V((D, H), BF16), V((3, nz * SD, D), BF16),
        V((2, 2, nz, SU, H), BF16), V((2, nz, 3, SD, D), BF16), V((SU, H), BF16),
        V((4 * T, D), BF16), V((4 * T, D), BF16), V((2 * T, D), BF16), V((2 * T, D), BF16),
        V((T, D), BF16), V((T, D), BF16),
        sem((6,)),
        *pair(4, 2, nz), *pair(N, 2, nz), *pair(2),
        *pair(2, N), *pair(2, N), *pair(2, N), *pair(2, N), *pair(2, N, 4), *pair(7),
        sem((2, nz)), sem((2, 2, nz)), sem((2 * N, nz)), sem((2 * N, 2, nz)), *pair(1),
        *pair(2, N), *pair(2, N, 3), *pair(2, N, 2),
        V((2, T), jnp.int32), V((2, T), F32), sem((2, N)), sem((2 * N,)), sem((1,)),
    ]
    outs = pl.pallas_call(
        functools.partial(grouped, nz),
        out_shape=(
            jax.ShapeDtypeStruct((T, D), BF16),
            jax.ShapeDtypeStruct((T, D), BF16),
            jax.ShapeDtypeStruct((1, SU, FF), BF16),
            jax.ShapeDtypeStruct((3, SD, D), BF16),
        ),
        in_specs=[anyspace] * 6,
        out_specs=(anyspace,) * 4,
        scratch_shapes=scratch,
        compiler_params=pltpu.CompilerParams(
            collective_id=0, has_side_effects=True, vmem_limit_bytes=64 * 1024 * 1024 - 262144
        ),
    )(tokens, cotangent, expert_ids.T, gates.T, up_weight, down_weight.reshape(3, SD, D))
    outs = pl.pallas_call(
        settle,
        out_shape=tuple(jax.ShapeDtypeStruct(out.shape, out.dtype) for out in outs),
        in_specs=[anyspace] * 4,
        out_specs=(anyspace,) * 4,
        scratch_shapes=[V(out.shape, BF16) for out in outs] + [sem((4,)), sem((4,))],
    )(*outs)
    return *outs[:3], outs[3].reshape(down_weight.shape)


def solution(mesh):
    placed = (
        P(("fsdp", "ep"), None),
        P(("fsdp", "ep"), None),
        P(("fsdp", "ep"), None),
        P("ep", "fsdp", None),
        P("ep", "fsdp", None),
        P(("fsdp", "ep"), None),
    )
    nf, ne = mesh.shape["fsdp"], mesh.shape["ep"]
    run = functools.partial(grouped_body, 4) if (nf, ne) == (8, 4) else body
    return jax.shard_map(
        run,
        mesh=mesh,
        in_specs=placed,
        out_specs=(
            P(("fsdp", "ep"), None),
            P(("fsdp", "ep"), None),
            P("ep", "fsdp", None),
            P("ep", "fsdp", None),
        ),
        check_vma=False,
    )
```
